32 devices in a mesh: dp: 2 (over x), seq: 4 (over y, core), heads: 4 (over z).
Axes of the slice: x: 2, y: 2, z: 4, core: 2. Of those that a mesh axis runs over, the one named last changes fastest.
Arguments:
- frames: bfloat16 [4, 2048, 1024], P('dp', 'seq'), may hold values from -6 to 6
- segment_ids: int32 [4, 2048], P('dp'), may hold values from 0 to 3, never falling along the last dimension, each value on 1 to 1024 neighbouring positions
- bucket_of: int32 [4095], replicated, may hold values from 0 to 31
- ffn1_gain: bfloat16 [1024], replicated, may hold values from 0.25 to 1.75
- ffn1_in: bfloat16 [1024, 4096], P(None, 'heads'), may hold values from -0.1875 to 0.1875
- ffn1_out: bfloat16 [4096, 1024], P('heads'), may hold values from -0.09375 to 0.09375
- attn_gain: bfloat16 [1024], replicated, may hold values from 0.25 to 1.75
- query_weight: bfloat16 [1024, 1024], P(None, 'heads'), may hold values from -0.1875 to 0.1875
- key_weight: bfloat16 [1024, 1024], P(None, 'heads'), may hold values from -0.1875 to 0.1875
- value_weight: bfloat16 [1024, 1024], P(None, 'heads'), may hold values from -0.1875 to 0.1875
- output_weight: bfloat16 [1024, 1024], P('heads'), may hold values from -1.5 to 1.5
- position_table: float32 [8, 32], P('heads'), may hold values from -4 to 4
- conv_gain: bfloat16 [1024], P(('dp', 'seq', 'heads')), may hold values from 0.25 to 1.75
- pointwise_in: bfloat16 [1024, 2048], P(('dp', 'seq', 'heads')), may hold values from -0.1875 to 0.1875
- depthwise: bfloat16 [5, 1024], P(None, ('dp', 'seq', 'heads')), may hold values from -2.5 to 2.5
- depth_gain: bfloat16 [1024], P(('dp', 'seq', 'heads')), may hold values from 0.25 to 1.75
- pointwise_out: bfloat16 [1024, 1024], P(('dp', 'seq', 'heads')), may hold values from -0.1875 to 0.1875
- ffn2_gain: bfloat16 [1024], replicated, may hold values from 0.25 to 1.75
- ffn2_in: bfloat16 [1024, 4096], P(None, 'heads'), may hold values from -0.1875 to 0.1875
- ffn2_out: bfloat16 [4096, 1024], P('heads'), may hold values from -0.09375 to 0.09375
- final_gain: bfloat16 [1024], replicated, may hold values from 0.25 to 1.75
- cotangent: bfloat16 [4, 2048, 1024], P('dp', 'seq'), may hold values from -6 to 6
Outputs:
- layer_out: bfloat16 [4, 2048, 1024], P('dp', 'seq')
- input_grad: float32 [4, 2048, 1024], P('dp', 'seq')
- ffn1_gain_grad: float32 [1024], P(('dp', 'seq'))
- ffn1_in_grad: float32 [1024, 4096], P(('dp', 'seq'), 'heads')
- ffn1_out_grad: float32 [4096, 1024], P('heads', ('dp', 'seq'))
- attn_gain_grad: float32 [1024], P(('dp', 'seq'))
- query_grad: float32 [1024, 1024], P(('dp', 'seq'), 'heads')
- key_grad: float32 [1024, 1024], P(('dp', 'seq'), 'heads')
- value_grad: float32 [1024, 1024], P(('dp', 'seq'), 'heads')
- output_grad: float32 [1024, 1024], P('heads', ('dp', 'seq'))
- table_grad: float32 [8, 32], P('heads', ('dp', 'seq'))
- conv_gain_grad: float32 [1024], P(('dp', 'seq', 'heads'))
- pointwise_in_grad: float32 [1024, 2048], P(('dp', 'seq', 'heads'))
- depthwise_grad: float32 [5, 1024], P(None, ('dp', 'seq', 'heads'))
- depth_gain_grad: float32 [1024], P(('dp', 'seq', 'heads'))
- pointwise_out_grad: float32 [1024, 1024], P(('dp', 'seq', 'heads'))
- ffn2_gain_grad: float32 [1024], P(('dp', 'seq'))
- ffn2_in_grad: float32 [1024, 4096], P(('dp', 'seq'), 'heads')
- ffn2_out_grad: float32 [4096, 1024], P('heads', ('dp', 'seq'))
- final_gain_grad: float32 [1024], P(('dp', 'seq'))
The draws below stay inside these ranges and needn't reach their ends.
Inputs may be any that keep to these rules, and one draw needn't show every extreme that they name: `segment_ids`: in each row, ids never fall along the frames; each utterance has at most 1024 frames and one has exactly that many.
All inputs are finite; a program needn't handle non-finite values.
Results may differ from the reference program's by a relative error of at most 0.029.
Values may be sent and summed in bfloat16 or wider, within the bound.
No kernel may reach another device: no remote copies, remote signals or barrier semaphores. Data moves between devices by JAX's collectives and lax.ppermute only.
A program may use at most 192 MiB of HBM per device.

```python
import math
import jax
import jax.numpy as jnp
import numpy as np
from jax import lax

D = 1024
FF = 4096
HEADS = 8
HEAD_DIM = 128
KERNEL = 5
BUCKETS = 32
LENGTH = 2048
SEGS = 4
TOTAL_ROWS = 4
OFFSETS = 4095


def with_ends(values, stream_key, low, largest):
    longest = values.shape.index(max(values.shape))
    spots = []
    for shift in (0, 1):
        where = [jax.random.randint(jax.random.fold_in(stream_key, axis), (), 0, length) for axis, length in enumerate(values.shape)]
        where[longest] = (where[longest] + shift) % values.shape[longest]
        spots.append(tuple(where))
    return values.at[spots[0]].set(low).at[spots[1]].set(largest)


def block_levels(stream_key, extent, shards, least, largest):
    def one(axis_at, shards_of):
        draws = jax.random.uniform(jax.random.fold_in(jax.random.fold_in(stream_key, 6), axis_at), (shards_of,), jnp.float32, least / len(shards), largest / len(shards))
        return jnp.repeat(jnp.exp(draws), extent[axis_at] // shards_of).reshape((-1,) + (1,) * (len(extent) - axis_at - 1))

    level = one(*shards[0])
    for cut in shards[1:]:
        level = level * one(*cut)
    return level


def length_profile(count, total, bound, skew):
    portions = [(1 << 20) // math.isqrt(standing ** skew) + 1 for standing in range(2, count + 1)]
    surplus, counts = total - bound - (count - 1), [1] * (count - 1)
    while surplus > 0:
        candidates = [i for i in range(count - 1) if counts[i] < bound]
        pool, remaining = sum([portions[i] for i in candidates]), surplus
        for i in candidates:
            extra = min(bound - counts[i], max(1, remaining * portions[i] // pool), surplus)
            counts[i] = counts[i] + extra
            surplus = surplus - extra
    return np.array([bound] + counts)


def uneven(stream_key, number_of, total, bound, lean):
    if number_of == 2:
        one = jax.random.randint(stream_key, (), max(1, total - bound), min(bound, total - 1) + 1)
        return jnp.stack([one, total - one])
    lengths = jnp.asarray(length_profile(number_of, total, bound, lean), jnp.int32)
    pairs = (number_of - 1) // 2
    source_of, receiver = lengths[1:1 + 2 * pairs:2], lengths[2:2 + 2 * pairs:2]
    margin = jnp.minimum(source_of - 1, bound - receiver)
    passed = jax.random.randint(jax.random.fold_in(stream_key, 1), (pairs,), 0, 1 << 20) % (margin + 1)
    lengths = lengths.at[1:1 + 2 * pairs:2].set(source_of - passed).at[2:2 + 2 * pairs:2].set(receiver + passed)
    return lengths[jax.random.permutation(jax.random.fold_in(stream_key, 2), number_of)]


def noise(own_key, extent, spread, bound, cuts=(), held_as=jnp.bfloat16):
    loudness = block_levels(own_key, extent, cuts, -0.22, 0.18) if cuts else 1.0
    values = jax.random.normal(own_key, extent, jnp.float32) * spread * loudness
    return jnp.minimum(jnp.maximum(values, -bound), bound).astype(held_as)


def setup_inputs(seed: int = 0) -> dict:
    key_of = jax.random.split(jax.random.key(seed), 23)
    frames = noise(key_of[0], (TOTAL_ROWS, LENGTH, D), 1.0, 6.0, ((0, 2), (1, 4)))
    segment_ids = jax.vmap(lambda own: jnp.searchsorted(jnp.cumsum(uneven(own, SEGS, LENGTH, LENGTH // 2, 0)), jnp.arange(LENGTH), side="right"))(jax.random.split(key_of[1], TOTAL_ROWS)).reshape((TOTAL_ROWS, LENGTH)).astype(jnp.int32)
    bucket_of = with_ends(jax.random.randint(key_of[2], (OFFSETS,), 0, BUCKETS), jax.random.fold_in(key_of[2], 1), 0, BUCKETS - 1).astype(jnp.int32)
    ffn1_gain = jnp.clip(1.0 + 0.15 * jax.random.normal(key_of[3], (D,), jnp.float32), 0.25, 1.75).astype(jnp.bfloat16)
    ffn1_in = noise(key_of[4], (D, FF), D ** -0.5, 0.1875, ((1, 4),))
    ffn1_out = noise(key_of[5], (FF, D), FF ** -0.5, 0.09375, ((0, 4),))
    attn_gain = jnp.clip(1.0 + 0.15 * jax.random.normal(key_of[6], (D,), jnp.float32), 0.25, 1.75).astype(jnp.bfloat16)
    query_weight = noise(key_of[7], (D, HEADS * HEAD_DIM), D ** -0.5, 0.1875, ((1, 4),))
    key_weight = noise(key_of[8], (D, HEADS * HEAD_DIM), D ** -0.5, 0.1875, ((1, 4),))
    value_weight = noise(key_of[9], (D, HEADS * HEAD_DIM), D ** -0.5, 0.1875, ((1, 4),))
    output_weight = noise(key_of[10], (HEADS * HEAD_DIM, D), (D // 64) ** -0.5, 1.5, ((0, 4),))
    position_table = noise(key_of[11], (HEADS, BUCKETS), 1.0, 4.0, ((0, 4),), jnp.float32)
    conv_gain = jnp.clip(1.0 + 0.15 * jax.random.normal(key_of[12], (D,), jnp.float32), 0.25, 1.75).astype(jnp.bfloat16)
    pointwise_in = noise(key_of[13], (D, 2 * D), D ** -0.5, 0.1875, ((0, 32),))
    depthwise = noise(key_of[14], (KERNEL, D), KERNEL ** -0.5, 2.5, ((1, 32),))
    depth_gain = jnp.clip(1.0 + 0.15 * jax.random.normal(key_of[15], (D,), jnp.float32), 0.25, 1.75).astype(jnp.bfloat16)
    pointwise_out = noise(key_of[16], (D, D), D ** -0.5, 0.1875, ((0, 32),))
    ffn2_gain = jnp.clip(1.0 + 0.15 * jax.random.normal(key_of[17], (D,), jnp.float32), 0.25, 1.75).astype(jnp.bfloat16)
    ffn2_in = noise(key_of[18], (D, FF), D ** -0.5, 0.1875, ((1, 4),))
    ffn2_out = noise(key_of[19], (FF, D), FF ** -0.5, 0.09375, ((0, 4),))
    final_gain = jnp.clip(1.0 + 0.15 * jax.random.normal(key_of[20], (D,), jnp.float32), 0.25, 1.75).astype(jnp.bfloat16)
    cotangent = noise(key_of[21], (TOTAL_ROWS, LENGTH, D), 1.0, 6.0, ((0, 2), (1, 4)))
    return {"frames": frames, "segment_ids": segment_ids, "bucket_of": bucket_of, "ffn1_gain": ffn1_gain, "ffn1_in": ffn1_in, "ffn1_out": ffn1_out, "attn_gain": attn_gain, "query_weight": query_weight, "key_weight": key_weight, "value_weight": value_weight, "output_weight": output_weight, "position_table": position_table, "conv_gain": conv_gain, "pointwise_in": pointwise_in, "depthwise": depthwise, "depth_gain": depth_gain, "pointwise_out": pointwise_out, "ffn2_gain": ffn2_gain, "ffn2_in": ffn2_in, "ffn2_out": ffn2_out, "final_gain": final_gain, "cotangent": cotangent}


@jax.custom_vjp
def low(v):
    return lax.optimization_barrier(v.astype(jnp.bfloat16)).astype(jnp.float32)

@jax.custom_vjp
def low_back(v):
    return v

def low_keep(v):
    return (low(v), None)

def low_pass(kept, grad):
    return (grad,)

def back_keep(v):
    return (v, None)

def back_low(kept, grad):
    return (low(grad),)
low.defvjp(low_keep, low_pass)
low_back.defvjp(back_keep, back_low)
EPSILON = 1e-05
NEGATIVE = -1e+30
HIGHEST = lax.Precision.HIGHEST

def norm(values, gain_vec):
    centred = values - lax.optimization_barrier(jnp.mean(values, axis=-1, keepdims=True))
    inverse = lax.rsqrt(lax.optimization_barrier(jnp.mean(centred * centred, axis=-1, keepdims=True)) + EPSILON)
    return centred * inverse * gain_vec

def project(values, weight):
    return jnp.matmul(values, weight, precision=HIGHEST)

def feed_forward(stream, gain_vec, weight_in, weight_out):
    normed = low(norm(stream, gain_vec))
    hidden = low_back(project(normed, weight_in))
    branch = low_back(project(low(jax.nn.silu(hidden)), weight_out))
    return stream + 0.5 * branch

def attention(stream, gain_vec, query_w, key_w, value_w, output_w, bias_table, bucket_of, segment_ids):
    normed = low(norm(stream, gain_vec))
    shape_four = stream.shape[:2] + (HEADS, HEAD_DIM)
    query = low(low_back(project(normed, query_w))).reshape(shape_four)
    keys = low(low_back(project(normed, key_w))).reshape(shape_four)
    values = low(low_back(project(normed, value_w))).reshape(shape_four)
    offsets = jnp.arange(LENGTH, dtype=jnp.int32)[None, :] - jnp.arange(LENGTH, dtype=jnp.int32)[:, None] + (LENGTH - 1)
    bias_full = bias_table[:, bucket_of[offsets]]

    def one_row(inputs):
        query_row, key_row, value_row, segment_row = inputs
        scores = jnp.einsum('ihd,jhd->hij', query_row, key_row, precision=HIGHEST) * HEAD_DIM ** (-0.5) + bias_full
        scores = low_back(scores)
        allowed = segment_row[:, None] == segment_row[None, :]
        scores = jnp.where(allowed[None], scores, NEGATIVE)
        row_max = lax.optimization_barrier(jnp.max(scores, axis=-1, keepdims=True))
        exponent = jnp.exp(scores - row_max)
        probs = exponent / lax.optimization_barrier(jnp.sum(exponent, axis=-1, keepdims=True))
        mixture = jnp.einsum('hij,jhd->ihd', low(probs), value_row, precision=HIGHEST)
        return low(low_back(mixture))
    mixture = lax.map(jax.checkpoint(one_row), (query, keys, values, segment_ids))
    mixture = mixture.reshape(stream.shape[:2] + (HEADS * HEAD_DIM,))
    return stream + low_back(project(mixture, output_w))

def convolve(stream, gain_one, in_weight, depth_weight, gain_two, out_weight, segment_ids):
    normed = low(norm(stream, gain_one))
    doubled = low_back(project(normed, in_weight))
    glu_value = low(doubled[..., :D] * jax.nn.sigmoid(doubled[..., D:]))
    reach = KERNEL // 2
    padded = jnp.pad(glu_value, ((0, 0), (reach, reach), (0, 0)))
    ids_pad = jnp.pad(segment_ids, ((0, 0), (reach, reach)), constant_values=-1)
    depth_out = jnp.zeros(glu_value.shape, jnp.float32)
    for offset in range(KERNEL):
        same = (ids_pad[:, offset:offset + LENGTH] == segment_ids)[..., None]
        depth_out = depth_out + jnp.where(same, padded[:, offset:offset + LENGTH] * depth_weight[offset], 0.0)
    depth_out = low_back(depth_out)
    swish = low(jax.nn.silu(norm(depth_out, gain_two)))
    return stream + low_back(project(swish, out_weight))

def reference(frames, segment_ids, bucket_of, ffn1_gain, ffn1_in, ffn1_out, attn_gain, query_weight, key_weight, value_weight, output_weight, position_table, conv_gain, pointwise_in, depthwise, depth_gain, pointwise_out, ffn2_gain, ffn2_in, ffn2_out, final_gain, cotangent):
    params = tuple((item.astype(jnp.float32) for item in (ffn1_gain, ffn1_in, ffn1_out, attn_gain, query_weight, key_weight, value_weight, output_weight, position_table, conv_gain, pointwise_in, depthwise, depth_gain, pointwise_out, ffn2_gain, ffn2_in, ffn2_out, final_gain)))

    def layer(stream, weights):
        f1_gain, f1_in, f1_out, at_gain, query_w, key_w, value_w, output_w, bias_table, cv_gain, pw_in, depth_w, dp_gain, pw_out, f2_gain, f2_in, f2_out, fin_gain = weights
        stream = feed_forward(stream, f1_gain, f1_in, f1_out)
        stream = attention(stream, at_gain, query_w, key_w, value_w, output_w, bias_table, bucket_of, segment_ids)
        stream = convolve(stream, cv_gain, pw_in, depth_w, dp_gain, pw_out, segment_ids)
        stream = feed_forward(stream, f2_gain, f2_in, f2_out)
        return norm(stream, fin_gain)
    output, pull = jax.vjp(layer, frames.astype(jnp.float32), params)
    input_grad, grads = pull(cotangent.astype(jnp.float32))
    return (output.astype(jnp.bfloat16), input_grad, grads[0], grads[1], grads[2], grads[3], grads[4], grads[5], grads[6], grads[7], grads[8], grads[9], grads[10], grads[11], grads[12], grads[13], grads[14], grads[15], grads[16], grads[17])
```

```python
import functools
import math
import jax
import jax.numpy as jnp
from jax import lax
from jax.experimental import pallas as pl
from jax.experimental.pallas import tpu as pltpu
from jax.sharding import PartitionSpec as P

HEAD_DIM=128
NEGATIVE=-1e30
LOG2E=math.log2(math.e)
TILE=256

def bias_tiles_kernel(win_ref, out_ref):
    width = win_ref.shape[2]
    rows = jnp.broadcast_to(win_ref[0], (8, width))
    rows = pltpu.roll(rows, width - (TILE - 1), 1, stride=1, stride_axis=0)
    step = 8
    while step < TILE:
        rows = jnp.concatenate([rows, pltpu.roll(rows, step, 1)], axis=0)
        step *= 2
    for t in range(out_ref.shape[1]):
        out_ref[0, t] = rows[:, t * TILE : (t + 1) * TILE]

def bias_tiles(window):
    heads, width = window.shape
    tiles = width // TILE - 1
    return pl.pallas_call(
        bias_tiles_kernel,
        grid=(heads,),
        in_specs=[pl.BlockSpec((1, 1, width), lambda h: (h, 0, 0))],
        out_specs=pl.BlockSpec((1, tiles, TILE, TILE), lambda h: (h, 0, 0, 0)),
        out_shape=jax.ShapeDtypeStruct((heads, tiles, TILE, TILE), jnp.float32),
        cost_estimate=pl.CostEstimate(flops=heads*tiles*TILE*TILE*4, transcendentals=0, bytes_accessed=heads*tiles*TILE*TILE*4),
    )(window[:, None])

def offset_sums_kernel(tiles_ref, out_ref, wide):
    tiles = tiles_ref.shape[1]
    for t in range(tiles):
        wide[:, t * TILE : (t + 1) * TILE] = tiles_ref[0, t]
    wide[:, tiles * TILE :] = jnp.zeros((TILE, TILE), jnp.float32)
    rows = wide[...]
    half = TILE // 2
    while half >= 1:
        rows = pltpu.roll(rows[:half], half, 1) + rows[half:]
        half //= 2
    out_ref[0] = rows

def offset_sums(tile_grads):
    heads, tiles = tile_grads.shape[:2]
    width = (tiles + 1) * TILE
    return pl.pallas_call(
        offset_sums_kernel,
        grid=(heads,),
        in_specs=[pl.BlockSpec((1, tiles, TILE, TILE), lambda h: (h, 0, 0, 0))],
        out_specs=pl.BlockSpec((1, 1, width), lambda h: (h, 0, 0)),
        out_shape=jax.ShapeDtypeStruct((heads, 1, width), jnp.float32),
        scratch_shapes=[pltpu.VMEM((TILE, width), jnp.float32)],
        cost_estimate=pl.CostEstimate(flops=heads*tiles*TILE*TILE*4, transcendentals=0, bytes_accessed=heads*tiles*TILE*TILE*4),
    )(tile_grads)[:, 0]

def columns_of(head, per_shard):
    shard, at = head // per_shard, head % per_shard
    key = (shard * 2 * per_shard + at) * HEAD_DIM
    value = key + per_shard * HEAD_DIM
    return pl.multiple_of(key, HEAD_DIM), pl.multiple_of(value, HEAD_DIM)

def load_pieces(scal, pieces, whole, sems):
    local = pieces[0].shape[1]
    copies = []
    count = sum(p.shape[0] for p in pieces)
    nbits = count.bit_length() - 1
    rel = [0]
    n = 0
    for p in pieces:
        ids = [0] if p is pieces[0] else None
        if ids is None:
            bit = nbits - 1 - (n.bit_length() - 1)
            ids = [r ^ (1 << bit) for r in rel]
            rel = rel + ids
        for k, r in enumerate(ids):
            at = pl.multiple_of((scal[0] ^ r) * local, local)
            copies.append(pltpu.make_async_copy(p.at[k], whole.at[pl.ds(at, local)], sems.at[n]))
            n += 1
    for c in copies: c.start()
    for c in copies: c.wait()

def forward_kernel(scal, per_shard, pieces_n, *refs):
    q_ref, bias_ref, qid_ref, kid_ref = refs[:4]
    pieces = refs[4 : 4 + pieces_n]
    out_ref, lse_ref, whole, sems = refs[4 + pieces_n :]
    head = pl.program_id(0)
    @pl.when(head == 0)
    def _(): load_pieces(scal, pieces, whole, sems)
    kcol, vcol = columns_of(head, per_shard)
    scale = LOG2E * HEAD_DIM ** -0.5
    nk = whole.shape[0] // TILE
    for qb in range(q_ref.shape[0] // TILE):
        q = q_ref[qb * TILE : (qb + 1) * TILE, :]
        qid = qid_ref[:, qb * TILE : (qb + 1) * TILE]
        def body(kb, carry):
            top, total, acc = carry
            at = pl.multiple_of(kb * TILE, TILE)
            k = whole[pl.ds(at, TILE), pl.ds(kcol, HEAD_DIM)]
            v = whole[pl.ds(at, TILE), pl.ds(vcol, HEAD_DIM)]
            s = lax.dot_general(k, q, (((1,), (1,)), ((), ())), preferred_element_type=jnp.float32)
            s = s * scale + bias_ref[0, qb - kb + nk - 1]
            s = jnp.where(kid_ref[pl.ds(at, TILE), :] == qid, s, NEGATIVE)
            new_top = jnp.maximum(top, jnp.max(s, axis=0, keepdims=True))
            p = jnp.exp2(s - new_top)
            fade = jnp.exp2(top - new_top)
            total = total * fade + jnp.sum(p, axis=0, keepdims=True)
            acc = acc * fade + lax.dot_general(v, p.astype(jnp.bfloat16), (((0,), (0,)), ((), ())), preferred_element_type=jnp.float32)
            return new_top, total, acc
        top, total, acc = lax.fori_loop(scal[1 + 2 * qb], scal[2 + 2 * qb], body, (
            jnp.full((1, TILE), NEGATIVE, jnp.float32), jnp.zeros((1, TILE), jnp.float32), jnp.zeros((HEAD_DIM, TILE), jnp.float32)))
        out_ref[qb * TILE : (qb + 1) * TILE, :] = (acc / total).T.astype(jnp.bfloat16)
        lse_ref[0, :, qb * TILE : (qb + 1) * TILE] = top + jnp.log2(total)

def attend(scalars, q, tiles, qid, kid, pieces, per_shard):
    tokens, width = q.shape
    heads = width // HEAD_DIM
    length = kid.shape[0]
    count = sum(p.shape[0] for p in pieces)
    n_tiles = tiles.shape[1]
    fn = lambda scal, *refs: forward_kernel(scal, per_shard, len(pieces), *refs)
    flops = 4 * heads * tokens * length * HEAD_DIM
    return pl.pallas_call(
        fn,
        grid_spec=pltpu.PrefetchScalarGridSpec(
            num_scalar_prefetch=1, grid=(heads,),
            in_specs=[
                pl.BlockSpec((tokens, HEAD_DIM), lambda h, s: (0, h)),
                pl.BlockSpec((1, n_tiles, TILE, TILE), lambda h, s: (h, 0, 0, 0)),
                pl.BlockSpec((1, tokens), lambda h, s: (0, 0)),
                pl.BlockSpec((length, 1), lambda h, s: (0, 0)),
            ] + [pl.BlockSpec(memory_space=pl.ANY)] * len(pieces),
            out_specs=[
                pl.BlockSpec((tokens, HEAD_DIM), lambda h, s: (0, h)),
                pl.BlockSpec((1, 1, tokens), lambda h, s: (h, 0, 0)),
            ],
            scratch_shapes=[pltpu.VMEM((length, pieces[0].shape[-1]), jnp.bfloat16), pltpu.SemaphoreType.DMA((count,))],
        ),
        out_shape=[jax.ShapeDtypeStruct((tokens, width), jnp.bfloat16), jax.ShapeDtypeStruct((heads, 1, tokens), jnp.float32)],
        cost_estimate=pl.CostEstimate(flops=flops, transcendentals=heads*tokens*length, bytes_accessed=heads*n_tiles*TILE*TILE*4),
    )(scalars, q, tiles, qid, kid, *pieces)

def backward_kernel(scal, per_shard, pieces_n, *refs):
    q_ref, bias_ref, qid_ref, kid_ref, mix_ref, dmix_ref, lse_ref = refs[:7]
    pieces = refs[7 : 7 + pieces_n]
    dq_ref, dkv_ref, dtile_ref, whole, dk_acc, dv_acc, sems = refs[7 + pieces_n :]
    head = pl.program_id(0)
    @pl.when(head == 0)
    def _(): load_pieces(scal, pieces, whole, sems)
    kcol, vcol = columns_of(head, per_shard)
    scale = HEAD_DIM ** -0.5
    nk = whole.shape[0] // TILE
    dk_acc[...] = jnp.zeros_like(dk_acc)
    dv_acc[...] = jnp.zeros_like(dv_acc)
    dtile_ref[...] = jnp.zeros_like(dtile_ref)
    for qb in range(q_ref.shape[0] // TILE):
        rows = slice(qb * TILE, (qb + 1) * TILE)
        q = q_ref[rows, :]
        qid = qid_ref[:, rows]
        dmix = dmix_ref[rows, :]
        lse = lse_ref[0, :, rows]
        delta = jnp.sum((dmix.astype(jnp.float32) * mix_ref[rows, :].astype(jnp.float32)).T, axis=0, keepdims=True)
        def body(kb, dq):
            at = pl.multiple_of(kb * TILE, TILE)
            k = whole[pl.ds(at, TILE), pl.ds(kcol, HEAD_DIM)]
            v = whole[pl.ds(at, TILE), pl.ds(vcol, HEAD_DIM)]
            s = lax.dot_general(k, q, (((1,), (1,)), ((), ())), preferred_element_type=jnp.float32)
            s = s * (scale * LOG2E) + bias_ref[0, qb - kb + nk - 1]
            s = jnp.where(kid_ref[pl.ds(at, TILE), :] == qid, s, NEGATIVE)
            p = jnp.exp2(s - lse)
            dp = lax.dot_general(v, dmix, (((1,), (1,)), ((), ())), preferred_element_type=jnp.float32)
            ds = p * (dp - delta)
            dtile_ref[0, qb - kb + nk - 1] += ds
            low = ds.astype(jnp.bfloat16)
            dv_acc[pl.ds(at, TILE), :] += jnp.dot(p.astype(jnp.bfloat16), dmix, preferred_element_type=jnp.float32)
            dk_acc[pl.ds(at, TILE), :] += jnp.dot(low, q, preferred_element_type=jnp.float32)
            return dq + lax.dot_general(k, low, (((0,), (0,)), ((), ())), preferred_element_type=jnp.float32)
        dq = lax.fori_loop(scal[1 + 2 * qb], scal[2 + 2 * qb], body, jnp.zeros((HEAD_DIM, TILE), jnp.float32))
        dq_ref[rows, :] = (dq * scale).T.astype(jnp.bfloat16)
    count, local = dkv_ref.shape[:2]
    nbits = count.bit_length() - 1
    for block in range(count):
        diff = scal[0] ^ block
        slot = 0
        for bit in range(nbits):
            slot = slot | (((diff >> bit) & 1) << (nbits - 1 - bit))
        rows = slice(block * local, (block + 1) * local)
        dkv_ref[slot, :, pl.ds(kcol, HEAD_DIM)] = (dk_acc[rows, :] * scale).astype(jnp.bfloat16)
        dkv_ref[slot, :, pl.ds(vcol, HEAD_DIM)] = dv_acc[rows, :].astype(jnp.bfloat16)

def attend_back(scalars, q, tiles, qid, kid, mixture, mix_grad, lse, pieces, per_shard):
    tokens, width = q.shape
    heads = width // HEAD_DIM
    length = kid.shape[0]
    count = sum(p.shape[0] for p in pieces)
    n_tiles = tiles.shape[1]
    kvw = pieces[0].shape[-1]
    fn = lambda scal, *refs: backward_kernel(scal, per_shard, len(pieces), *refs)
    head_block = pl.BlockSpec((tokens, HEAD_DIM), lambda h, s: (0, h))
    tile_block = pl.BlockSpec((1, n_tiles, TILE, TILE), lambda h, s: (h, 0, 0, 0))
    return pl.pallas_call(
        fn,
        grid_spec=pltpu.PrefetchScalarGridSpec(
            num_scalar_prefetch=1, grid=(heads,),
            in_specs=[head_block, tile_block,
                pl.BlockSpec((1, tokens), lambda h, s: (0, 0)),
                pl.BlockSpec((length, 1), lambda h, s: (0, 0)),
                head_block, head_block,
                pl.BlockSpec((1, 1, tokens), lambda h, s: (h, 0, 0)),
            ] + [pl.BlockSpec(memory_space=pl.ANY)] * len(pieces),
            out_specs=[head_block,
                pl.BlockSpec((count, length // count, kvw), lambda h, s: (0, 0, 0)),
                tile_block],
            scratch_shapes=[pltpu.VMEM((length, kvw), jnp.bfloat16), pltpu.VMEM((length, HEAD_DIM), jnp.float32), pltpu.VMEM((length, HEAD_DIM), jnp.float32), pltpu.SemaphoreType.DMA((count,))],
        ),
        out_shape=[jax.ShapeDtypeStruct((tokens, width), jnp.bfloat16),
                   jax.ShapeDtypeStruct((count, length // count, kvw), jnp.bfloat16),
                   jax.ShapeDtypeStruct(tiles.shape, jnp.float32)],
        compiler_params=pltpu.CompilerParams(vmem_limit_bytes=50 * 1024 * 1024),
        cost_estimate=pl.CostEstimate(flops=10 * heads * tokens * length * HEAD_DIM, transcendentals=heads*tokens*length, bytes_accessed=2*heads*n_tiles*TILE*TILE*4),
    )(scalars, q, tiles, qid, kid, mixture, mix_grad, lse, *pieces)


EPSILON = 1e-05
KERNEL = 5
HIGHEST = lax.Precision.HIGHEST


def bits(count):
    return list(range(count.bit_length() - 1))


def swap(array, axis, bit):
    count = lax.axis_size(axis)
    return lax.ppermute(array, axis, [(i, i ^ (1 << bit)) for i in range(count)])


def bit_of(axis, bit):
    return (lax.axis_index(axis) >> bit) & 1


def row_dims(axes):
    return [(axis, bit) for axis in axes for bit in reversed(bits(lax.axis_size(axis)))]


def orders():
    seq = [("seq", bit) for bit in reversed(bits(lax.axis_size("seq")))]
    dp = [("dp", bit) for bit in reversed(bits(lax.axis_size("dp")))]
    near, far = seq[-1:], seq[:-1]
    return dp + far + near, far + dp + near


def gather_rows(piece, order, axes=("dp", "seq")):
    dims = row_dims(axes)
    array = piece.reshape((1,) * len(dims) + piece.shape)
    for axis, bit in order:
        dim = dims.index((axis, bit))
        other = swap(array, axis, bit)
        lower = bit_of(axis, bit) == 0
        array = jnp.concatenate(
            [jnp.where(lower, array, other), jnp.where(lower, other, array)], axis=dim
        )
    return array.reshape(-1, piece.shape[-1])


def own_rows(array, axes=("dp", "seq")):
    count = math.prod(lax.axis_size(axis) for axis in axes)
    part = array.shape[0] // count
    return lax.dynamic_slice_in_dim(array, lax.axis_index(axes) * part, part, 0)


def outer(left, right):
    return lax.dot_general(
        left, right, (((0,), (0,)), ((), ())), preferred_element_type=jnp.float32
    )


def plain(left, right):
    return jnp.dot(left, right, preferred_element_type=jnp.float32)


def against(left, right):
    return lax.dot_general(
        left, right, (((1,), (1,)), ((), ())), preferred_element_type=jnp.float32
    )


def scatter_rows(low, right, order, axes=("dp", "seq")):
    dims = row_dims(axes)
    tokens, rows = low.shape
    part = rows >> len(dims)
    (axis, bit), later = order[0], order[1:]
    dim = dims.index((axis, bit))
    stride = part << (len(dims) - 1 - dim)
    pairs = rows // (2 * stride)
    lower = bit_of(axis, bit) == 0
    first = [low[:, (2 * i) * stride : (2 * i + 1) * stride] for i in range(pairs)]
    second = [low[:, (2 * i + 1) * stride : (2 * i + 2) * stride] for i in range(pairs)]
    first, second = jnp.concatenate(first, 1), jnp.concatenate(second, 1)
    sent = outer(jnp.where(lower, second, first), right).astype(jnp.bfloat16)
    came = swap(sent, axis, bit)
    array = outer(jnp.where(lower, first, second), right) + came.astype(jnp.float32)
    shape = [2] * len(dims) + [part, right.shape[1]]
    shape[dim] = 1
    array = array.reshape(shape)
    for axis, bit in later:
        array = array.astype(jnp.bfloat16)
        dim = dims.index((axis, bit))
        here = bit_of(axis, bit)
        kept = lax.dynamic_index_in_dim(array, here, dim)
        sent = lax.dynamic_index_in_dim(array, 1 - here, dim)
        array = kept.astype(jnp.float32) + swap(sent, axis, bit).astype(jnp.float32)
    return array.reshape(part, right.shape[1])


def norm_forward(values, gain_vec):
    centred = values - jnp.mean(values, axis=-1, keepdims=True)
    inverse = lax.rsqrt(jnp.mean(centred * centred, axis=-1, keepdims=True) + EPSILON)
    normed = centred * inverse
    return (normed * gain_vec.astype(jnp.float32), normed, inverse)


def norm_backward(gradient, normed, inverse, gain_vec):
    scaled = gradient * gain_vec.astype(jnp.float32)
    mean_grad = jnp.mean(scaled, axis=-1, keepdims=True)
    second = jnp.mean(scaled * normed, axis=-1, keepdims=True)
    gain_grad = jnp.sum((gradient * normed).reshape(-1, gradient.shape[-1]), axis=0)
    return (inverse * (scaled - mean_grad - normed * second), gain_grad)


def silu_slope(values):
    sigmoid = jax.nn.sigmoid(values)
    return sigmoid * (1.0 + values * (1.0 - sigmoid))


def team_sum(partial):
    for bit in bits(lax.axis_size("heads"))[:-1]:
        partial = partial + swap(partial.astype(jnp.bfloat16), "heads", bit).astype(jnp.float32)
    return partial


def sum_everyone(array):
    for axis in ("seq", "dp", "heads"):
        for bit in bits(lax.axis_size(axis)):
            array = array + swap(array, axis, bit)
    return array


def far_swap(array):
    return swap(array, "heads", bits(lax.axis_size("heads"))[-1])


def ffn_forward(stream, gain_vec, weights):
    normed_out, normed, inverse = norm_forward(stream, gain_vec)
    low = normed_out.astype(jnp.bfloat16)
    pres, acts, partial = [], [], 0.0
    for weight_in, weight_out in weights:
        pre = plain(low, weight_in)
        act = jax.nn.silu(pre).astype(jnp.bfloat16)
        partial = partial + plain(act, weight_out)
        pres.append(pre)
        acts.append(act)
    return (stream + 0.5 * team_sum(partial), (normed, inverse, low, pres, acts))


def ffn_backward(gradient, saved_state, gain_vec, weights):
    normed, inverse, low, pres, acts = saved_state
    order_a, order_b = orders()
    branch_low = (0.5 * gradient).astype(jnp.bfloat16)
    partial, pre_lows = 0.0, []
    for (weight_in, weight_out), pre in zip(weights, pres):
        pre_low = (against(branch_low, weight_out) * silu_slope(pre)).astype(jnp.bfloat16)
        partial = partial + against(pre_low, weight_in)
        pre_lows.append(pre_low)
    normed_grad = team_sum(partial)
    out_grad = scatter_rows(branch_low, jnp.concatenate(acts, 1), order_b[::-1])
    in_grad = scatter_rows(low, jnp.concatenate(pre_lows, 1), order_a[::-1])
    stream_part, gain_grad = norm_backward(normed_grad, normed, inverse, gain_vec)
    hidden = in_grad.shape[1] // 2
    came = far_swap(
        jnp.concatenate([in_grad[:, hidden:], out_grad[:, hidden:]], 1).astype(jnp.bfloat16)
    ).astype(jnp.float32)
    in_grad = in_grad[:, :hidden] + came[:, :hidden]
    out_grad = (out_grad[:, :hidden] + came[:, hidden:]).T
    return (gradient + stream_part, gain_grad, in_grad, out_grad)


def halo(array, reach):
    peers, length = lax.axis_size("seq"), array.shape[0]
    up = [(i, i + 1) for i in range(peers - 1)]
    down = [(j, i) for i, j in up]
    before = lax.ppermute(array[length - reach :], "seq", up)
    after = lax.ppermute(array[:reach], "seq", down)
    return jnp.concatenate([before, array, after], axis=0)


def conv_forward(stream, window_ids, weights):
    in_weight, out_weight, taps, gain_one, gain_two = weights
    tokens, width = stream.shape
    reach = KERNEL // 2
    normed_out, normed, inverse = norm_forward(stream, gain_one)
    low = normed_out.astype(jnp.bfloat16)
    doubled = plain(low, in_weight)
    gate = jax.nn.sigmoid(doubled[:, width:])
    glu_low = (doubled[:, :width] * gate).astype(jnp.bfloat16)
    padded = halo(glu_low, reach)
    centre = window_ids[reach : reach + tokens]
    taps_float = taps.astype(jnp.float32)
    depth = jnp.zeros((tokens, width), jnp.float32)
    for k in range(KERNEL):
        same = (window_ids[k : k + tokens] == centre).astype(jnp.float32)[:, None]
        depth = depth + padded[k : k + tokens].astype(jnp.float32) * taps_float[k] * same
    norm_two, hat_two, inverse_two = norm_forward(depth, gain_two)
    swish_low = jax.nn.silu(norm_two).astype(jnp.bfloat16)
    branch = plain(swish_low, out_weight)
    saved = (normed, inverse, low, doubled, gate, padded, hat_two, inverse_two, norm_two, swish_low)
    return (stream + branch, saved)


def conv_backward(gradient, saved, window_ids, weights):
    in_weight, out_weight, taps, gain_one, gain_two = weights
    normed, inverse, low, doubled, gate, padded, hat_two, inverse_two, norm_two, swish_low = saved
    tokens, width = gradient.shape
    reach = KERNEL // 2
    branch_low = gradient.astype(jnp.bfloat16)
    swish_grad = against(branch_low, out_weight)
    depth_grad, gain_two_grad = norm_backward(
        swish_grad * silu_slope(norm_two), hat_two, inverse_two, gain_two
    )
    depth_low = depth_grad.astype(jnp.bfloat16)
    beside = halo(depth_low, reach)
    centre = window_ids[reach : reach + tokens]
    taps_float = taps.astype(jnp.float32)
    depth_float = depth_low.astype(jnp.float32)
    glu_grad = jnp.zeros((tokens, width), jnp.float32)
    tap_grads = []
    for k in range(KERNEL):
        same = (window_ids[k : k + tokens] == centre).astype(jnp.float32)[:, None]
        tap_grads.append(
            jnp.sum(depth_float * padded[k : k + tokens].astype(jnp.float32) * same, axis=0)
        )
        mirror = 2 * reach - k
        back = (window_ids[mirror : mirror + tokens] == centre).astype(jnp.float32)[:, None]
        glu_grad = (
            glu_grad + beside[mirror : mirror + tokens].astype(jnp.float32) * taps_float[k] * back
        )
    gate_in = doubled[:, :width]
    doubled_low = jnp.concatenate(
        [glu_grad * gate, glu_grad * gate_in * gate * (1.0 - gate)], axis=-1
    ).astype(jnp.bfloat16)
    normed_grad = against(doubled_low, in_weight)
    team = lax.axis_size("heads") // 2
    share = tokens // team
    mine = (lax.axis_index("heads") % team) * share
    cut = lambda array: lax.dynamic_slice_in_dim(array, mine, share, 0)
    order_a, order_b = orders()
    axes = ("dp", "seq", "heads")
    heads = [("heads", bit) for bit in reversed(bits(lax.axis_size("heads")))]
    out_grad = scatter_rows(cut(swish_low), cut(branch_low), order_b[::-1] + heads, axes)
    in_grad = scatter_rows(cut(low), cut(doubled_low), order_a[::-1] + heads, axes)
    part, gain_one_grad = norm_backward(normed_grad, normed, inverse, gain_one)
    small = [gain_one_grad, gain_two_grad] + tap_grads
    return (gradient + part, in_grad, out_grad, small)


def on_device(
    frames,
    segment_ids,
    bucket_of,
    ffn1_gain,
    ffn1_in,
    ffn1_out,
    attn_gain,
    query_weight,
    key_weight,
    value_weight,
    output_weight,
    position_table,
    conv_gain,
    pointwise_in,
    depthwise,
    depth_gain,
    pointwise_out,
    ffn2_gain,
    ffn2_in,
    ffn2_out,
    final_gain,
    cotangent,
):
    row_count, local, width = frames.shape
    length = segment_ids.shape[1]
    n_heads = lax.axis_size("heads")
    team = n_heads // 2
    place = lax.axis_index("heads")
    seq_at = lax.axis_index("seq")
    rows_mine = row_count // 2
    my_row = place // team
    order_a, order_b = orders()
    bf16 = jnp.bfloat16

    far_in = gather_rows(far_swap(own_rows(ffn1_in)), order_a)
    far_out = gather_rows(far_swap(own_rows(ffn1_out)), order_b)
    ffn1_weights = [(ffn1_in, ffn1_out), (far_in, far_out)]
    qkv = jnp.concatenate([query_weight, key_weight, value_weight], axis=1)
    out_cols = output_weight.shape[0]
    groups = lax.axis_size("dp") * lax.axis_size("seq")
    group_at = lax.axis_index(("dp", "seq"))
    part = width // groups
    out_piece = lax.dynamic_slice_in_dim(output_weight, group_at * part, part, 1).T
    attn_piece = far_swap(jnp.concatenate([own_rows(qkv), out_piece], axis=1))
    small_piece = jnp.concatenate([depthwise, conv_gain[None], depth_gain[None]], axis=0).T
    small_piece = jnp.pad(small_piece, ((0, 0), (0, 128 - small_piece.shape[1])))
    conv_piece = jnp.concatenate([pointwise_in, pointwise_out, small_piece], axis=1)
    for bit in bits(n_heads):
        other = swap(conv_piece, "heads", bit)
        lower = bit_of("heads", bit) == 0
        conv_piece = jnp.concatenate(
            [jnp.where(lower, conv_piece, other), jnp.where(lower, other, conv_piece)], axis=0
        )
    group_a = gather_rows(
        jnp.concatenate([attn_piece, conv_piece[:, 2 * width :]], axis=1), order_a
    )
    pw_in = gather_rows(conv_piece[:, : 2 * width], order_b)
    n_qkv = qkv.shape[1]
    far_qkv = group_a[:, :n_qkv]
    far_output = group_a[:, n_qkv : n_qkv + out_cols]
    pw_out = group_a[:, n_qkv + out_cols : n_qkv + out_cols + width]
    small_all = group_a[:, n_qkv + out_cols + width :][:, : KERNEL + 2].T
    far_in2 = gather_rows(far_swap(own_rows(ffn2_in)), order_a)
    far_out2 = gather_rows(far_swap(own_rows(ffn2_out)), order_b)
    ffn2_weights = [(ffn2_in, ffn2_out), (far_in2, far_out2)]
    taps, conv_gain_all, depth_gain_all = (
        small_all[:KERNEL],
        small_all[KERNEL],
        small_all[KERNEL + 1],
    )
    conv_weights = (pw_in, pw_out, taps, conv_gain_all, depth_gain_all)

    table = jnp.concatenate([position_table, far_swap(position_table)], axis=0)
    n_q, n_k = local // TILE, length // TILE
    reversed_buckets = jnp.pad(bucket_of[::-1], (0, 1))
    window = lax.dynamic_slice_in_dim(reversed_buckets, seq_at * local, (n_q + n_k) * TILE, 0)
    levels = lax.broadcasted_iota(jnp.int32, (position_table.shape[1], window.shape[0]), 0)
    onehot = (levels == window[None, :]).astype(jnp.float32)
    tiles = bias_tiles(jnp.dot(table, onehot, precision=HIGHEST) * LOG2E)

    outs = []
    for at in range(rows_mine):
        row = my_row * rows_mine + at
        pick = lambda array: lax.dynamic_index_in_dim(array, row, 0, keepdims=False)
        ids = pick(segment_ids)
        reach = KERNEL // 2
        ids_pad = jnp.pad(ids, (reach, reach), constant_values=-1)
        window_ids = lax.dynamic_slice_in_dim(ids_pad, seq_at * local, local + 2 * reach, 0)
        query_ids = window_ids[reach : reach + local]
        scalars = [seq_at.astype(jnp.int32)]
        for block in range(n_q):
            low_id = query_ids[block * TILE]
            top_id = query_ids[(block + 1) * TILE - 1]
            scalars.append(jnp.sum((ids < low_id).astype(jnp.int32)) // TILE)
            scalars.append((jnp.sum((ids <= top_id).astype(jnp.int32)) + TILE - 1) // TILE)
        scalars = jnp.stack(scalars)

        stream_zero = pick(frames).astype(jnp.float32)
        stream_one, ffn1_state = ffn_forward(stream_zero, ffn1_gain, ffn1_weights)

        normed_out, normed, inverse = norm_forward(stream_one, attn_gain)
        low = normed_out.astype(bf16)
        q_cols = query_weight.shape[1]
        kv = jnp.concatenate(
            [plain(low, qkv[:, q_cols:]).astype(bf16), plain(low, far_qkv[:, q_cols:]).astype(bf16)],
            axis=1,
        )[None]
        pieces = [kv]
        for bit in reversed(bits(lax.axis_size("seq"))):
            held = pieces[0] if len(pieces) == 1 else jnp.concatenate(pieces, axis=0)
            pieces.append(swap(held, "seq", bit))
        query = jnp.concatenate(
            [plain(low, qkv[:, :q_cols]).astype(bf16), plain(low, far_qkv[:, :q_cols]).astype(bf16)],
            axis=1,
        )
        per_shard = q_cols // HEAD_DIM
        mixture, log_total = attend(
            scalars, query, tiles, query_ids[None], ids[:, None], pieces, per_shard
        )
        branch = team_sum(
            plain(mixture[:, :out_cols], output_weight)
            + against(mixture[:, out_cols:], far_output)
        )
        stream_two = stream_one + branch

        stream_three, conv_state = conv_forward(stream_two, window_ids, conv_weights)
        stream_four, ffn2_state = ffn_forward(stream_three, ffn2_gain, ffn2_weights)
        final_out, final_hat, final_inverse = norm_forward(stream_four, final_gain)
        layer_low = final_out.astype(bf16)
        grad_four, final_gain_grad = norm_backward(
            pick(cotangent).astype(jnp.float32), final_hat, final_inverse, final_gain
        )
        grad_three, ffn2_gain_grad, f2_in_g, f2_out_g = ffn_backward(
            grad_four, ffn2_state, ffn2_gain, ffn2_weights
        )
        grad_two, pw_in_g, pw_out_g, conv_small = conv_backward(
            grad_three, conv_state, window_ids, conv_weights
        )

        branch_low = grad_two.astype(bf16)
        mix_grad = jnp.concatenate(
            [
                against(branch_low, output_weight).astype(bf16),
                plain(branch_low, far_output).astype(bf16),
            ],
            axis=1,
        )
        q_grad, kv_grad, tile_grads = attend_back(
            scalars, query, tiles, query_ids[None], ids[:, None], mixture, mix_grad, log_total, pieces, per_shard
        )
        for bit in bits(lax.axis_size("seq")):
            half = kv_grad.shape[0] // 2
            kv_grad = (
                kv_grad[:half].astype(jnp.float32)
                + swap(kv_grad[half:], "seq", bit).astype(jnp.float32)
            ).astype(bf16)
        kv_grad = kv_grad[0]
        kv_cols = 2 * q_cols
        own_grads = jnp.concatenate([q_grad[:, :q_cols], kv_grad[:, :kv_cols]], axis=1)
        far_grads = jnp.concatenate([q_grad[:, q_cols:], kv_grad[:, kv_cols:]], axis=1)
        normed_grad = team_sum(against(own_grads, qkv) + against(far_grads, far_qkv))
        o_g = scatter_rows(branch_low, mixture, order_b[::-1])
        qkv_g = scatter_rows(low, jnp.concatenate([own_grads, far_grads], 1), order_a[::-1])
        came = far_swap(
            jnp.concatenate([qkv_g[:, n_qkv:], o_g[:, out_cols:]], 1).astype(bf16)
        ).astype(jnp.float32)
        qkv_g = qkv_g[:, :n_qkv] + came[:, :n_qkv]
        o_g = (o_g[:, :out_cols] + came[:, n_qkv:]).T
        table_grad = lax.dot_general(
            offset_sums(tile_grads), onehot, (((1,), (1,)), ((), ())), precision=HIGHEST
        )
        stream_part, attn_gain_grad = norm_backward(normed_grad, normed, inverse, attn_gain)
        grad_one = grad_two + stream_part
        grad_zero, ffn1_gain_grad, f1_in_g, f1_out_g = ffn_backward(
            grad_one, ffn1_state, ffn1_gain, ffn1_weights
        )
        big = (f1_in_g, f1_out_g, qkv_g, o_g, pw_in_g, pw_out_g, f2_in_g, f2_out_g)
        gains = [ffn2_gain_grad, final_gain_grad] + conv_small
        outs.append((layer_low, grad_zero, big, gains, table_grad, ffn1_gain_grad, attn_gain_grad))

    total = lambda items: functools.reduce(lambda one, two: one + two, items)
    big = [total([out[2][i] for out in outs]) for i in range(8)]
    f1_in_g, f1_out_g, qkv_g, o_g, pw_in_g, pw_out_g, f2_in_g, f2_out_g = big
    gains = [total([out[3][i] for out in outs]) for i in range(len(outs[0][3]))]
    table_grad = total([out[4] for out in outs])
    per_shard = position_table.shape[0]
    all_heads = jnp.zeros((n_heads * per_shard, position_table.shape[1]), jnp.float32)
    all_heads = lax.dynamic_update_slice_in_dim(
        all_heads, team * table_grad[:per_shard], place * per_shard, 0
    )
    all_heads = lax.dynamic_update_slice_in_dim(
        all_heads, team * table_grad[per_shard:], (place ^ team) * per_shard, 0
    )
    small = jnp.concatenate([jnp.stack(gains).reshape(-1), all_heads.reshape(-1)])
    small = small.reshape(-1, 128) * (1.0 / team)
    everyone = ("dp", "seq", "heads")
    small = sum_everyone(small).reshape(-1)
    gains_all = small[: len(gains) * width].reshape(len(gains), width)
    table_all = small[len(gains) * width :].reshape(all_heads.shape)
    table_mine = lax.dynamic_slice_in_dim(table_all, place * per_shard, per_shard, 0)
    table_cols = table_mine.shape[1] // groups
    table_mine = lax.dynamic_slice_in_dim(table_mine, group_at * table_cols, table_cols, 1)
    group_part = lax.dynamic_slice_in_dim(gains_all[:2], group_at * part, part, 1)
    every = width // (groups * n_heads)
    conv_part = lax.dynamic_slice_in_dim(
        gains_all[2:], lax.axis_index(everyone) * every, every, 1
    )
    last = jnp.stack([total([out[5] for out in outs]), total([out[6] for out in outs])])
    last = last.reshape(-1, 128) * (1.0 / team)
    last = sum_everyone(last).reshape(2, width)
    last_part = lax.dynamic_slice_in_dim(last, group_at * part, part, 1)

    def both_rows(pieces):
        mine = jnp.stack(pieces)
        other = far_swap(mine.astype(bf16)).astype(mine.dtype)
        first = my_row == 0
        return jnp.concatenate([jnp.where(first, mine, other), jnp.where(first, other, mine)], 0)

    layer_out = both_rows([out[0] for out in outs])
    input_grad = both_rows([out[1] for out in outs])
    q_cols = query_weight.shape[1]
    return (
        layer_out,
        input_grad,
        last_part[0],
        f1_in_g,
        f1_out_g,
        last_part[1],
        qkv_g[:, :q_cols],
        qkv_g[:, q_cols : 2 * q_cols],
        qkv_g[:, 2 * q_cols :],
        o_g,
        table_mine,
        conv_part[0],
        pw_in_g,
        conv_part[2:],
        conv_part[1],
        pw_out_g,
        group_part[0],
        f2_in_g,
        f2_out_g,
        group_part[1],
    )


def solution(mesh):
    return jax.shard_map(
        on_device,
        mesh=mesh,
        in_specs=(
            P("dp", "seq", None),
            P("dp", None),
            P(),
            P(),
            P(None, "heads"),
            P("heads", None),
            P(),
            P(None, "heads"),
            P(None, "heads"),
            P(None, "heads"),
            P("heads", None),
            P("heads", None),
            P(("dp", "seq", "heads")),
            P(("dp", "seq", "heads"), None),
            P(None, ("dp", "seq", "heads")),
            P(("dp", "seq", "heads")),
            P(("dp", "seq", "heads"), None),
            P(),
            P(None, "heads"),
            P("heads", None),
            P(),
            P("dp", "seq", None),
        ),
        out_specs=(
            P("dp", "seq", None),
            P("dp", "seq", None),
            P(("dp", "seq")),
            P(("dp", "seq"), "heads"),
            P("heads", ("dp", "seq")),
            P(("dp", "seq")),
            P(("dp", "seq"), "heads"),
            P(("dp", "seq"), "heads"),
            P(("dp", "seq"), "heads"),
            P("heads", ("dp", "seq")),
            P("heads", ("dp", "seq")),
            P(("dp", "seq", "heads")),
            P(("dp", "seq", "heads"), None),
            P(None, ("dp", "seq", "heads")),
            P(("dp", "seq", "heads")),
            P(("dp", "seq", "heads"), None),
            P(("dp", "seq")),
            P(("dp", "seq"), "heads"),
            P("heads", ("dp", "seq")),
            P(("dp", "seq")),
        ),
        check_vma=False,
    )
```

```python
import math
import jax
import jax.numpy as jnp
from jax import lax
from jax.experimental import pallas as pl
from jax.experimental.pallas import tpu as pltpu
from jax.sharding import PartitionSpec as P

HEAD_DIM=128
NEGATIVE=-1e30
LOG2E=math.log2(math.e)
TILE=256

def bias_tiles_kernel(win_ref, out_ref):
    width = win_ref.shape[2]
    rows = jnp.broadcast_to(win_ref[0], (8, width))
    rows = pltpu.roll(rows, width - (TILE - 1), 1, stride=1, stride_axis=0)
    step = 8
    while step < TILE:
        rows = jnp.concatenate([rows, pltpu.roll(rows, step, 1)], axis=0)
        step *= 2
    for t in range(out_ref.shape[1]):
        out_ref[0, t] = rows[:, t * TILE : (t + 1) * TILE]

def bias_tiles(window):
    heads, width = window.shape
    tiles = width // TILE - 1
    return pl.pallas_call(
        bias_tiles_kernel,
        grid=(heads,),
        in_specs=[pl.BlockSpec((1, 1, width), lambda h: (h, 0, 0))],
        out_specs=pl.BlockSpec((1, tiles, TILE, TILE), lambda h: (h, 0, 0, 0)),
        out_shape=jax.ShapeDtypeStruct((heads, tiles, TILE, TILE), jnp.float32),
        cost_estimate=pl.CostEstimate(flops=heads*tiles*TILE*TILE*4, transcendentals=0, bytes_accessed=heads*tiles*TILE*TILE*4),
    )(window[:, None])

def offset_sums_kernel(tiles_ref, out_ref, wide):
    tiles = tiles_ref.shape[1]
    for t in range(tiles):
        wide[:, t * TILE : (t + 1) * TILE] = tiles_ref[0, t]
    wide[:, tiles * TILE :] = jnp.zeros((TILE, TILE), jnp.float32)
    rows = wide[...]
    half = TILE // 2
    while half >= 1:
        rows = pltpu.roll(rows[:half], half, 1) + rows[half:]
        half //= 2
    out_ref[0] = rows

def offset_sums(tile_grads):
    heads, tiles = tile_grads.shape[:2]
    width = (tiles + 1) * TILE
    return pl.pallas_call(
        offset_sums_kernel,
        grid=(heads,),
        in_specs=[pl.BlockSpec((1, tiles, TILE, TILE), lambda h: (h, 0, 0, 0))],
        out_specs=pl.BlockSpec((1, 1, width), lambda h: (h, 0, 0)),
        out_shape=jax.ShapeDtypeStruct((heads, 1, width), jnp.float32),
        scratch_shapes=[pltpu.VMEM((TILE, width), jnp.float32)],
        cost_estimate=pl.CostEstimate(flops=heads*tiles*TILE*TILE*4, transcendentals=0, bytes_accessed=heads*tiles*TILE*TILE*4),
    )(tile_grads)[:, 0]

def columns_of(head, per_shard):
    shard, at = head // per_shard, head % per_shard
    key = (shard * 2 * per_shard + at) * HEAD_DIM
    value = key + per_shard * HEAD_DIM
    return pl.multiple_of(key, HEAD_DIM), pl.multiple_of(value, HEAD_DIM)

def load_pieces(scal, pieces, whole, sems):
    local = pieces[0].shape[1]
    copies = []
    count = sum(p.shape[0] for p in pieces)
    nbits = count.bit_length() - 1
    rel = [0]
    n = 0
    for p in pieces:
        ids = [0] if p is pieces[0] else None
        if ids is None:
            bit = nbits - 1 - (n.bit_length() - 1)
            ids = [r ^ (1 << bit) for r in rel]
            rel = rel + ids
        for k, r in enumerate(ids):
            at = pl.multiple_of((scal[0] ^ r) * local, local)
            copies.append(pltpu.make_async_copy(p.at[k], whole.at[pl.ds(at, local)], sems.at[n]))
            n += 1
    for c in copies: c.start()
    for c in copies: c.wait()

def forward_kernel(scal, per_shard, pieces_n, *refs):
    q_ref, bias_ref, qid_ref, kid_ref = refs[:4]
    pieces = refs[4 : 4 + pieces_n]
    out_ref, lse_ref, whole, sems = refs[4 + pieces_n :]
    head = pl.program_id(0)
    @pl.when(head == 0)
    def _(): load_pieces(scal, pieces, whole, sems)
    kcol, vcol = columns_of(head, per_shard)
    scale = LOG2E * HEAD_DIM ** -0.5
    nk = whole.shape[0] // TILE
    for qb in range(q_ref.shape[0] // TILE):
        q = q_ref[qb * TILE : (qb + 1) * TILE, :]
        qid = qid_ref[:, qb * TILE : (qb + 1) * TILE]
        def body(kb, carry):
            top, total, acc = carry
            at = pl.multiple_of(kb * TILE, TILE)
            k = whole[pl.ds(at, TILE), pl.ds(kcol, HEAD_DIM)]
            v = whole[pl.ds(at, TILE), pl.ds(vcol, HEAD_DIM)]
            s = lax.dot_general(k, q, (((1,), (1,)), ((), ())), preferred_element_type=jnp.float32)
            s = s * scale + bias_ref[0, qb - kb + nk - 1]
            s = jnp.where(kid_ref[pl.ds(at, TILE), :] == qid, s, NEGATIVE)
            new_top = jnp.maximum(top, jnp.max(s, axis=0, keepdims=True))
            p = jnp.exp2(s - new_top)
            fade = jnp.exp2(top - new_top)
            total = total * fade + jnp.sum(p, axis=0, keepdims=True)
            acc = acc * fade + lax.dot_general(v, p.astype(jnp.bfloat16), (((0,), (0,)), ((), ())), preferred_element_type=jnp.float32)
            return new_top, total, acc
        top, total, acc = lax.fori_loop(scal[1 + 2 * qb], scal[2 + 2 * qb], body, (
            jnp.full((1, TILE), NEGATIVE, jnp.float32), jnp.zeros((1, TILE), jnp.float32), jnp.zeros((HEAD_DIM, TILE), jnp.float32)))
        out_ref[qb * TILE : (qb + 1) * TILE, :] = (acc / total).T.astype(jnp.bfloat16)
        lse_ref[0, :, qb * TILE : (qb + 1) * TILE] = top + jnp.log2(total)

def attend(scalars, q, tiles, qid, kid, pieces, per_shard):
    tokens, width = q.shape
    heads = width // HEAD_DIM
    length = kid.shape[0]
    count = sum(p.shape[0] for p in pieces)
    n_tiles = tiles.shape[1]
    fn = lambda scal, *refs: forward_kernel(scal, per_shard, len(pieces), *refs)
    flops = 4 * heads * tokens * length * HEAD_DIM
    return pl.pallas_call(
        fn,
        grid_spec=pltpu.PrefetchScalarGridSpec(
            num_scalar_prefetch=1, grid=(heads,),
            in_specs=[
                pl.BlockSpec((tokens, HEAD_DIM), lambda h, s: (0, h)),
                pl.BlockSpec((1, n_tiles, TILE, TILE), lambda h, s: (h, 0, 0, 0)),
                pl.BlockSpec((1, tokens), lambda h, s: (0, 0)),
                pl.BlockSpec((length, 1), lambda h, s: (0, 0)),
            ] + [pl.BlockSpec(memory_space=pl.ANY)] * len(pieces),
            out_specs=[
                pl.BlockSpec((tokens, HEAD_DIM), lambda h, s: (0, h)),
                pl.BlockSpec((1, 1, tokens), lambda h, s: (h, 0, 0)),
            ],
            scratch_shapes=[pltpu.VMEM((length, pieces[0].shape[-1]), jnp.bfloat16), pltpu.SemaphoreType.DMA((count,))],
        ),
        out_shape=[jax.ShapeDtypeStruct((tokens, width), jnp.bfloat16), jax.ShapeDtypeStruct((heads, 1, tokens), jnp.float32)],
        cost_estimate=pl.CostEstimate(flops=flops, transcendentals=heads*tokens*length, bytes_accessed=heads*n_tiles*TILE*TILE*4),
    )(scalars, q, tiles, qid, kid, *pieces)

def backward_kernel(scal, per_shard, pieces_n, *refs):
    q_ref, bias_ref, qid_ref, kid_ref, mix_ref, dmix_ref, lse_ref = refs[:7]
    pieces = refs[7 : 7 + pieces_n]
    dq_ref, dkv_ref, dtile_ref, whole, dk_acc, dv_acc, sems = refs[7 + pieces_n :]
    head = pl.program_id(0)
    @pl.when(head == 0)
    def _(): load_pieces(scal, pieces, whole, sems)
    kcol, vcol = columns_of(head, per_shard)
    scale = HEAD_DIM ** -0.5
    nk = whole.shape[0] // TILE
    dk_acc[...] = jnp.zeros_like(dk_acc)
    dv_acc[...] = jnp.zeros_like(dv_acc)
    dtile_ref[...] = jnp.zeros_like(dtile_ref)
    for qb in range(q_ref.shape[0] // TILE):
        rows = slice(qb * TILE, (qb + 1) * TILE)
        q = q_ref[rows, :]
        qid = qid_ref[:, rows]
        dmix = dmix_ref[rows, :]
        lse = lse_ref[0, :, rows]
        delta = jnp.sum((dmix.astype(jnp.float32) * mix_ref[rows, :].astype(jnp.float32)).T, axis=0, keepdims=True)
        def body(kb, dq):
            at = pl.multiple_of(kb * TILE, TILE)
            k = whole[pl.ds(at, TILE), pl.ds(kcol, HEAD_DIM)]
            v = whole[pl.ds(at, TILE), pl.ds(vcol, HEAD_DIM)]
            s = lax.dot_general(k, q, (((1,), (1,)), ((), ())), preferred_element_type=jnp.float32)
            s = s * (scale * LOG2E) + bias_ref[0, qb - kb + nk - 1]
            s = jnp.where(kid_ref[pl.ds(at, TILE), :] == qid, s, NEGATIVE)
            p = jnp.exp2(s - lse)
            dp = lax.dot_general(v, dmix, (((1,), (1,)), ((), ())), preferred_element_type=jnp.float32)
            ds = p * (dp - delta)
            dtile_ref[0, qb - kb + nk - 1] += ds
            low = ds.astype(jnp.bfloat16)
            dv_acc[pl.ds(at, TILE), :] += jnp.dot(p.astype(jnp.bfloat16), dmix, preferred_element_type=jnp.float32)
            dk_acc[pl.ds(at, TILE), :] += jnp.dot(low, q, preferred_element_type=jnp.float32)
            return dq + lax.dot_general(k, low, (((0,), (0,)), ((), ())), preferred_element_type=jnp.float32)
        dq = lax.fori_loop(scal[1 + 2 * qb], scal[2 + 2 * qb], body, jnp.zeros((HEAD_DIM, TILE), jnp.float32))
        dq_ref[rows, :] = (dq * scale).T.astype(jnp.bfloat16)
    count, local = dkv_ref.shape[:2]
    nbits = count.bit_length() - 1
    for block in range(count):
        diff = scal[0] ^ block
        slot = 0
        for bit in range(nbits):
            slot = slot | (((diff >> bit) & 1) << (nbits - 1 - bit))
        rows = slice(block * local, (block + 1) * local)
        dkv_ref[slot, :, pl.ds(kcol, HEAD_DIM)] = (dk_acc[rows, :] * scale).astype(jnp.bfloat16)
        dkv_ref[slot, :, pl.ds(vcol, HEAD_DIM)] = dv_acc[rows, :].astype(jnp.bfloat16)

def attend_back(scalars, q, tiles, qid, kid, mixture, mix_grad, lse, pieces, per_shard):
    tokens, width = q.shape
    heads = width // HEAD_DIM
    length = kid.shape[0]
    count = sum(p.shape[0] for p in pieces)
    n_tiles = tiles.shape[1]
    kvw = pieces[0].shape[-1]
    fn = lambda scal, *refs: backward_kernel(scal, per_shard, len(pieces), *refs)
    head_block = pl.BlockSpec((tokens, HEAD_DIM), lambda h, s: (0, h))
    tile_block = pl.BlockSpec((1, n_tiles, TILE, TILE), lambda h, s: (h, 0, 0, 0))
    return pl.pallas_call(
        fn,
        grid_spec=pltpu.PrefetchScalarGridSpec(
            num_scalar_prefetch=1, grid=(heads,),
            in_specs=[head_block, tile_block,
                pl.BlockSpec((1, tokens), lambda h, s: (0, 0)),
                pl.BlockSpec((length, 1), lambda h, s: (0, 0)),
                head_block, head_block,
                pl.BlockSpec((1, 1, tokens), lambda h, s: (h, 0, 0)),
            ] + [pl.BlockSpec(memory_space=pl.ANY)] * len(pieces),
            out_specs=[head_block,
                pl.BlockSpec((count, length // count, kvw), lambda h, s: (0, 0, 0)),
                tile_block],
            scratch_shapes=[pltpu.VMEM((length, kvw), jnp.bfloat16), pltpu.VMEM((length, HEAD_DIM), jnp.float32), pltpu.VMEM((length, HEAD_DIM), jnp.float32), pltpu.SemaphoreType.DMA((count,))],
        ),
        out_shape=[jax.ShapeDtypeStruct((tokens, width), jnp.bfloat16),
                   jax.ShapeDtypeStruct((count, length // count, kvw), jnp.bfloat16),
                   jax.ShapeDtypeStruct(tiles.shape, jnp.float32)],
        compiler_params=pltpu.CompilerParams(vmem_limit_bytes=50 * 1024 * 1024),
        cost_estimate=pl.CostEstimate(flops=10 * heads * tokens * length * HEAD_DIM, transcendentals=heads*tokens*length, bytes_accessed=2*heads*n_tiles*TILE*TILE*4),
    )(scalars, q, tiles, qid, kid, mixture, mix_grad, lse, *pieces)


EPSILON = 1e-05
KERNEL = 5
HIGHEST = lax.Precision.HIGHEST


def bits(count):
    return list(range(count.bit_length() - 1))


def swap(array, axis, bit):
    count = lax.axis_size(axis)
    return lax.ppermute(array, axis, [(i, i ^ (1 << bit)) for i in range(count)])


def bit_of(axis, bit):
    return (lax.axis_index(axis) >> bit) & 1


def gather_all(piece):
    return lax.all_gather(piece, ("dp", "seq"), axis=0, tiled=True)


def own_rows(array, axes=("dp", "seq")):
    count = math.prod(lax.axis_size(axis) for axis in axes)
    part = array.shape[0] // count
    return lax.dynamic_slice_in_dim(array, lax.axis_index(axes) * part, part, 0)


def outer(left, right):
    return lax.dot_general(
        left, right, (((0,), (0,)), ((), ())), preferred_element_type=jnp.float32
    )


def plain(left, right):
    return jnp.dot(left, right, preferred_element_type=jnp.float32)


def against(left, right):
    return lax.dot_general(
        left, right, (((1,), (1,)), ((), ())), preferred_element_type=jnp.float32
    )


def norm_forward(values, gain_vec):
    centred = values - jnp.mean(values, axis=-1, keepdims=True)
    inverse = lax.rsqrt(jnp.mean(centred * centred, axis=-1, keepdims=True) + EPSILON)
    normed = centred * inverse
    return (normed * gain_vec.astype(jnp.float32), normed, inverse)


def norm_backward(gradient, normed, inverse, gain_vec):
    scaled = gradient * gain_vec.astype(jnp.float32)
    mean_grad = jnp.mean(scaled, axis=-1, keepdims=True)
    second = jnp.mean(scaled * normed, axis=-1, keepdims=True)
    gain_grad = jnp.sum((gradient * normed).reshape(-1, gradient.shape[-1]), axis=0)
    return (inverse * (scaled - mean_grad - normed * second), gain_grad)


def silu_slope(values):
    sigmoid = jax.nn.sigmoid(values)
    return sigmoid * (1.0 + values * (1.0 - sigmoid))


def sum_everyone(array):
    for axis in ("seq", "dp", "heads"):
        for bit in bits(lax.axis_size(axis)):
            array = array + swap(array, axis, bit)
    return array


def after(array, *events):
    return lax.optimization_barrier((array,) + events)[0]


def far_swap(array):
    return swap(array, "heads", bits(lax.axis_size("heads"))[-1])


def team_bits():
    return bits(lax.axis_size("heads"))[:-1]


def gather_parts(own):
    parts = [own]
    for bit in team_bits():
        held = parts[0] if len(parts) == 1 else jnp.concatenate(parts, axis=0)
        parts.append(swap(held, "heads", bit))
    return parts


def reduce_parts(partials):
    partials = list(partials)
    for bit in reversed(team_bits()):
        came = swap(partials.pop().astype(jnp.bfloat16), "heads", bit).astype(jnp.float32)
        at, kept = 0, []
        for item in partials:
            kept.append(item + came[at : at + item.shape[0]])
            at += item.shape[0]
        partials = kept
    return partials[0]


def reorder(parts):
    team = lax.axis_size("heads") // 2
    mine = lax.axis_index("heads") % team
    whole = join(parts)
    block = whole.shape[0] // team
    if team == 2:
        first, second = parts
        lower = mine == 0
        return jnp.concatenate(
            [jnp.where(lower, first, second), jnp.where(lower, second, first)], axis=0
        )
    return jnp.concatenate(
        [lax.dynamic_slice_in_dim(whole, (at ^ mine) * block, block, 0) for at in range(team)],
        axis=0,
    )


def cut_parts(array):
    team = lax.axis_size("heads") // 2
    mine = lax.axis_index("heads") % team
    block = array.shape[0] // team
    take = lambda at: lax.dynamic_slice_in_dim(array, (at ^ mine) * block, block, 0)
    parts = [take(0)]
    for bit in team_bits():
        parts.append(join([take(at) for at in range(1 << bit, 2 << bit)]))
    return parts


def join(parts):
    return parts[0] if len(parts) == 1 else jnp.concatenate(parts, axis=0)


def scatter_groups(array):
    return lax.psum_scatter(array, ("dp", "seq"), scatter_dimension=0, tiled=True)


def grad_of(left, right):
    return outer(left, right).astype(jnp.bfloat16)


def ffn_forward(low_own, weights):
    lows = gather_parts(low_own)
    pres = [[plain(low, weight_in) for weight_in, _ in weights] for low in lows]
    acts = [[jax.nn.silu(pre).astype(jnp.bfloat16) for pre in pair] for pair in pres]
    partials = [
        sum(plain(act, weight_out) for act, (_, weight_out) in zip(pair, weights))
        for pair in acts
    ]
    return reduce_parts(partials), (lows, pres, acts)


def ffn_backward(gradient, saved, weights):
    lows, pres, acts = saved
    branches = gather_parts((0.5 * gradient).astype(jnp.bfloat16))
    pre_lows = [
        [
            (against(branch, weight_out) * silu_slope(pre)).astype(jnp.bfloat16)
            for (_, weight_out), pre in zip(weights, pair)
        ]
        for branch, pair in zip(branches, pres)
    ]
    partials = [
        sum(against(pre_low, weight_in) for pre_low, (weight_in, _) in zip(pair, weights))
        for pair in pre_lows
    ]
    normed_grad = reduce_parts(partials)
    low, branch = join(lows), join(branches)
    wide = lambda items: join([jnp.concatenate(pair, axis=1) for pair in items])
    grads = jnp.concatenate(
        [grad_of(branch, wide(acts)), grad_of(low, wide(pre_lows))], axis=1
    )
    return normed_grad, scatter_groups(grads)


def fold_far(array, far_cols, own_cols):
    came = far_swap(jnp.concatenate([array[:, a:b] for a, b in far_cols], axis=1))
    came, outs, at = came.astype(jnp.float32), [], 0
    for a, b in own_cols:
        outs.append(array[:, a:b].astype(jnp.float32) + came[:, at : at + b - a])
        at += b - a
    return outs


def halo(array, reach):
    peers, n_heads = lax.axis_size("seq"), lax.axis_size("heads")
    team = n_heads // 2
    spot = lambda row, at: (at // team) * n_heads + row * team + at % team
    up = [
        (spot(row, at), spot(row, at + 1))
        for row in range(2)
        for at in range(peers * team - 1)
    ]
    down = [(j, i) for i, j in up]
    before = lax.ppermute(array[array.shape[0] - reach :], ("seq", "heads"), up)
    after_it = lax.ppermute(array[:reach], ("seq", "heads"), down)
    return jnp.concatenate([before, array, after_it], axis=0)


def conv_forward(stream, window_ids, weights):
    in_weight, out_weight, taps, gain_one, gain_two = weights
    tokens, width = stream.shape
    reach = KERNEL // 2
    normed_out, normed, inverse = norm_forward(stream, gain_one)
    low = normed_out.astype(jnp.bfloat16)
    doubled = plain(low, in_weight)
    gate = jax.nn.sigmoid(doubled[:, width:])
    glu_low = (doubled[:, :width] * gate).astype(jnp.bfloat16)
    padded = halo(glu_low, reach)
    centre = window_ids[reach : reach + tokens]
    taps_float = taps.astype(jnp.float32)
    depth = jnp.zeros((tokens, width), jnp.float32)
    for k in range(KERNEL):
        same = (window_ids[k : k + tokens] == centre).astype(jnp.float32)[:, None]
        depth = depth + padded[k : k + tokens].astype(jnp.float32) * taps_float[k] * same
    norm_two, hat_two, inverse_two = norm_forward(depth, gain_two)
    swish_low = jax.nn.silu(norm_two).astype(jnp.bfloat16)
    branch = plain(swish_low, out_weight)
    saved = (normed, inverse, low, doubled, gate, padded, hat_two, inverse_two, norm_two, swish_low)
    return (stream + branch, saved)


def conv_backward(gradient, saved, window_ids, weights):
    in_weight, out_weight, taps, gain_one, gain_two = weights
    normed, inverse, low, doubled, gate, padded, hat_two, inverse_two, norm_two, swish_low = saved
    tokens, width = gradient.shape
    reach = KERNEL // 2
    branch_low = gradient.astype(jnp.bfloat16)
    swish_grad = against(branch_low, out_weight)
    depth_grad, gain_two_grad = norm_backward(
        swish_grad * silu_slope(norm_two), hat_two, inverse_two, gain_two
    )
    depth_low = depth_grad.astype(jnp.bfloat16)
    beside = halo(depth_low, reach)
    centre = window_ids[reach : reach + tokens]
    taps_float = taps.astype(jnp.float32)
    depth_float = depth_low.astype(jnp.float32)
    glu_grad = jnp.zeros((tokens, width), jnp.float32)
    tap_grads = []
    for k in range(KERNEL):
        same = (window_ids[k : k + tokens] == centre).astype(jnp.float32)[:, None]
        tap_grads.append(
            jnp.sum(depth_float * padded[k : k + tokens].astype(jnp.float32) * same, axis=0)
        )
        mirror = 2 * reach - k
        back = (window_ids[mirror : mirror + tokens] == centre).astype(jnp.float32)[:, None]
        glu_grad = (
            glu_grad + beside[mirror : mirror + tokens].astype(jnp.float32) * taps_float[k] * back
        )
    gate_in = doubled[:, :width]
    doubled_low = jnp.concatenate(
        [glu_grad * gate, glu_grad * gate_in * gate * (1.0 - gate)], axis=-1
    ).astype(jnp.bfloat16)
    normed_grad = against(doubled_low, in_weight)
    grads = scatter_groups(
        jnp.concatenate([grad_of(low, doubled_low), grad_of(swish_low, branch_low)], axis=1)
    )
    part, gain_one_grad = norm_backward(normed_grad, normed, inverse, gain_one)
    small = [gain_one_grad, gain_two_grad] + tap_grads
    return (gradient + part, grads, small)


def fold_heads(both):
    for bit in reversed(bits(lax.axis_size("heads"))):
        both = both.astype(jnp.bfloat16)
        half = both.shape[0] // 2
        here = bit_of("heads", bit) * half
        kept = lax.dynamic_slice_in_dim(both, here, half, 0)
        sent = lax.dynamic_slice_in_dim(both, half - here, half, 0)
        both = kept.astype(jnp.float32) + swap(sent, "heads", bit).astype(jnp.float32)
    return both


def on_device(
    frames,
    segment_ids,
    bucket_of,
    ffn1_gain,
    ffn1_in,
    ffn1_out,
    attn_gain,
    query_weight,
    key_weight,
    value_weight,
    output_weight,
    position_table,
    conv_gain,
    pointwise_in,
    depthwise,
    depth_gain,
    pointwise_out,
    ffn2_gain,
    ffn2_in,
    ffn2_out,
    final_gain,
    cotangent,
):
    row_count, local, width = frames.shape
    length = segment_ids.shape[1]
    n_heads = lax.axis_size("heads")
    team = n_heads // 2
    place = lax.axis_index("heads")
    seq_at = lax.axis_index("seq")
    assert row_count == 2
    my_row, mine = place // team, place % team
    block = local // team
    bf16 = jnp.bfloat16
    groups = lax.axis_size("dp") * lax.axis_size("seq")
    group_at = lax.axis_index(("dp", "seq"))
    part = width // groups

    own_qkv = jnp.concatenate([query_weight, key_weight, value_weight], axis=1)
    q_cols, out_cols, n_qkv = query_weight.shape[1], output_weight.shape[0], own_qkv.shape[1]
    output_piece = lax.dynamic_slice_in_dim(output_weight, group_at * part, part, 1).T
    attn_piece = far_swap(jnp.concatenate([own_rows(own_qkv), output_piece], axis=1))
    far_attn = gather_all(attn_piece)
    far_qkv, far_output = far_attn[:, :n_qkv], far_attn[:, n_qkv:]
    small_piece = jnp.concatenate([depthwise, conv_gain[None], depth_gain[None]], axis=0).T
    small_piece = jnp.pad(small_piece, ((0, 0), (0, 128 - small_piece.shape[1])))
    conv_piece = jnp.concatenate([pointwise_in, pointwise_out, small_piece], axis=1)
    conv_piece = after(conv_piece, attn_piece)
    for bit in bits(n_heads):
        other = swap(conv_piece, "heads", bit)
        lower = bit_of("heads", bit) == 0
        conv_piece = jnp.concatenate(
            [jnp.where(lower, conv_piece, other), jnp.where(lower, other, conv_piece)], axis=0
        )
    conv_all = gather_all(conv_piece)
    pw_in, pw_out = conv_all[:, : 2 * width], conv_all[:, 2 * width : 3 * width]
    small_all = conv_all[:, 3 * width : 3 * width + KERNEL + 2].T
    conv_weights = (pw_in, pw_out, small_all[:KERNEL], small_all[KERNEL], small_all[KERNEL + 1])

    rows = [lax.dynamic_index_in_dim(frames, my_row ^ f, 0, keepdims=False) for f in (0, 1)]
    units = [cut_parts(row) for row in rows]
    stream_zero = units[0][0].astype(jnp.float32)
    ffn1_low, ffn1_pre, ffn1_act, ffn1_partial = [], [], [], []
    ffn1_norm = None
    for f in (0, 1):
        lows, pres, acts, partials = [], [], [], []
        for unit in units[f]:
            normed_out, normed, inverse = norm_forward(unit.astype(jnp.float32), ffn1_gain)
            if ffn1_norm is None:
                ffn1_norm = (normed, inverse)
            low = normed_out.astype(bf16)
            pre = plain(low, ffn1_in)
            act = jax.nn.silu(pre).astype(bf16)
            lows.append(low)
            pres.append(pre)
            acts.append(act)
            partials.append(plain(act, ffn1_out))
        ffn1_low.append(lows)
        ffn1_pre.append(pres)
        ffn1_act.append(acts)
        ffn1_partial.append(partials)
    summed = reduce_parts(ffn1_partial[1])
    far_part = far_swap(summed.astype(bf16)).astype(jnp.float32)
    stream_one = stream_zero + 0.5 * (reduce_parts(ffn1_partial[0]) + far_part)

    n_q, n_k = local // TILE, length // TILE
    early = ffn1_act[0][0]
    my_ids = lax.dynamic_index_in_dim(after(segment_ids, early), my_row, 0, keepdims=False)
    reach = KERNEL // 2
    ids_pad = jnp.pad(my_ids, (reach, reach), constant_values=-1)
    query_ids = lax.dynamic_slice_in_dim(my_ids, seq_at * local, local, 0)
    window_ids = lax.dynamic_slice_in_dim(
        ids_pad, seq_at * local + mine * block, block + 2 * reach, 0
    )
    low_ids = query_ids.reshape(n_q, TILE)[:, 0]
    top_ids = query_ids.reshape(n_q, TILE)[:, TILE - 1]
    starts = jnp.sum((my_ids[None] < low_ids[:, None]).astype(jnp.int32), axis=1) // TILE
    ends = jnp.sum((my_ids[None] <= top_ids[:, None]).astype(jnp.int32), axis=1)
    ends = (ends + TILE - 1) // TILE
    scalars = jnp.concatenate(
        [seq_at.astype(jnp.int32)[None], jnp.stack([starts, ends], axis=1).reshape(-1)]
    )
    reversed_buckets = jnp.pad(after(bucket_of, early)[::-1], (0, 1))
    window = lax.dynamic_slice_in_dim(reversed_buckets, seq_at * local, (n_q + n_k) * TILE, 0)
    levels = lax.broadcasted_iota(jnp.int32, (position_table.shape[1], window.shape[0]), 0)
    onehot = (levels == window[None, :]).astype(jnp.float32)
    tables = jnp.concatenate([position_table, far_swap(position_table)], axis=0)
    biases = jnp.dot(tables, onehot, precision=HIGHEST) * LOG2E
    per_shard = q_cols // HEAD_DIM
    tiles = [bias_tiles(biases[:per_shard]), bias_tiles(biases[per_shard:])]

    attn_out, attn_hat, attn_inverse = norm_forward(stream_one, attn_gain)
    low = reorder(gather_parts(attn_out.astype(bf16)))
    hidden = ffn2_in.shape[1]
    ffn2_pieces = [own_rows(ffn2_in), own_rows(ffn2_out)]
    if hidden == width:
        ffn2_piece = jnp.concatenate(ffn2_pieces, axis=1)
        far_ffn2 = gather_all(far_swap(after(ffn2_piece, low)))
        far_ffn2 = (far_ffn2[:, :hidden], far_ffn2[:, hidden:])
    else:
        far_ffn2 = tuple(gather_all(far_swap(after(piece, low))) for piece in ffn2_pieces)
    ffn2_weights = [(ffn2_in, ffn2_out), far_ffn2]
    seq_bits = bits(lax.axis_size("seq"))
    pieces, queries, mixtures, log_totals = [], [], [], []
    for qkv in (own_qkv, far_qkv):
        held = [plain(low, qkv[:, q_cols:]).astype(bf16)[None]]
        for bit in reversed(seq_bits):
            held.append(swap(join(held), "seq", bit))
        pieces.append(held)
        queries.append(plain(low, qkv[:, :q_cols]).astype(bf16))
    for shard in (0, 1):
        mixture, log_total = attend(
            scalars, queries[shard], tiles[shard], query_ids[None], my_ids[:, None],
            pieces[shard], per_shard,
        )
        mixtures.append(mixture)
        log_totals.append(log_total)
    mix_parts = [cut_parts(mixture) for mixture in mixtures]
    branch = reduce_parts(
        [
            plain(own, output_weight) + against(far, far_output)
            for own, far in zip(*mix_parts)
        ]
    )
    stream_two = stream_one + branch

    stream_three, conv_state = conv_forward(stream_two, window_ids, conv_weights)
    ffn2_out_norm, ffn2_hat, ffn2_inverse = norm_forward(stream_three, ffn2_gain)
    branch, ffn2_state = ffn_forward(ffn2_out_norm.astype(bf16), ffn2_weights)
    stream_four = stream_three + 0.5 * branch
    final_out, final_hat, final_inverse = norm_forward(stream_four, final_gain)
    layer_low = final_out.astype(bf16)
    cot = lax.dynamic_index_in_dim(cotangent, my_row, 0, keepdims=False)
    cot = lax.dynamic_slice_in_dim(cot, mine * block, block, 0).astype(jnp.float32)
    grad_four, final_gain_grad = norm_backward(cot, final_hat, final_inverse, final_gain)

    normed_grad, ffn2_grads = ffn_backward(grad_four, ffn2_state, ffn2_weights)
    stream_part, ffn2_gain_grad = norm_backward(normed_grad, ffn2_hat, ffn2_inverse, ffn2_gain)
    grad_three = grad_four + stream_part
    grad_two, conv_grads, conv_small = conv_backward(
        grad_three, conv_state, window_ids, conv_weights
    )
    branch_low = reorder(gather_parts(grad_two.astype(bf16)))
    mix_grads = [
        against(branch_low, output_weight).astype(bf16),
        plain(branch_low, far_output).astype(bf16),
    ]
    q_grads, kv_grads, table_grads = [], [], []
    for shard in (0, 1):
        q_grad, kv_grad, tile_grads = attend_back(
            scalars, queries[shard], tiles[shard], query_ids[None], my_ids[:, None],
            mixtures[shard], mix_grads[shard], log_totals[shard], pieces[shard], per_shard,
        )
        for bit in seq_bits:
            half = kv_grad.shape[0] // 2
            kv_grad = (
                kv_grad[:half].astype(jnp.float32)
                + swap(kv_grad[half:], "seq", bit).astype(jnp.float32)
            ).astype(bf16)
        q_grads.append(q_grad)
        kv_grads.append(kv_grad[0])
        table_grads.append(
            lax.dot_general(
                offset_sums(tile_grads), onehot, (((1,), (1,)), ((), ())), precision=HIGHEST
            )
        )
    qkv_grads = [jnp.concatenate(pair, axis=1) for pair in zip(q_grads, kv_grads)]
    grad_parts = [cut_parts(grads) for grads in qkv_grads]
    normed_grad = reduce_parts(
        [against(own, own_qkv) + against(far, far_qkv) for own, far in zip(*grad_parts)]
    )
    attn_grads = scatter_groups(
        jnp.concatenate(
            [
                grad_of(branch_low, jnp.concatenate(mixtures, axis=1)),
                grad_of(low, jnp.concatenate(qkv_grads, axis=1)),
            ],
            axis=1,
        )
    )
    stream_part, attn_gain_grad = norm_backward(normed_grad, attn_hat, attn_inverse, attn_gain)
    grad_one = grad_two + stream_part

    own_branch = (0.5 * grad_one).astype(bf16)
    branches = [gather_parts(own_branch), gather_parts(far_swap(own_branch))]
    pre_lows, partials = [], []
    for f in (0, 1):
        pre_lows.append(
            [
                (against(branch, ffn1_out) * silu_slope(pre)).astype(bf16)
                for branch, pre in zip(branches[f], ffn1_pre[f])
            ]
        )
        partials.append([against(pre_low, ffn1_in) for pre_low in pre_lows[f]])
    every_frame = lambda lists: join(lists[0] + lists[1])
    f1_out_g = scatter_groups(grad_of(every_frame(branches), every_frame(ffn1_act)))
    f1_in_g = scatter_groups(grad_of(every_frame(ffn1_low), every_frame(pre_lows)))
    far_part = far_swap(reduce_parts(partials[1]).astype(bf16)).astype(jnp.float32)
    normed_grad = reduce_parts(partials[0]) + far_part
    stream_part, ffn1_gain_grad = norm_backward(normed_grad, *ffn1_norm, ffn1_gain)
    grad_zero = grad_one + stream_part

    ffn2_grads = after(ffn2_grads, kv_grads[0])
    n_hid = 2 * hidden
    f2_out_g, f2_in_g = fold_far(
        ffn2_grads,
        [(hidden, n_hid), (n_hid + hidden, 2 * n_hid)],
        [(0, hidden), (n_hid, n_hid + hidden)],
    )
    conv_grads = fold_heads(after(conv_grads, kv_grads[1]))
    attn_grads = after(attn_grads, branches[0][-1])
    n_out = 2 * out_cols
    o_g, qkv_g = fold_far(
        attn_grads,
        [(out_cols, n_out), (n_out + n_qkv, n_out + 2 * n_qkv)],
        [(0, out_cols), (n_out, n_out + n_qkv)],
    )

    gains = [ffn2_gain_grad, final_gain_grad] + conv_small
    all_heads = jnp.zeros((n_heads * per_shard, position_table.shape[1]), jnp.float32)
    all_heads = lax.dynamic_update_slice_in_dim(all_heads, table_grads[0], place * per_shard, 0)
    all_heads = lax.dynamic_update_slice_in_dim(
        all_heads, table_grads[1], (place ^ team) * per_shard, 0
    )
    small = jnp.concatenate([jnp.stack(gains).reshape(-1), all_heads.reshape(-1)])
    everyone = ("dp", "seq", "heads")
    small = sum_everyone(small.reshape(-1, 128)).reshape(-1)
    gains_all = small[: len(gains) * width].reshape(len(gains), width)
    table_all = small[len(gains) * width :].reshape(all_heads.shape)
    table_mine = lax.dynamic_slice_in_dim(table_all, place * per_shard, per_shard, 0)
    table_cols = table_mine.shape[1] // groups
    table_mine = lax.dynamic_slice_in_dim(table_mine, group_at * table_cols, table_cols, 1)
    group_part = lax.dynamic_slice_in_dim(gains_all[:2], group_at * part, part, 1)
    every = width // (groups * n_heads)
    conv_part = lax.dynamic_slice_in_dim(
        gains_all[2:], lax.axis_index(everyone) * every, every, 1
    )
    last = jnp.stack([ffn1_gain_grad, attn_gain_grad]).reshape(-1, 128)
    last = sum_everyone(last).reshape(2, width)
    last_part = lax.dynamic_slice_in_dim(last, group_at * part, part, 1)

    def everywhere(own):
        near, far = gather_parts(own), gather_parts(far_swap(own))
        near, far = reorder(near), reorder(far)
        first = my_row == 0
        return jnp.stack([jnp.where(first, near, far), jnp.where(first, far, near)])

    return (
        everywhere(after(layer_low, branch_low)),
        everywhere(grad_zero.astype(bf16)).astype(jnp.float32),
        last_part[0],
        f1_in_g.astype(jnp.float32),
        f1_out_g.T.astype(jnp.float32),
        last_part[1],
        qkv_g[:, :q_cols],
        qkv_g[:, q_cols : 2 * q_cols],
        qkv_g[:, 2 * q_cols :],
        o_g.T,
        table_mine,
        conv_part[0],
        conv_grads[:, : 2 * width],
        conv_part[2:],
        conv_part[1],
        conv_grads[:, 2 * width :],
        group_part[0],
        f2_in_g,
        f2_out_g.T,
        group_part[1],
    )


def solution(mesh):
    return jax.shard_map(
        on_device,
        mesh=mesh,
        in_specs=(
            P("dp", "seq", None),
            P("dp", None),
            P(),
            P(),
            P(None, "heads"),
            P("heads", None),
            P(),
            P(None, "heads"),
            P(None, "heads"),
            P(None, "heads"),
            P("heads", None),
            P("heads", None),
            P(("dp", "seq", "heads")),
            P(("dp", "seq", "heads"), None),
            P(None, ("dp", "seq", "heads")),
            P(("dp", "seq", "heads")),
            P(("dp", "seq", "heads"), None),
            P(),
            P(None, "heads"),
            P("heads", None),
            P(),
            P("dp", "seq", None),
        ),
        out_specs=(
            P("dp", "seq", None),
            P("dp", "seq", None),
            P(("dp", "seq")),
            P(("dp", "seq"), "heads"),
            P("heads", ("dp", "seq")),
            P(("dp", "seq")),
            P(("dp", "seq"), "heads"),
            P(("dp", "seq"), "heads"),
            P(("dp", "seq"), "heads"),
            P("heads", ("dp", "seq")),
            P("heads", ("dp", "seq")),
            P(("dp", "seq", "heads")),
            P(("dp", "seq", "heads"), None),
            P(None, ("dp", "seq", "heads")),
            P(("dp", "seq", "heads")),
            P(("dp", "seq", "heads"), None),
            P(("dp", "seq")),
            P(("dp", "seq"), "heads"),
            P("heads", ("dp", "seq")),
            P(("dp", "seq")),
        ),
        check_vma=False,
    )
```

```python
import math
import jax
import jax.numpy as jnp
from jax import lax
from jax.experimental import pallas as pl
from jax.experimental.pallas import tpu as pltpu
from jax.sharding import PartitionSpec as P

HEAD_DIM=128
NEGATIVE=-1e30
LOG2E=math.log2(math.e)
TILE=256

def bias_tiles_kernel(win_ref, out_ref):
    width = win_ref.shape[2]
    rows = jnp.broadcast_to(win_ref[0], (8, width))
    rows = pltpu.roll(rows, width - (TILE - 1), 1, stride=1, stride_axis=0)
    step = 8
    while step < TILE:
        rows = jnp.concatenate([rows, pltpu.roll(rows, step, 1)], axis=0)
        step *= 2
    for t in range(out_ref.shape[1]):
        out_ref[0, t] = rows[:, t * TILE : (t + 1) * TILE]

def bias_tiles(window):
    heads, width = window.shape
    tiles = width // TILE - 1
    return pl.pallas_call(
        bias_tiles_kernel,
        grid=(heads,),
        in_specs=[pl.BlockSpec((1, 1, width), lambda h: (h, 0, 0))],
        out_specs=pl.BlockSpec((1, tiles, TILE, TILE), lambda h: (h, 0, 0, 0)),
        out_shape=jax.ShapeDtypeStruct((heads, tiles, TILE, TILE), jnp.float32),
        cost_estimate=pl.CostEstimate(flops=heads*TILE*TILE, transcendentals=0, bytes_accessed=heads*TILE*TILE),
    )(window[:, None])

def offset_sums_kernel(when_ref, tiles_ref, out_ref, wide):
    tiles = tiles_ref.shape[1]
    for t in range(tiles):
        wide[:, t * TILE : (t + 1) * TILE] = tiles_ref[0, t]
    wide[:, tiles * TILE :] = jnp.zeros((TILE, TILE), jnp.float32)
    rows = wide[...]
    half = TILE // 2
    while half >= 1:
        rows = pltpu.roll(rows[:half], half, 1) + rows[half:]
        half //= 2
    out_ref[0] = rows

def offset_sums(tile_grads, when):
    heads, tiles = tile_grads.shape[:2]
    width = (tiles + 1) * TILE
    return pl.pallas_call(
        offset_sums_kernel,
        grid=(heads,),
        in_specs=[
            pl.BlockSpec(memory_space=pltpu.SMEM),
            pl.BlockSpec((1, tiles, TILE, TILE), lambda h: (h, 0, 0, 0)),
        ],
        out_specs=pl.BlockSpec((1, 1, width), lambda h: (h, 0, 0)),
        out_shape=jax.ShapeDtypeStruct((heads, 1, width), jnp.float32),
        scratch_shapes=[pltpu.VMEM((TILE, width), jnp.float32)],
        cost_estimate=pl.CostEstimate(flops=heads*TILE*TILE, transcendentals=0, bytes_accessed=heads*TILE*TILE),
    )(mark(when)[None], tile_grads)[:, 0]

def columns_of(head, per_shard):
    shard, at = head // per_shard, head % per_shard
    key = (shard * 2 * per_shard + at) * HEAD_DIM
    value = key + per_shard * HEAD_DIM
    return pl.multiple_of(key, HEAD_DIM), pl.multiple_of(value, HEAD_DIM)

def load_pieces(scal, pieces, whole, sems):
    local = pieces[0].shape[1]
    copies = []
    count = sum(p.shape[0] for p in pieces)
    nbits = count.bit_length() - 1
    rel = [0]
    n = 0
    for p in pieces:
        ids = [0] if p is pieces[0] else None
        if ids is None:
            bit = nbits - 1 - (n.bit_length() - 1)
            ids = [r ^ (1 << bit) for r in rel]
            rel = rel + ids
        for k, r in enumerate(ids):
            at = pl.multiple_of((scal[0] ^ r) * local, local)
            copies.append(pltpu.make_async_copy(p.at[k], whole.at[pl.ds(at, local)], sems.at[n]))
            n += 1
    for c in copies: c.start()
    for c in copies: c.wait()

def forward_kernel(scal, per_shard, pieces_n, *refs):
    q_ref, bias_ref, qid_ref, kid_ref = refs[:4]
    pieces = refs[4 : 4 + pieces_n]
    out_ref, lse_ref, whole, sems = refs[4 + pieces_n :]
    head = pl.program_id(0)
    @pl.when(head == 0)
    def _(): load_pieces(scal, pieces, whole, sems)
    kcol, vcol = columns_of(head, per_shard)
    scale = LOG2E * HEAD_DIM ** -0.5
    nk = whole.shape[0] // TILE
    for qb in range(q_ref.shape[0] // TILE):
        q = q_ref[qb * TILE : (qb + 1) * TILE, :]
        qid = qid_ref[:, qb * TILE : (qb + 1) * TILE]
        def body(kb, carry):
            top, total, acc = carry
            at = pl.multiple_of(kb * TILE, TILE)
            k = whole[pl.ds(at, TILE), pl.ds(kcol, HEAD_DIM)]
            v = whole[pl.ds(at, TILE), pl.ds(vcol, HEAD_DIM)]
            s = lax.dot_general(k, q, (((1,), (1,)), ((), ())), preferred_element_type=jnp.float32)
            s = s * scale + bias_ref[0, qb - kb + nk - 1]
            s = jnp.where(kid_ref[pl.ds(at, TILE), :] == qid, s, NEGATIVE)
            new_top = jnp.maximum(top, jnp.max(s, axis=0, keepdims=True))
            p = jnp.exp2(s - new_top)
            fade = jnp.exp2(top - new_top)
            total = total * fade + jnp.sum(p, axis=0, keepdims=True)
            acc = acc * fade + lax.dot_general(v, p.astype(jnp.bfloat16), (((0,), (0,)), ((), ())), preferred_element_type=jnp.float32)
            return new_top, total, acc
        top, total, acc = lax.fori_loop(scal[1 + 2 * qb], scal[2 + 2 * qb], body, (
            jnp.full((1, TILE), NEGATIVE, jnp.float32), jnp.zeros((1, TILE), jnp.float32), jnp.zeros((HEAD_DIM, TILE), jnp.float32)))
        out_ref[qb * TILE : (qb + 1) * TILE, :] = (acc / total).T.astype(jnp.bfloat16)
        lse_ref[0, :, qb * TILE : (qb + 1) * TILE] = top + jnp.log2(total)

def attend(scalars, q, tiles, qid, kid, pieces, per_shard):
    tokens, width = q.shape
    heads = width // HEAD_DIM
    length = kid.shape[0]
    count = sum(p.shape[0] for p in pieces)
    n_tiles = tiles.shape[1]
    fn = lambda scal, *refs: forward_kernel(scal, per_shard, len(pieces), *refs)
    flops = 4 * heads * tokens * length * HEAD_DIM
    return pl.pallas_call(
        fn,
        grid_spec=pltpu.PrefetchScalarGridSpec(
            num_scalar_prefetch=1, grid=(heads,),
            in_specs=[
                pl.BlockSpec((tokens, HEAD_DIM), lambda h, s: (0, h)),
                pl.BlockSpec((1, n_tiles, TILE, TILE), lambda h, s: (h, 0, 0, 0)),
                pl.BlockSpec((1, tokens), lambda h, s: (0, 0)),
                pl.BlockSpec((length, 1), lambda h, s: (0, 0)),
            ] + [pl.BlockSpec(memory_space=pl.ANY)] * len(pieces),
            out_specs=[
                pl.BlockSpec((tokens, HEAD_DIM), lambda h, s: (0, h)),
                pl.BlockSpec((1, 1, tokens), lambda h, s: (h, 0, 0)),
            ],
            scratch_shapes=[pltpu.VMEM((length, pieces[0].shape[-1]), jnp.bfloat16), pltpu.SemaphoreType.DMA((count,))],
        ),
        out_shape=[jax.ShapeDtypeStruct((tokens, width), jnp.bfloat16), jax.ShapeDtypeStruct((heads, 1, tokens), jnp.float32)],
        cost_estimate=pl.CostEstimate(flops=flops, transcendentals=heads*tokens*length, bytes_accessed=heads*n_tiles*TILE*TILE*4),
    )(scalars, q, tiles, qid, kid, *pieces)

def backward_kernel(scal, per_shard, pieces_n, *refs):
    q_ref, bias_ref, qid_ref, kid_ref, mix_ref, dmix_ref, lse_ref = refs[:7]
    pieces = refs[7 : 7 + pieces_n]
    dq_ref, dkv_ref, dtile_ref, whole, dk_acc, dv_acc, sems = refs[7 + pieces_n :]
    head = pl.program_id(0)
    @pl.when(head == 0)
    def _(): load_pieces(scal, pieces, whole, sems)
    kcol, vcol = columns_of(head, per_shard)
    scale = HEAD_DIM ** -0.5
    nk = whole.shape[0] // TILE
    dk_acc[...] = jnp.zeros_like(dk_acc)
    dv_acc[...] = jnp.zeros_like(dv_acc)
    dtile_ref[...] = jnp.zeros_like(dtile_ref)
    for qb in range(q_ref.shape[0] // TILE):
        rows = slice(qb * TILE, (qb + 1) * TILE)
        q = q_ref[rows, :]
        qid = qid_ref[:, rows]
        dmix = dmix_ref[rows, :]
        lse = lse_ref[0, :, rows]
        delta = jnp.sum((dmix.astype(jnp.float32) * mix_ref[rows, :].astype(jnp.float32)).T, axis=0, keepdims=True)
        def body(kb, dq):
            at = pl.multiple_of(kb * TILE, TILE)
            k = whole[pl.ds(at, TILE), pl.ds(kcol, HEAD_DIM)]
            v = whole[pl.ds(at, TILE), pl.ds(vcol, HEAD_DIM)]
            s = lax.dot_general(k, q, (((1,), (1,)), ((), ())), preferred_element_type=jnp.float32)
            s = s * (scale * LOG2E) + bias_ref[0, qb - kb + nk - 1]
            s = jnp.where(kid_ref[pl.ds(at, TILE), :] == qid, s, NEGATIVE)
            p = jnp.exp2(s - lse)
            dp = lax.dot_general(v, dmix, (((1,), (1,)), ((), ())), preferred_element_type=jnp.float32)
            ds = p * (dp - delta)
            dtile_ref[0, qb - kb + nk - 1] += ds
            low = ds.astype(jnp.bfloat16)
            dv_acc[pl.ds(at, TILE), :] += jnp.dot(p.astype(jnp.bfloat16), dmix, preferred_element_type=jnp.float32)
            dk_acc[pl.ds(at, TILE), :] += jnp.dot(low, q, preferred_element_type=jnp.float32)
            return dq + lax.dot_general(k, low, (((0,), (0,)), ((), ())), preferred_element_type=jnp.float32)
        dq = lax.fori_loop(scal[1 + 2 * qb], scal[2 + 2 * qb], body, jnp.zeros((HEAD_DIM, TILE), jnp.float32))
        dq_ref[rows, :] = (dq * scale).T.astype(jnp.bfloat16)
    count, local = dkv_ref.shape[:2]
    nbits = count.bit_length() - 1
    for block in range(count):
        diff = scal[0] ^ block
        slot = 0
        for bit in range(nbits):
            slot = slot | (((diff >> bit) & 1) << (nbits - 1 - bit))
        rows = slice(block * local, (block + 1) * local)
        dkv_ref[slot, :, pl.ds(kcol, HEAD_DIM)] = (dk_acc[rows, :] * scale).astype(jnp.bfloat16)
        dkv_ref[slot, :, pl.ds(vcol, HEAD_DIM)] = dv_acc[rows, :].astype(jnp.bfloat16)

def attend_back(scalars, q, tiles, qid, kid, mixture, mix_grad, lse, pieces, per_shard):
    tokens, width = q.shape
    heads = width // HEAD_DIM
    length = kid.shape[0]
    count = sum(p.shape[0] for p in pieces)
    n_tiles = tiles.shape[1]
    kvw = pieces[0].shape[-1]
    fn = lambda scal, *refs: backward_kernel(scal, per_shard, len(pieces), *refs)
    head_block = pl.BlockSpec((tokens, HEAD_DIM), lambda h, s: (0, h))
    tile_block = pl.BlockSpec((1, n_tiles, TILE, TILE), lambda h, s: (h, 0, 0, 0))
    return pl.pallas_call(
        fn,
        grid_spec=pltpu.PrefetchScalarGridSpec(
            num_scalar_prefetch=1, grid=(heads,),
            in_specs=[head_block, tile_block,
                pl.BlockSpec((1, tokens), lambda h, s: (0, 0)),
                pl.BlockSpec((length, 1), lambda h, s: (0, 0)),
                head_block, head_block,
                pl.BlockSpec((1, 1, tokens), lambda h, s: (h, 0, 0)),
            ] + [pl.BlockSpec(memory_space=pl.ANY)] * len(pieces),
            out_specs=[head_block,
                pl.BlockSpec((count, length // count, kvw), lambda h, s: (0, 0, 0)),
                tile_block],
            scratch_shapes=[pltpu.VMEM((length, kvw), jnp.bfloat16), pltpu.VMEM((length, HEAD_DIM), jnp.float32), pltpu.VMEM((length, HEAD_DIM), jnp.float32), pltpu.SemaphoreType.DMA((count,))],
        ),
        out_shape=[jax.ShapeDtypeStruct((tokens, width), jnp.bfloat16),
                   jax.ShapeDtypeStruct((count, length // count, kvw), jnp.bfloat16),
                   jax.ShapeDtypeStruct(tiles.shape, jnp.float32)],
        compiler_params=pltpu.CompilerParams(vmem_limit_bytes=50 * 1024 * 1024),
        cost_estimate=pl.CostEstimate(flops=10 * heads * tokens * length * HEAD_DIM, transcendentals=heads*tokens*length, bytes_accessed=2*heads*n_tiles*TILE*TILE*4),
    )(scalars, q, tiles, qid, kid, mixture, mix_grad, lse, *pieces)


EPSILON = 1e-05
KERNEL = 5
HIGHEST = lax.Precision.HIGHEST


def bits(count):
    return list(range(count.bit_length() - 1))


def swap(array, axis, bit):
    count = lax.axis_size(axis)
    return lax.ppermute(array, axis, [(i, i ^ (1 << bit)) for i in range(count)])


def bit_of(axis, bit):
    return (lax.axis_index(axis) >> bit) & 1


def gather_all(piece):
    return lax.all_gather(piece, ("dp", "seq"), axis=0, tiled=True)


def own_rows(array, shift=0):
    axes = ("dp", "seq")
    count = math.prod(lax.axis_size(axis) for axis in axes)
    part = array.shape[0] // count
    return lax.dynamic_slice_in_dim(array, lax.axis_index(axes) * part + shift, part, 0)


def outer(left, right):
    return lax.dot_general(
        left, right, (((0,), (0,)), ((), ())), preferred_element_type=jnp.float32
    )


def plain(left, right):
    return jnp.dot(left, right, preferred_element_type=jnp.float32)


def against(left, right):
    return lax.dot_general(
        left, right, (((1,), (1,)), ((), ())), preferred_element_type=jnp.float32
    )


def norm_forward(values, gain_vec):
    centred = values - jnp.mean(values, axis=-1, keepdims=True)
    inverse = lax.rsqrt(jnp.mean(centred * centred, axis=-1, keepdims=True) + EPSILON)
    normed = centred * inverse
    return (normed * gain_vec.astype(jnp.float32), normed, inverse)


def norm_backward(gradient, normed, inverse, gain_vec):
    scaled = gradient * gain_vec.astype(jnp.float32)
    mean_grad = jnp.mean(scaled, axis=-1, keepdims=True)
    second = jnp.mean(scaled * normed, axis=-1, keepdims=True)
    gain_grad = jnp.sum((gradient * normed).reshape(-1, gradient.shape[-1]), axis=0)
    return (inverse * (scaled - mean_grad - normed * second), gain_grad)


def silu_slope(values):
    sigmoid = jax.nn.sigmoid(values)
    return sigmoid * (1.0 + values * (1.0 - sigmoid))


def sum_everyone(array):
    for axis in ("seq", "dp", "heads"):
        for bit in bits(lax.axis_size(axis)):
            array = array + swap(array, axis, bit)
    return array


def tie(*arrays):
    return lax.optimization_barrier(arrays)


def mark(value):
    first = value[(0,) * value.ndim]
    return (first != first).astype(jnp.int32)


def later(array, value):
    return array + mark(value).astype(array.dtype)


def far_swap(array):
    return swap(array, "heads", bits(lax.axis_size("heads"))[-1])


def team_bits():
    return bits(lax.axis_size("heads"))[:-1]


def gather_parts(own):
    parts = [own]
    for bit in team_bits():
        held = parts[0] if len(parts) == 1 else jnp.concatenate(parts, axis=0)
        parts.append(swap(held, "heads", bit))
    return parts


def reduce_parts(partials):
    partials = list(partials)
    for bit in reversed(team_bits()):
        came = swap(partials.pop().astype(jnp.bfloat16), "heads", bit).astype(jnp.float32)
        at, kept = 0, []
        for item in partials:
            kept.append(item + came[at : at + item.shape[0]])
            at += item.shape[0]
        partials = kept
    return partials[0]


def spread(own):
    return gather_parts(own), gather_parts(far_swap(own))


def reorder(parts):
    team = lax.axis_size("heads") // 2
    mine = lax.axis_index("heads") % team
    whole = join(parts)
    block = whole.shape[0] // team
    if team == 2:
        first, second = parts
        lower = mine == 0
        return jnp.concatenate(
            [jnp.where(lower, first, second), jnp.where(lower, second, first)], axis=0
        )
    return jnp.concatenate(
        [lax.dynamic_slice_in_dim(whole, (at ^ mine) * block, block, 0) for at in range(team)],
        axis=0,
    )


def cut_parts(array):
    team = lax.axis_size("heads") // 2
    mine = lax.axis_index("heads") % team
    block = array.shape[0] // team
    take = lambda at: lax.dynamic_slice_in_dim(array, (at ^ mine) * block, block, 0)
    parts = [take(0)]
    for bit in team_bits():
        parts.append(join([take(at) for at in range(1 << bit, 2 << bit)]))
    return parts


def join(parts):
    return parts[0] if len(parts) == 1 else jnp.concatenate(parts, axis=0)


def scatter_groups(array):
    return lax.psum_scatter(array, ("dp", "seq"), scatter_dimension=0, tiled=True)


def grad_of(left, right):
    return outer(left, right).astype(jnp.bfloat16)


def ffn_forward(low_own, weights):
    lows = gather_parts(low_own)
    pres = [[plain(low, weight_in) for weight_in, _ in weights] for low in lows]
    acts = [[jax.nn.silu(pre).astype(jnp.bfloat16) for pre in pair] for pair in pres]
    partials = [
        sum(plain(act, weight_out) for act, (_, weight_out) in zip(pair, weights))
        for pair in acts
    ]
    return reduce_parts(partials), (lows, pres, acts)


def ffn_backward(gradient, saved, weights):
    lows, pres, acts = saved
    branches = gather_parts((0.5 * gradient).astype(jnp.bfloat16))
    pre_lows = [
        [
            (against(branch, weight_out) * silu_slope(pre)).astype(jnp.bfloat16)
            for (_, weight_out), pre in zip(weights, pair)
        ]
        for branch, pair in zip(branches, pres)
    ]
    partials = [
        sum(against(pre_low, weight_in) for pre_low, (weight_in, _) in zip(pair, weights))
        for pair in pre_lows
    ]
    normed_grad = reduce_parts(partials)
    low, branch = join(lows), join(branches)
    wide = lambda items: join([jnp.concatenate(pair, axis=1) for pair in items])
    grads = jnp.concatenate(
        [grad_of(branch, wide(acts)), grad_of(low, wide(pre_lows))], axis=1
    )
    return tie(normed_grad, grads)


def far_columns(array, ranges):
    return far_swap(jnp.concatenate([array[:, a:b] for a, b in ranges], axis=1))


def add_far(array, came, ranges):
    outs, at = [], 0
    for a, b in ranges:
        outs.append(array[:, a:b].astype(jnp.float32) + came[:, at : at + b - a].astype(jnp.float32))
        at += b - a
    return outs


def halo(array, reach):
    peers, n_heads = lax.axis_size("seq"), lax.axis_size("heads")
    team = n_heads // 2
    spot = lambda row, at: (at // team) * n_heads + row * team + at % team
    up = [
        (spot(row, at), spot(row, at + 1))
        for row in range(2)
        for at in range(peers * team - 1)
    ]
    down = [(j, i) for i, j in up]
    before = lax.ppermute(array[array.shape[0] - reach :], ("seq", "heads"), up)
    after_it = lax.ppermute(array[:reach], ("seq", "heads"), down)
    return jnp.concatenate([before, array, after_it], axis=0)


def conv_forward(stream, window_ids, weights):
    in_weight, out_weight, taps, gain_one, gain_two = weights
    tokens, width = stream.shape
    reach = KERNEL // 2
    normed_out, normed, inverse = norm_forward(stream, gain_one)
    low = normed_out.astype(jnp.bfloat16)
    doubled = plain(low, in_weight)
    gate = jax.nn.sigmoid(doubled[:, width:])
    glu_low = (doubled[:, :width] * gate).astype(jnp.bfloat16)
    padded = halo(glu_low, reach)
    centre = window_ids[reach : reach + tokens]
    taps_float = taps.astype(jnp.float32)
    depth = jnp.zeros((tokens, width), jnp.float32)
    for k in range(KERNEL):
        same = (window_ids[k : k + tokens] == centre).astype(jnp.float32)[:, None]
        depth = depth + padded[k : k + tokens].astype(jnp.float32) * taps_float[k] * same
    norm_two, hat_two, inverse_two = norm_forward(depth, gain_two)
    swish_low = jax.nn.silu(norm_two).astype(jnp.bfloat16)
    branch = plain(swish_low, out_weight)
    saved = (normed, inverse, low, doubled, gate, padded, hat_two, inverse_two, norm_two, swish_low)
    return (stream + branch, saved)


def conv_backward(gradient, saved, window_ids, weights):
    in_weight, out_weight, taps, gain_one, gain_two = weights
    normed, inverse, low, doubled, gate, padded, hat_two, inverse_two, norm_two, swish_low = saved
    tokens, width = gradient.shape
    reach = KERNEL // 2
    branch_low = gradient.astype(jnp.bfloat16)
    swish_grad = against(branch_low, out_weight)
    depth_grad, gain_two_grad = norm_backward(
        swish_grad * silu_slope(norm_two), hat_two, inverse_two, gain_two
    )
    depth_low = depth_grad.astype(jnp.bfloat16)
    beside = halo(depth_low, reach)
    centre = window_ids[reach : reach + tokens]
    taps_float = taps.astype(jnp.float32)
    depth_float = depth_low.astype(jnp.float32)
    glu_grad = jnp.zeros((tokens, width), jnp.float32)
    tap_grads = []
    for k in range(KERNEL):
        same = (window_ids[k : k + tokens] == centre).astype(jnp.float32)[:, None]
        tap_grads.append(
            jnp.sum(depth_float * padded[k : k + tokens].astype(jnp.float32) * same, axis=0)
        )
        mirror = 2 * reach - k
        back = (window_ids[mirror : mirror + tokens] == centre).astype(jnp.float32)[:, None]
        glu_grad = (
            glu_grad + beside[mirror : mirror + tokens].astype(jnp.float32) * taps_float[k] * back
        )
    gate_in = doubled[:, :width]
    doubled_low = jnp.concatenate(
        [glu_grad * gate, glu_grad * gate_in * gate * (1.0 - gate)], axis=-1
    ).astype(jnp.bfloat16)
    normed_grad = against(doubled_low, in_weight)
    grads = jnp.concatenate([grad_of(low, doubled_low), grad_of(swish_low, branch_low)], axis=1)
    part, gain_one_grad = norm_backward(normed_grad, normed, inverse, gain_one)
    small = [gain_one_grad, gain_two_grad] + tap_grads
    return (gradient + part, grads, small)


def fold_heads(both):
    for bit in reversed(bits(lax.axis_size("heads"))):
        both = both.astype(jnp.bfloat16)
        half = both.shape[0] // 2
        here = bit_of("heads", bit) * half
        kept = lax.dynamic_slice_in_dim(both, here, half, 0)
        sent = lax.dynamic_slice_in_dim(both, half - here, half, 0)
        both = kept.astype(jnp.float32) + swap(sent, "heads", bit).astype(jnp.float32)
    return both


def on_device(
    frames,
    segment_ids,
    bucket_of,
    ffn1_gain,
    ffn1_in,
    ffn1_out,
    attn_gain,
    query_weight,
    key_weight,
    value_weight,
    output_weight,
    position_table,
    conv_gain,
    pointwise_in,
    depthwise,
    depth_gain,
    pointwise_out,
    ffn2_gain,
    ffn2_in,
    ffn2_out,
    final_gain,
    cotangent,
):
    row_count, local, width = frames.shape
    length = segment_ids.shape[1]
    n_heads = lax.axis_size("heads")
    team = n_heads // 2
    place = lax.axis_index("heads")
    seq_at = lax.axis_index("seq")
    assert row_count == 2
    my_row, mine = place // team, place % team
    block = local // team
    bf16 = jnp.bfloat16
    groups = lax.axis_size("dp") * lax.axis_size("seq")
    group_at = lax.axis_index(("dp", "seq"))
    part = width // groups

    own_qkv = jnp.concatenate([query_weight, key_weight, value_weight], axis=1)
    q_cols, out_cols, n_qkv = query_weight.shape[1], output_weight.shape[0], own_qkv.shape[1]
    output_piece = lax.dynamic_slice_in_dim(output_weight, group_at * part, part, 1).T
    attn_piece = far_swap(jnp.concatenate([own_rows(own_qkv), output_piece], axis=1))
    small_piece = jnp.concatenate([depthwise, conv_gain[None], depth_gain[None]], axis=0).T
    small_piece = jnp.pad(small_piece, ((0, 0), (0, 128 - small_piece.shape[1])))
    conv_piece = jnp.concatenate([pointwise_in, pointwise_out, small_piece], axis=1)
    rows = [lax.dynamic_index_in_dim(frames, my_row ^ f, 0, keepdims=False) for f in (0, 1)]
    units = [cut_parts(row) for row in rows]
    stream_zero = units[0][0].astype(jnp.float32)
    hidden1 = ffn1_in.shape[1]
    ffn1_low, ffn1_pre, ffn1_act, ffn1_partial = [], [], [], []
    ffn1_norm = None
    for f in (0, 1):
        lows, pres, acts, partials = [], [], [], []
        for unit in units[f]:
            normed_out, normed, inverse = norm_forward(unit.astype(jnp.float32), ffn1_gain)
            if ffn1_norm is None:
                ffn1_norm = (normed, inverse)
            low = normed_out.astype(bf16)
            pre = plain(low, ffn1_in)
            act = jax.nn.silu(pre).astype(bf16)
            lows.append(low)
            pres.append(pre)
            acts.append(act)
            partials.append(plain(act, ffn1_out))
        ffn1_low.append(lows)
        ffn1_pre.append(pres)
        ffn1_act.append(acts)
        ffn1_partial.append(partials)
    attn_piece = later(attn_piece, ffn1_act[0][0])
    far_attn = gather_all(attn_piece)
    far_qkv, far_output = far_attn[:, :n_qkv], far_attn[:, n_qkv:]
    for bit in bits(n_heads):
        other = swap(conv_piece, "heads", bit)
        lower = bit_of("heads", bit) == 0
        conv_piece = jnp.concatenate(
            [jnp.where(lower, conv_piece, other), jnp.where(lower, other, conv_piece)], axis=0
        )
        if bit < len(bits(n_heads)) - 1:
            conv_piece = later(conv_piece, ffn1_act[1][-1])
    summed = reduce_parts(ffn1_partial[1])
    conv_all = gather_all(later(conv_piece, summed))
    pw_in, pw_out = conv_all[:, : 2 * width], conv_all[:, 2 * width : 3 * width]
    small_all = conv_all[:, 3 * width : 3 * width + KERNEL + 2].T
    conv_weights = (pw_in, pw_out, small_all[:KERNEL], small_all[KERNEL], small_all[KERNEL + 1])
    n_q, n_k = local // TILE, length // TILE
    my_ids = lax.dynamic_index_in_dim(segment_ids, my_row, 0, keepdims=False)
    reach = KERNEL // 2
    ids_pad = jnp.pad(my_ids, (reach, reach), constant_values=-1)
    query_ids = lax.dynamic_slice_in_dim(my_ids, seq_at * local, local, 0)
    window_ids = lax.dynamic_slice_in_dim(
        ids_pad, seq_at * local + mine * block, block + 2 * reach, 0
    )
    low_ids = query_ids.reshape(n_q, TILE)[:, 0]
    top_ids = query_ids.reshape(n_q, TILE)[:, TILE - 1]
    starts = jnp.sum((my_ids[None] < low_ids[:, None]).astype(jnp.int32), axis=1) // TILE
    ends = jnp.sum((my_ids[None] <= top_ids[:, None]).astype(jnp.int32), axis=1)
    ends = (ends + TILE - 1) // TILE
    scalars = jnp.concatenate(
        [seq_at.astype(jnp.int32)[None], jnp.stack([starts, ends], axis=1).reshape(-1)]
    )
    reversed_buckets = jnp.pad(bucket_of[::-1], (0, 1))
    window = lax.dynamic_slice_in_dim(reversed_buckets, seq_at * local, (n_q + n_k) * TILE, 0)
    levels = lax.broadcasted_iota(jnp.int32, (position_table.shape[1], window.shape[0]), 0)
    onehot = (levels == window[None, :]).astype(jnp.float32)
    tables = jnp.concatenate([position_table, far_swap(position_table)], axis=0)
    biases = jnp.dot(tables, onehot, precision=HIGHEST) * LOG2E
    per_shard = q_cols // HEAD_DIM
    tiles = [bias_tiles(biases[:per_shard]), bias_tiles(biases[per_shard:])]
    far_part = far_swap(summed.astype(bf16))
    far_part, tiles[0], tiles[1], scalars = tie(far_part, tiles[0], tiles[1], scalars)
    stream_one = stream_zero + 0.5 * (
        reduce_parts(ffn1_partial[0]) + far_part.astype(jnp.float32)
    )

    attn_out, attn_hat, attn_inverse = norm_forward(stream_one, attn_gain)
    low = reorder(gather_parts(attn_out.astype(bf16)))
    hidden = ffn2_in.shape[1]
    ffn2_pieces = [own_rows(ffn2_in, mark(low)), own_rows(ffn2_out, mark(low))]
    if hidden == width:
        ffn2_pieces = [jnp.concatenate(ffn2_pieces, axis=1)]
    ffn2_pieces = [far_swap(piece) for piece in ffn2_pieces]
    seq_bits = bits(lax.axis_size("seq"))
    both_kv = [plain(low, qkv[:, q_cols:]).astype(bf16)[None] for qkv in (own_qkv, far_qkv)]
    pieces, queries, mixtures, log_totals = [], [], [], []
    for shard in (0, 1):
        held = [both_kv[shard]]
        first = both_kv[1] if shard == 0 else mixtures[0]
        for bit in reversed(seq_bits):
            whole = join(held)
            if len(held) == len(seq_bits):
                whole = later(whole, first)
            held.append(swap(whole, "seq", bit))
        pieces.append(held)
        queries.append(plain(low, (own_qkv, far_qkv)[shard][:, :q_cols]).astype(bf16))
        mixture, log_total = attend(
            scalars, queries[shard], tiles[shard], query_ids[None], my_ids[:, None],
            pieces[shard], per_shard,
        )
        mixtures.append(mixture)
        log_totals.append(log_total)
    mixtures[1], ffn2_pieces = tie(mixtures[1], ffn2_pieces)
    far_ffn2 = [gather_all(piece) for piece in ffn2_pieces]
    if hidden == width:
        far_ffn2 = [far_ffn2[0][:, :hidden], far_ffn2[0][:, hidden:]]
    ffn2_weights = [(ffn2_in, ffn2_out), tuple(far_ffn2)]
    mix_parts = [cut_parts(mixture) for mixture in mixtures]
    branch = reduce_parts(
        [
            plain(own, output_weight) + against(far, far_output)
            for own, far in zip(*mix_parts)
        ]
    )
    stream_two = stream_one + branch

    stream_three, conv_state = conv_forward(stream_two, window_ids, conv_weights)
    ffn2_out_norm, ffn2_hat, ffn2_inverse = norm_forward(stream_three, ffn2_gain)
    branch, ffn2_state = ffn_forward(ffn2_out_norm.astype(bf16), ffn2_weights)
    stream_four = stream_three + 0.5 * branch
    final_out, final_hat, final_inverse = norm_forward(stream_four, final_gain)
    layer_low = final_out.astype(bf16)
    cot = lax.dynamic_index_in_dim(cotangent, my_row, 0, keepdims=False)
    cot = lax.dynamic_slice_in_dim(cot, mine * block, block, 0).astype(jnp.float32)
    grad_four, final_gain_grad = norm_backward(cot, final_hat, final_inverse, final_gain)

    normed_grad, ffn2_grads = ffn_backward(grad_four, ffn2_state, ffn2_weights)
    ffn2_grads = scatter_groups(ffn2_grads)
    stream_part, ffn2_gain_grad = norm_backward(normed_grad, ffn2_hat, ffn2_inverse, ffn2_gain)
    grad_three = grad_four + stream_part
    grad_two, conv_grads, conv_small = conv_backward(
        grad_three, conv_state, window_ids, conv_weights
    )
    branch_low = reorder(gather_parts(grad_two.astype(bf16)))
    branch_low, conv_grads = tie(branch_low, conv_grads)
    mix_grads = [
        against(branch_low, output_weight).astype(bf16),
        plain(branch_low, far_output).astype(bf16),
    ]
    layer_low = later(layer_low, branch_low)
    layer_near, layer_far = gather_parts(layer_low), far_swap(layer_low)
    q_grads, kv_grads, all_tile_grads = [], [], []
    turn = scalars
    for shard in (0, 1):
        q_grad, kv_grad, tile_grads = attend_back(
            turn, queries[shard], tiles[shard], query_ids[None], my_ids[:, None],
            mixtures[shard], mix_grads[shard], log_totals[shard], pieces[shard], per_shard,
        )
        if shard == 1:
            kv_grad, kv_grads[0], layer_near, layer_far = tie(
                kv_grad, kv_grads[0], layer_near, layer_far
            )
        for bit in seq_bits:
            half = kv_grad.shape[0] // 2
            kv_grad = (
                kv_grad[:half].astype(jnp.float32)
                + swap(kv_grad[half:], "seq", bit).astype(jnp.float32)
            ).astype(bf16)
            if shard == 0 and bit == 0:
                turn = scalars + mark(kv_grad)
        q_grads.append(q_grad)
        kv_grads.append(kv_grad[0])
        all_tile_grads.append(tile_grads)
    layer_far = gather_parts(layer_far)
    ffn2_grads, conv_grads, kv_grads[1] = tie(ffn2_grads, conv_grads, kv_grads[1])
    conv_grads = scatter_groups(conv_grads)
    n_hid = 2 * hidden
    ffn2_out_came = far_columns(ffn2_grads, [(hidden, n_hid)])
    qkv_grads = [jnp.concatenate(pair, axis=1) for pair in zip(q_grads, kv_grads)]
    grad_parts = [cut_parts(grads) for grads in qkv_grads]
    partials = [against(own, own_qkv) + against(far, far_qkv) for own, far in zip(*grad_parts)]
    normed_grad = reduce_parts(partials)
    low = later(low, partials[0])
    attn_grads = jnp.concatenate(
        [
            grad_of(later(branch_low, partials[0]), jnp.concatenate(mixtures, axis=1)),
            grad_of(low, jnp.concatenate(qkv_grads, axis=1)),
        ],
        axis=1,
    )
    normed_grad, attn_grads, ffn2_out_came, layer_far = tie(
        normed_grad, attn_grads, ffn2_out_came, layer_far
    )
    stream_part, attn_gain_grad = norm_backward(normed_grad, attn_hat, attn_inverse, attn_gain)
    grad_one = grad_two + stream_part

    own_branch = (0.5 * grad_one).astype(bf16)
    near, far = tie(gather_parts(own_branch), far_swap(own_branch))
    branches = [near, gather_parts(far)]
    attn_grads, conv_grads, branches[0][-1] = tie(attn_grads, conv_grads, branches[0][-1])
    attn_grads = scatter_groups(attn_grads)
    conv_grads = fold_heads(conv_grads)
    branches[1][-1], conv_grads = tie(branches[1][-1], conv_grads)
    pre_lows, partials = [], []
    for f in (0, 1):
        pre_lows.append(
            [
                (against(branch, ffn1_out) * silu_slope(pre)).astype(bf16)
                for branch, pre in zip(branches[f], ffn1_pre[f])
            ]
        )
        partials.append([against(pre_low, ffn1_in) for pre_low in pre_lows[f]])
    every_frame = lambda lists: join(lists[0] + lists[1])
    table_grads = [
        lax.dot_general(
            offset_sums(tile_grads, branches[0][-1]), onehot, (((1,), (1,)), ((), ())),
            precision=HIGHEST,
        )
        for tile_grads in all_tile_grads
    ]
    last_sent = partials[1][-1]
    ffn1_grads = jnp.concatenate(
        [
            grad_of(later(every_frame(branches), last_sent), every_frame(ffn1_act)),
            grad_of(later(every_frame(ffn1_low), last_sent), every_frame(pre_lows)),
        ],
        axis=1,
    )
    ffn1_grads, attn_grads = tie(ffn1_grads, attn_grads)
    ffn1_grads = scatter_groups(ffn1_grads).astype(jnp.float32)
    far_part = far_swap(reduce_parts(partials[1]).astype(bf16)).astype(jnp.float32)
    near_sum = reduce_parts(partials[0])
    normed_grad = near_sum + far_part
    stream_part, ffn1_gain_grad = norm_backward(normed_grad, *ffn1_norm, ffn1_gain)
    grad_zero = grad_one + stream_part

    low = grad_zero.astype(bf16)
    near, far = tie(gather_parts(low), far_swap(low))
    spread_grad = near, gather_parts(far)

    (f2_out_g,) = add_far(ffn2_grads, ffn2_out_came, [(0, hidden)])
    ffn2_in_came = far_columns(later(ffn2_grads, spread_grad[1][0]), [(n_hid + hidden, 2 * n_hid)])
    (f2_in_g,) = add_far(ffn2_grads, ffn2_in_came, [(n_hid, n_hid + hidden)])
    n_out = 2 * out_cols
    attn_came = far_columns(later(attn_grads, spread_grad[1][0]), [(out_cols, n_out), (n_out + n_qkv, n_out + 2 * n_qkv)])
    o_g, qkv_g = add_far(attn_grads, attn_came, [(0, out_cols), (n_out, n_out + n_qkv)])

    all_heads = jnp.zeros((n_heads * per_shard, position_table.shape[1]), jnp.float32)
    all_heads = lax.dynamic_update_slice_in_dim(all_heads, table_grads[0], place * per_shard, 0)
    all_heads = lax.dynamic_update_slice_in_dim(
        all_heads, table_grads[1], (place ^ team) * per_shard, 0
    )
    gains = [ffn1_gain_grad, attn_gain_grad, ffn2_gain_grad, final_gain_grad] + conv_small
    small = jnp.concatenate([jnp.stack(gains).reshape(-1), all_heads.reshape(-1)])
    small = later(small.reshape(-1, 128), spread_grad[1][0])
    small = sum_everyone(small).reshape(-1)
    gains_all = small[: len(gains) * width].reshape(len(gains), width)
    table_all = small[len(gains) * width :].reshape(all_heads.shape)
    table_mine = lax.dynamic_slice_in_dim(table_all, place * per_shard, per_shard, 0)
    table_cols = table_mine.shape[1] // groups
    table_mine = lax.dynamic_slice_in_dim(table_mine, group_at * table_cols, table_cols, 1)
    group_part = lax.dynamic_slice_in_dim(gains_all[:4], group_at * part, part, 1)
    every = width // (groups * n_heads)
    conv_part = lax.dynamic_slice_in_dim(
        gains_all[4:], lax.axis_index(("dp", "seq", "heads")) * every, every, 1
    )

    def everywhere(parts):
        near, far = reorder(parts[0]), reorder(parts[1])
        first = my_row == 0
        return jnp.stack([jnp.where(first, near, far), jnp.where(first, far, near)])

    return (
        everywhere((layer_near, layer_far)),
        everywhere(spread_grad).astype(jnp.float32),
        group_part[0],
        ffn1_grads[:, hidden1:],
        ffn1_grads[:, :hidden1].T,
        group_part[1],
        qkv_g[:, :q_cols],
        qkv_g[:, q_cols : 2 * q_cols],
        qkv_g[:, 2 * q_cols :],
        o_g.T,
        table_mine,
        conv_part[0],
        conv_grads[:, : 2 * width],
        conv_part[2:],
        conv_part[1],
        conv_grads[:, 2 * width :],
        group_part[2],
        f2_in_g,
        f2_out_g.T,
        group_part[3],
    )


def solution(mesh):
    return jax.shard_map(
        on_device,
        mesh=mesh,
        in_specs=(
            P("dp", "seq", None),
            P("dp", None),
            P(),
            P(),
            P(None, "heads"),
            P("heads", None),
            P(),
            P(None, "heads"),
            P(None, "heads"),
            P(None, "heads"),
            P("heads", None),
            P("heads", None),
            P(("dp", "seq", "heads")),
            P(("dp", "seq", "heads"), None),
            P(None, ("dp", "seq", "heads")),
            P(("dp", "seq", "heads")),
            P(("dp", "seq", "heads"), None),
            P(),
            P(None, "heads"),
            P("heads", None),
            P(),
            P("dp", "seq", None),
        ),
        out_specs=(
            P("dp", "seq", None),
            P("dp", "seq", None),
            P(("dp", "seq")),
            P(("dp", "seq"), "heads"),
            P("heads", ("dp", "seq")),
            P(("dp", "seq")),
            P(("dp", "seq"), "heads"),
            P(("dp", "seq"), "heads"),
            P(("dp", "seq"), "heads"),
            P("heads", ("dp", "seq")),
            P("heads", ("dp", "seq")),
            P(("dp", "seq", "heads")),
            P(("dp", "seq", "heads"), None),
            P(None, ("dp", "seq", "heads")),
            P(("dp", "seq", "heads")),
            P(("dp", "seq", "heads"), None),
            P(("dp", "seq")),
            P(("dp", "seq"), "heads"),
            P("heads", ("dp", "seq")),
            P(("dp", "seq")),
        ),
        check_vma=False,
    )
```

```python
import math
import jax
import jax.numpy as jnp
from jax import lax
from jax.experimental import pallas as pl
from jax.experimental.pallas import tpu as pltpu
from jax.sharding import PartitionSpec as P

HEAD_DIM=128
NEGATIVE=-1e30
LOG2E=math.log2(math.e)
TILE=256

def bias_tiles_kernel(win_ref, out_ref):
    width = win_ref.shape[2]
    rows = jnp.broadcast_to(win_ref[0], (8, width))
    rows = pltpu.roll(rows, width - (TILE - 1), 1, stride=1, stride_axis=0)
    step = 8
    while step < TILE:
        rows = jnp.concatenate([rows, pltpu.roll(rows, step, 1)], axis=0)
        step *= 2
    for t in range(out_ref.shape[1]):
        out_ref[0, t] = rows[:, t * TILE : (t + 1) * TILE]

def bias_tiles(window):
    heads, width = window.shape
    tiles = width // TILE - 1
    return pl.pallas_call(
        bias_tiles_kernel,
        grid=(heads,),
        in_specs=[pl.BlockSpec((1, 1, width), lambda h: (h, 0, 0))],
        out_specs=pl.BlockSpec((1, tiles, TILE, TILE), lambda h: (h, 0, 0, 0)),
        out_shape=jax.ShapeDtypeStruct((heads, tiles, TILE, TILE), jnp.float32),
        cost_estimate=pl.CostEstimate(flops=TILE, transcendentals=0, bytes_accessed=TILE),
    )(window[:, None])

def offset_sums_kernel(when_ref, tiles_ref, out_ref, wide):
    tiles = tiles_ref.shape[1]
    for t in range(tiles):
        wide[:, t * TILE : (t + 1) * TILE] = tiles_ref[0, t]
    wide[:, tiles * TILE :] = jnp.zeros((TILE, TILE), jnp.float32)
    rows = wide[...]
    half = TILE // 2
    while half >= 1:
        rows = pltpu.roll(rows[:half], half, 1) + rows[half:]
        half //= 2
    out_ref[0] = rows

def offset_sums(tile_grads, when):
    heads, tiles = tile_grads.shape[:2]
    width = (tiles + 1) * TILE
    return pl.pallas_call(
        offset_sums_kernel,
        grid=(heads,),
        in_specs=[
            pl.BlockSpec(memory_space=pltpu.SMEM),
            pl.BlockSpec((1, tiles, TILE, TILE), lambda h: (h, 0, 0, 0)),
        ],
        out_specs=pl.BlockSpec((1, 1, width), lambda h: (h, 0, 0)),
        out_shape=jax.ShapeDtypeStruct((heads, 1, width), jnp.float32),
        scratch_shapes=[pltpu.VMEM((TILE, width), jnp.float32)],
        cost_estimate=pl.CostEstimate(flops=TILE, transcendentals=0, bytes_accessed=TILE),
    )(mark(when)[None], tile_grads)[:, 0]

def columns_of(head, per_shard):
    shard, at = head // per_shard, head % per_shard
    key = (shard * 2 * per_shard + at) * HEAD_DIM
    value = key + per_shard * HEAD_DIM
    return pl.multiple_of(key, HEAD_DIM), pl.multiple_of(value, HEAD_DIM)

def load_pieces(scal, pieces, whole, sems):
    local = pieces[0].shape[1]
    copies = []
    count = sum(p.shape[0] for p in pieces)
    nbits = count.bit_length() - 1
    rel = [0]
    n = 0
    for p in pieces:
        ids = [0] if p is pieces[0] else None
        if ids is None:
            bit = nbits - 1 - (n.bit_length() - 1)
            ids = [r ^ (1 << bit) for r in rel]
            rel = rel + ids
        for k, r in enumerate(ids):
            at = pl.multiple_of((scal[0] ^ r) * local, local)
            copies.append(pltpu.make_async_copy(p.at[k], whole.at[pl.ds(at, local)], sems.at[n]))
            n += 1
    for c in copies: c.start()
    for c in copies: c.wait()

def forward_kernel(scal, per_shard, pieces_n, *refs):
    q_ref, bias_ref, qid_ref, kid_ref = refs[:4]
    pieces = refs[4 : 4 + pieces_n]
    out_ref, lse_ref, whole, sems = refs[4 + pieces_n :]
    head = pl.program_id(0)
    @pl.when(head == 0)
    def _(): load_pieces(scal, pieces, whole, sems)
    kcol, vcol = columns_of(head, per_shard)
    scale = LOG2E * HEAD_DIM ** -0.5
    nk = whole.shape[0] // TILE
    for qb in range(q_ref.shape[0] // TILE):
        q = q_ref[qb * TILE : (qb + 1) * TILE, :]
        qid = qid_ref[:, qb * TILE : (qb + 1) * TILE]
        def body(kb, carry):
            top, total, acc = carry
            at = pl.multiple_of(kb * TILE, TILE)
            k = whole[pl.ds(at, TILE), pl.ds(kcol, HEAD_DIM)]
            v = whole[pl.ds(at, TILE), pl.ds(vcol, HEAD_DIM)]
            s = lax.dot_general(k, q, (((1,), (1,)), ((), ())), preferred_element_type=jnp.float32)
            s = s * scale + bias_ref[0, qb - kb + nk - 1]
            s = jnp.where(kid_ref[pl.ds(at, TILE), :] == qid, s, NEGATIVE)
            new_top = jnp.maximum(top, jnp.max(s, axis=0, keepdims=True))
            p = jnp.exp2(s - new_top)
            fade = jnp.exp2(top - new_top)
            total = total * fade + jnp.sum(p, axis=0, keepdims=True)
            acc = acc * fade + lax.dot_general(v, p.astype(jnp.bfloat16), (((0,), (0,)), ((), ())), preferred_element_type=jnp.float32)
            return new_top, total, acc
        top, total, acc = lax.fori_loop(scal[1 + 2 * qb], scal[2 + 2 * qb], body, (
            jnp.full((1, TILE), NEGATIVE, jnp.float32), jnp.zeros((1, TILE), jnp.float32), jnp.zeros((HEAD_DIM, TILE), jnp.float32)))
        out_ref[qb * TILE : (qb + 1) * TILE, :] = (acc / total).T.astype(jnp.bfloat16)
        lse_ref[0, :, qb * TILE : (qb + 1) * TILE] = top + jnp.log2(total)

def attend(scalars, q, tiles, qid, kid, pieces, per_shard):
    tokens, width = q.shape
    heads = width // HEAD_DIM
    length = kid.shape[0]
    count = sum(p.shape[0] for p in pieces)
    n_tiles = tiles.shape[1]
    fn = lambda scal, *refs: forward_kernel(scal, per_shard, len(pieces), *refs)
    flops = 4 * heads * tokens * length * HEAD_DIM
    return pl.pallas_call(
        fn,
        grid_spec=pltpu.PrefetchScalarGridSpec(
            num_scalar_prefetch=1, grid=(heads,),
            in_specs=[
                pl.BlockSpec((tokens, HEAD_DIM), lambda h, s: (0, h)),
                pl.BlockSpec((1, n_tiles, TILE, TILE), lambda h, s: (h, 0, 0, 0)),
                pl.BlockSpec((1, tokens), lambda h, s: (0, 0)),
                pl.BlockSpec((length, 1), lambda h, s: (0, 0)),
            ] + [pl.BlockSpec(memory_space=pl.ANY)] * len(pieces),
            out_specs=[
                pl.BlockSpec((tokens, HEAD_DIM), lambda h, s: (0, h)),
                pl.BlockSpec((1, 1, tokens), lambda h, s: (h, 0, 0)),
            ],
            scratch_shapes=[pltpu.VMEM((length, pieces[0].shape[-1]), jnp.bfloat16), pltpu.SemaphoreType.DMA((count,))],
        ),
        out_shape=[jax.ShapeDtypeStruct((tokens, width), jnp.bfloat16), jax.ShapeDtypeStruct((heads, 1, tokens), jnp.float32)],
        cost_estimate=pl.CostEstimate(flops=flops, transcendentals=heads*tokens*length, bytes_accessed=heads*n_tiles*TILE*TILE*4),
    )(scalars, q, tiles, qid, kid, *pieces)

def backward_kernel(scal, per_shard, pieces_n, *refs):
    q_ref, bias_ref, qid_ref, kid_ref, mix_ref, dmix_ref, lse_ref = refs[:7]
    pieces = refs[7 : 7 + pieces_n]
    dq_ref, dkv_ref, dtile_ref, whole, dk_acc, dv_acc, sems = refs[7 + pieces_n :]
    head = pl.program_id(0)
    @pl.when(head == 0)
    def _(): load_pieces(scal, pieces, whole, sems)
    kcol, vcol = columns_of(head, per_shard)
    scale = HEAD_DIM ** -0.5
    nk = whole.shape[0] // TILE
    dk_acc[...] = jnp.zeros_like(dk_acc)
    dv_acc[...] = jnp.zeros_like(dv_acc)
    dtile_ref[...] = jnp.zeros_like(dtile_ref)
    for qb in range(q_ref.shape[0] // TILE):
        rows = slice(qb * TILE, (qb + 1) * TILE)
        q = q_ref[rows, :]
        qid = qid_ref[:, rows]
        dmix = dmix_ref[rows, :]
        lse = lse_ref[0, :, rows]
        delta = jnp.sum((dmix.astype(jnp.float32) * mix_ref[rows, :].astype(jnp.float32)).T, axis=0, keepdims=True)
        def body(kb, dq):
            at = pl.multiple_of(kb * TILE, TILE)
            k = whole[pl.ds(at, TILE), pl.ds(kcol, HEAD_DIM)]
            v = whole[pl.ds(at, TILE), pl.ds(vcol, HEAD_DIM)]
            s = lax.dot_general(k, q, (((1,), (1,)), ((), ())), preferred_element_type=jnp.float32)
            s = s * (scale * LOG2E) + bias_ref[0, qb - kb + nk - 1]
            s = jnp.where(kid_ref[pl.ds(at, TILE), :] == qid, s, NEGATIVE)
            p = jnp.exp2(s - lse)
            dp = lax.dot_general(v, dmix, (((1,), (1,)), ((), ())), preferred_element_type=jnp.float32)
            ds = p * (dp - delta)
            dtile_ref[0, qb - kb + nk - 1] += ds
            low = ds.astype(jnp.bfloat16)
            dv_acc[pl.ds(at, TILE), :] += jnp.dot(p.astype(jnp.bfloat16), dmix, preferred_element_type=jnp.float32)
            dk_acc[pl.ds(at, TILE), :] += jnp.dot(low, q, preferred_element_type=jnp.float32)
            return dq + lax.dot_general(k, low, (((0,), (0,)), ((), ())), preferred_element_type=jnp.float32)
        dq = lax.fori_loop(scal[1 + 2 * qb], scal[2 + 2 * qb], body, jnp.zeros((HEAD_DIM, TILE), jnp.float32))
        dq_ref[rows, :] = (dq * scale).T.astype(jnp.bfloat16)
    count, local = dkv_ref.shape[:2]
    nbits = count.bit_length() - 1
    for block in range(count):
        diff = scal[0] ^ block
        slot = 0
        for bit in range(nbits):
            slot = slot | (((diff >> bit) & 1) << (nbits - 1 - bit))
        rows = slice(block * local, (block + 1) * local)
        dkv_ref[slot, :, pl.ds(kcol, HEAD_DIM)] = (dk_acc[rows, :] * scale).astype(jnp.bfloat16)
        dkv_ref[slot, :, pl.ds(vcol, HEAD_DIM)] = dv_acc[rows, :].astype(jnp.bfloat16)

def attend_back(scalars, q, tiles, qid, kid, mixture, mix_grad, lse, pieces, per_shard):
    tokens, width = q.shape
    heads = width // HEAD_DIM
    length = kid.shape[0]
    count = sum(p.shape[0] for p in pieces)
    n_tiles = tiles.shape[1]
    kvw = pieces[0].shape[-1]
    fn = lambda scal, *refs: backward_kernel(scal, per_shard, len(pieces), *refs)
    head_block = pl.BlockSpec((tokens, HEAD_DIM), lambda h, s: (0, h))
    tile_block = pl.BlockSpec((1, n_tiles, TILE, TILE), lambda h, s: (h, 0, 0, 0))
    return pl.pallas_call(
        fn,
        grid_spec=pltpu.PrefetchScalarGridSpec(
            num_scalar_prefetch=1, grid=(heads,),
            in_specs=[head_block, tile_block,
                pl.BlockSpec((1, tokens), lambda h, s: (0, 0)),
                pl.BlockSpec((length, 1), lambda h, s: (0, 0)),
                head_block, head_block,
                pl.BlockSpec((1, 1, tokens), lambda h, s: (h, 0, 0)),
            ] + [pl.BlockSpec(memory_space=pl.ANY)] * len(pieces),
            out_specs=[head_block,
                pl.BlockSpec((count, length // count, kvw), lambda h, s: (0, 0, 0)),
                tile_block],
            scratch_shapes=[pltpu.VMEM((length, kvw), jnp.bfloat16), pltpu.VMEM((length, HEAD_DIM), jnp.float32), pltpu.VMEM((length, HEAD_DIM), jnp.float32), pltpu.SemaphoreType.DMA((count,))],
        ),
        out_shape=[jax.ShapeDtypeStruct((tokens, width), jnp.bfloat16),
                   jax.ShapeDtypeStruct((count, length // count, kvw), jnp.bfloat16),
                   jax.ShapeDtypeStruct(tiles.shape, jnp.float32)],
        compiler_params=pltpu.CompilerParams(vmem_limit_bytes=50 * 1024 * 1024),
        cost_estimate=pl.CostEstimate(flops=10 * heads * tokens * length * HEAD_DIM, transcendentals=heads*tokens*length, bytes_accessed=2*heads*n_tiles*TILE*TILE*4),
    )(scalars, q, tiles, qid, kid, mixture, mix_grad, lse, *pieces)


EPSILON = 1e-05
KERNEL = 5
HIGHEST = lax.Precision.HIGHEST


def bits(count):
    return list(range(count.bit_length() - 1))


def swap(array, axis, bit):
    count = lax.axis_size(axis)
    return lax.ppermute(array, axis, [(i, i ^ (1 << bit)) for i in range(count)])


def bit_of(axis, bit):
    return (lax.axis_index(axis) >> bit) & 1


def gather_all(piece):
    return lax.all_gather(piece, ("dp", "seq"), axis=0, tiled=True)


def own_rows(array, shift=0):
    axes = ("dp", "seq")
    count = math.prod(lax.axis_size(axis) for axis in axes)
    part = array.shape[0] // count
    return lax.dynamic_slice_in_dim(array, lax.axis_index(axes) * part + shift, part, 0)


def outer(left, right):
    return lax.dot_general(
        left, right, (((0,), (0,)), ((), ())), preferred_element_type=jnp.float32
    )


def plain(left, right):
    return jnp.dot(left, right, preferred_element_type=jnp.float32)


def against(left, right):
    return lax.dot_general(
        left, right, (((1,), (1,)), ((), ())), preferred_element_type=jnp.float32
    )


def norm_forward(values, gain_vec):
    centred = values - jnp.mean(values, axis=-1, keepdims=True)
    inverse = lax.rsqrt(jnp.mean(centred * centred, axis=-1, keepdims=True) + EPSILON)
    normed = centred * inverse
    return (normed * gain_vec.astype(jnp.float32), normed, inverse)


def norm_backward(gradient, normed, inverse, gain_vec):
    scaled = gradient * gain_vec.astype(jnp.float32)
    mean_grad = jnp.mean(scaled, axis=-1, keepdims=True)
    second = jnp.mean(scaled * normed, axis=-1, keepdims=True)
    gain_grad = jnp.sum((gradient * normed).reshape(-1, gradient.shape[-1]), axis=0)
    return (inverse * (scaled - mean_grad - normed * second), gain_grad)


def silu_slope(values):
    sigmoid = jax.nn.sigmoid(values)
    return sigmoid * (1.0 + values * (1.0 - sigmoid))


def sum_everyone(array):
    for axis in ("heads", "dp", "seq"):
        for bit in bits(lax.axis_size(axis)):
            array = array + swap(array, axis, bit)
    return array


def tie(*arrays):
    return lax.optimization_barrier(arrays)


def mark(value):
    first = value[(0,) * value.ndim]
    return (first != first).astype(jnp.int32)


def later(array, value):
    return array + mark(value).astype(array.dtype)


def far_swap(array):
    return swap(array, "heads", bits(lax.axis_size("heads"))[-1])


def team_bits():
    return bits(lax.axis_size("heads"))[:-1]


def gather_parts(own):
    parts = [own]
    for bit in team_bits():
        held = parts[0] if len(parts) == 1 else jnp.concatenate(parts, axis=0)
        parts.append(swap(held, "heads", bit))
    return parts


def reduce_parts(partials):
    partials = list(partials)
    for bit in reversed(team_bits()):
        came = swap(partials.pop().astype(jnp.bfloat16), "heads", bit).astype(jnp.float32)
        at, kept = 0, []
        for item in partials:
            kept.append(item + came[at : at + item.shape[0]])
            at += item.shape[0]
        partials = kept
    return partials[0]


def spread(own):
    return gather_parts(own), gather_parts(far_swap(own))


def reorder(parts):
    team = lax.axis_size("heads") // 2
    mine = lax.axis_index("heads") % team
    whole = join(parts)
    block = whole.shape[0] // team
    if team == 2:
        first, second = parts
        lower = mine == 0
        return jnp.concatenate(
            [jnp.where(lower, first, second), jnp.where(lower, second, first)], axis=0
        )
    return jnp.concatenate(
        [lax.dynamic_slice_in_dim(whole, (at ^ mine) * block, block, 0) for at in range(team)],
        axis=0,
    )


def cut_parts(array):
    team = lax.axis_size("heads") // 2
    mine = lax.axis_index("heads") % team
    block = array.shape[0] // team
    take = lambda at: lax.dynamic_slice_in_dim(array, (at ^ mine) * block, block, 0)
    parts = [take(0)]
    for bit in team_bits():
        parts.append(join([take(at) for at in range(1 << bit, 2 << bit)]))
    return parts


def join(parts):
    return parts[0] if len(parts) == 1 else jnp.concatenate(parts, axis=0)


def scatter_groups(array):
    return lax.psum_scatter(array, ("dp", "seq"), scatter_dimension=0, tiled=True)


def grad_of(left, right):
    return outer(left, right).astype(jnp.bfloat16)


def ffn_forward(low_own, weights):
    lows = gather_parts(low_own)
    pres = [[plain(low, weight_in) for weight_in, _ in weights] for low in lows]
    acts = [[jax.nn.silu(pre).astype(jnp.bfloat16) for pre in pair] for pair in pres]
    partials = [
        sum(plain(act, weight_out) for act, (_, weight_out) in zip(pair, weights))
        for pair in acts
    ]
    return reduce_parts(partials), (lows, pres, acts)


def ffn_backward(gradient, saved, weights):
    lows, pres, acts = saved
    branches = gather_parts((0.5 * gradient).astype(jnp.bfloat16))
    pre_lows = [
        [
            (against(branch, weight_out) * silu_slope(pre)).astype(jnp.bfloat16)
            for (_, weight_out), pre in zip(weights, pair)
        ]
        for branch, pair in zip(branches, pres)
    ]
    partials = [
        sum(against(pre_low, weight_in) for pre_low, (weight_in, _) in zip(pair, weights))
        for pair in pre_lows
    ]
    normed_grad = reduce_parts(partials)
    low, branch = join(lows), join(branches)
    wide = lambda items: join([jnp.concatenate(pair, axis=1) for pair in items])
    grads = jnp.concatenate(
        [grad_of(branch, wide(acts)), grad_of(low, wide(pre_lows))], axis=1
    )
    return tie(normed_grad, grads)


def far_columns(array, ranges):
    return far_swap(jnp.concatenate([array[:, a:b] for a, b in ranges], axis=1))


def add_far(array, came, ranges):
    outs, at = [], 0
    for a, b in ranges:
        outs.append(array[:, a:b].astype(jnp.float32) + came[:, at : at + b - a].astype(jnp.float32))
        at += b - a
    return outs


def halo(array, reach):
    peers, n_heads = lax.axis_size("seq"), lax.axis_size("heads")
    team = n_heads // 2
    spot = lambda row, at: (at // team) * n_heads + row * team + at % team
    up = [
        (spot(row, at), spot(row, at + 1))
        for row in range(2)
        for at in range(peers * team - 1)
    ]
    down = [(j, i) for i, j in up]
    before = lax.ppermute(array[array.shape[0] - reach :], ("seq", "heads"), up)
    after_it = lax.ppermute(array[:reach], ("seq", "heads"), down)
    return jnp.concatenate([before, array, after_it], axis=0)


def conv_forward(stream, window_ids, weights):
    in_weight, out_weight, taps, gain_one, gain_two = weights
    tokens, width = stream.shape
    reach = KERNEL // 2
    normed_out, normed, inverse = norm_forward(stream, gain_one)
    low = normed_out.astype(jnp.bfloat16)
    doubled = plain(low, in_weight)
    gate = jax.nn.sigmoid(doubled[:, width:])
    glu_low = (doubled[:, :width] * gate).astype(jnp.bfloat16)
    padded = halo(glu_low, reach)
    centre = window_ids[reach : reach + tokens]
    taps_float = taps.astype(jnp.float32)
    depth = jnp.zeros((tokens, width), jnp.float32)
    for k in range(KERNEL):
        same = (window_ids[k : k + tokens] == centre).astype(jnp.float32)[:, None]
        depth = depth + padded[k : k + tokens].astype(jnp.float32) * taps_float[k] * same
    norm_two, hat_two, inverse_two = norm_forward(depth, gain_two)
    swish_low = jax.nn.silu(norm_two).astype(jnp.bfloat16)
    branch = plain(swish_low, out_weight)
    saved = (normed, inverse, low, doubled, gate, padded, hat_two, inverse_two, norm_two, swish_low)
    return (stream + branch, saved)


def conv_backward(gradient, saved, window_ids, weights):
    in_weight, out_weight, taps, gain_one, gain_two = weights
    normed, inverse, low, doubled, gate, padded, hat_two, inverse_two, norm_two, swish_low = saved
    tokens, width = gradient.shape
    reach = KERNEL // 2
    branch_low = gradient.astype(jnp.bfloat16)
    swish_grad = against(branch_low, out_weight)
    depth_grad, gain_two_grad = norm_backward(
        swish_grad * silu_slope(norm_two), hat_two, inverse_two, gain_two
    )
    depth_low = depth_grad.astype(jnp.bfloat16)
    beside = halo(depth_low, reach)
    centre = window_ids[reach : reach + tokens]
    taps_float = taps.astype(jnp.float32)
    depth_float = depth_low.astype(jnp.float32)
    glu_grad = jnp.zeros((tokens, width), jnp.float32)
    tap_grads = []
    for k in range(KERNEL):
        same = (window_ids[k : k + tokens] == centre).astype(jnp.float32)[:, None]
        tap_grads.append(
            jnp.sum(depth_float * padded[k : k + tokens].astype(jnp.float32) * same, axis=0)
        )
        mirror = 2 * reach - k
        back = (window_ids[mirror : mirror + tokens] == centre).astype(jnp.float32)[:, None]
        glu_grad = (
            glu_grad + beside[mirror : mirror + tokens].astype(jnp.float32) * taps_float[k] * back
        )
    gate_in = doubled[:, :width]
    doubled_low = jnp.concatenate(
        [glu_grad * gate, glu_grad * gate_in * gate * (1.0 - gate)], axis=-1
    ).astype(jnp.bfloat16)
    normed_grad = against(doubled_low, in_weight)
    grads = jnp.concatenate([grad_of(low, doubled_low), grad_of(swish_low, branch_low)], axis=1)
    part, gain_one_grad = norm_backward(normed_grad, normed, inverse, gain_one)
    small = [gain_one_grad, gain_two_grad] + tap_grads
    return (gradient + part, grads, small)


def fold_step(both, bit):
    here = bit_of("heads", bit)
    kept = lax.dynamic_index_in_dim(both, here, both.ndim - 3, keepdims=False)
    sent = lax.dynamic_index_in_dim(both, 1 - here, both.ndim - 3, keepdims=False)
    came = swap(sent.astype(jnp.bfloat16), "heads", bit)
    return kept.astype(jnp.float32) + came.astype(jnp.float32)


def on_device(
    frames,
    segment_ids,
    bucket_of,
    ffn1_gain,
    ffn1_in,
    ffn1_out,
    attn_gain,
    query_weight,
    key_weight,
    value_weight,
    output_weight,
    position_table,
    conv_gain,
    pointwise_in,
    depthwise,
    depth_gain,
    pointwise_out,
    ffn2_gain,
    ffn2_in,
    ffn2_out,
    final_gain,
    cotangent,
):
    row_count, local, width = frames.shape
    length = segment_ids.shape[1]
    n_heads = lax.axis_size("heads")
    team = n_heads // 2
    place = lax.axis_index("heads")
    seq_at = lax.axis_index("seq")
    assert row_count == 2
    my_row, mine = place // team, place % team
    block = local // team
    bf16 = jnp.bfloat16
    groups = lax.axis_size("dp") * lax.axis_size("seq")
    group_at = lax.axis_index(("dp", "seq"))
    part = width // groups

    own_qkv = jnp.concatenate([query_weight, key_weight, value_weight], axis=1)
    q_cols, out_cols, n_qkv = query_weight.shape[1], output_weight.shape[0], own_qkv.shape[1]
    output_piece = lax.dynamic_slice_in_dim(output_weight, group_at * part, part, 1).T
    attn_piece = [own_rows(w) for w in (query_weight, key_weight, value_weight)]
    attn_piece = far_swap(jnp.concatenate(attn_piece + [output_piece], axis=1))
    small_piece = jnp.concatenate([depthwise, conv_gain[None], depth_gain[None]], axis=0).T
    small_piece = jnp.pad(small_piece, ((0, 0), (0, 128 - small_piece.shape[1])))
    conv_piece = jnp.concatenate([pointwise_in, pointwise_out, small_piece], axis=1)
    rows = [lax.dynamic_index_in_dim(frames, my_row ^ f, 0, keepdims=False) for f in (0, 1)]
    units = [cut_parts(row) for row in rows]
    stream_zero = units[0][0].astype(jnp.float32)
    hidden1 = ffn1_in.shape[1]
    ffn1_low, ffn1_pre, ffn1_act, ffn1_partial = [], [], [], []
    ffn1_norm = None
    for f in (0, 1):
        lows, pres, acts, partials = [], [], [], []
        for unit in units[f]:
            normed_out, normed, inverse = norm_forward(unit.astype(jnp.float32), ffn1_gain)
            if ffn1_norm is None:
                ffn1_norm = (normed, inverse)
            low = normed_out.astype(bf16)
            pre = plain(low, ffn1_in)
            act = jax.nn.silu(pre).astype(bf16)
            lows.append(low)
            pres.append(pre)
            acts.append(act)
            partials.append(plain(act, ffn1_out))
        ffn1_low.append(lows)
        ffn1_pre.append(pres)
        ffn1_act.append(acts)
        ffn1_partial.append(partials)
    attn_piece = later(attn_piece, ffn1_partial[1][-1])
    far_attn = gather_all(attn_piece)
    far_qkv, far_output = far_attn[:, :n_qkv], far_attn[:, n_qkv:]
    for bit in bits(n_heads):
        other = swap(conv_piece, "heads", bit)
        lower = bit_of("heads", bit) == 0
        conv_piece = jnp.concatenate(
            [jnp.where(lower, conv_piece, other), jnp.where(lower, other, conv_piece)], axis=0
        )
        if bit < len(bits(n_heads)) - 1:
            conv_piece = later(conv_piece, ffn1_partial[1][-1])
    summed = reduce_parts(ffn1_partial[1])
    conv_all = gather_all(later(conv_piece, ffn1_partial[1][0]))
    pw_in, pw_out = conv_all[:, : 2 * width], conv_all[:, 2 * width : 3 * width]
    small_all = conv_all[:, 3 * width : 3 * width + KERNEL + 2].T
    conv_weights = (pw_in, pw_out, small_all[:KERNEL], small_all[KERNEL], small_all[KERNEL + 1])
    n_q, n_k = local // TILE, length // TILE
    my_ids = lax.dynamic_index_in_dim(segment_ids, my_row, 0, keepdims=False)
    reach = KERNEL // 2
    ids_pad = jnp.pad(my_ids, (reach, reach), constant_values=-1)
    query_ids = lax.dynamic_slice_in_dim(my_ids, seq_at * local, local, 0)
    window_ids = lax.dynamic_slice_in_dim(
        ids_pad, seq_at * local + mine * block, block + 2 * reach, 0
    )
    low_ids = query_ids.reshape(n_q, TILE)[:, 0]
    top_ids = query_ids.reshape(n_q, TILE)[:, TILE - 1]
    starts = jnp.sum((my_ids[None] < low_ids[:, None]).astype(jnp.int32), axis=1) // TILE
    ends = jnp.sum((my_ids[None] <= top_ids[:, None]).astype(jnp.int32), axis=1)
    ends = (ends + TILE - 1) // TILE
    scalars = jnp.concatenate(
        [seq_at.astype(jnp.int32)[None], jnp.stack([starts, ends], axis=1).reshape(-1)]
    )
    reversed_buckets = jnp.pad(bucket_of[::-1], (0, 1))
    window = lax.dynamic_slice_in_dim(reversed_buckets, seq_at * local + mark(summed), (n_q + n_k) * TILE, 0)
    levels = lax.broadcasted_iota(jnp.int32, (position_table.shape[1], window.shape[0]), 0)
    onehot = (levels == window[None, :]).astype(jnp.float32)
    tables = jnp.concatenate([position_table, far_swap(position_table)], axis=0)
    biases = jnp.dot(tables, onehot, precision=HIGHEST) * LOG2E
    per_shard = q_cols // HEAD_DIM
    tiles = [bias_tiles(biases[:per_shard]), bias_tiles(biases[per_shard:])]
    summed = later(later(summed.astype(bf16), ffn1_partial[0][0]), ffn1_partial[0][-1])
    far_part = far_swap(summed)
    far_part, tiles[0], tiles[1], scalars, own_qkv = tie(
        far_part, tiles[0], tiles[1], scalars, own_qkv
    )
    stream_one = stream_zero + 0.5 * (
        reduce_parts(ffn1_partial[0]) + far_part.astype(jnp.float32)
    )

    attn_out, attn_hat, attn_inverse = norm_forward(stream_one, attn_gain)
    low = reorder(gather_parts(attn_out.astype(bf16)))
    hidden = ffn2_in.shape[1]
    ffn2_pieces = [own_rows(ffn2_in, mark(low)), own_rows(ffn2_out, mark(low))]
    ffn2_pieces = [far_swap(piece) for piece in ffn2_pieces]
    seq_bits = bits(lax.axis_size("seq"))
    both_kv = [plain(low, qkv[:, q_cols:]).astype(bf16)[None] for qkv in (own_qkv, far_qkv)]
    pieces, queries, mixtures, log_totals = [], [], [], []
    for shard in (0, 1):
        held = [both_kv[shard]]
        first = both_kv[1] if shard == 0 else mixtures[0]
        for bit in reversed(seq_bits):
            whole = join(held)
            if len(held) == len(seq_bits):
                whole = later(whole, first)
            held.append(swap(whole, "seq", bit))
        pieces.append(held)
        queries.append(plain(low, (own_qkv, far_qkv)[shard][:, :q_cols]).astype(bf16))
        mixture, log_total = attend(
            scalars, queries[shard], tiles[shard], query_ids[None], my_ids[:, None],
            pieces[shard], per_shard,
        )
        mixture, ffn2_pieces[shard] = tie(mixture, ffn2_pieces[shard])
        mixtures.append(mixture)
        log_totals.append(log_total)
    if hidden == width:
        ffn2_pieces = [jnp.concatenate(ffn2_pieces, axis=1)]
    far_ffn2 = [gather_all(piece) for piece in ffn2_pieces]
    if hidden == width:
        far_ffn2 = [far_ffn2[0][:, :hidden], far_ffn2[0][:, hidden:]]
    ffn2_weights = [(ffn2_in, ffn2_out), tuple(far_ffn2)]
    mix_parts = [cut_parts(mixture) for mixture in mixtures]
    branch = reduce_parts(
        [
            plain(own, output_weight) + against(far, far_output)
            for own, far in zip(*mix_parts)
        ]
    )
    stream_two = stream_one + branch

    stream_three, conv_state = conv_forward(stream_two, window_ids, conv_weights)
    ffn2_out_norm, ffn2_hat, ffn2_inverse = norm_forward(stream_three, ffn2_gain)
    branch, ffn2_state = ffn_forward(ffn2_out_norm.astype(bf16), ffn2_weights)
    stream_four = stream_three + 0.5 * branch
    final_out, final_hat, final_inverse = norm_forward(stream_four, final_gain)
    layer_low = final_out.astype(bf16)
    cot = lax.dynamic_index_in_dim(cotangent, my_row, 0, keepdims=False)
    cot = lax.dynamic_slice_in_dim(cot, mine * block, block, 0).astype(jnp.float32)
    grad_four, final_gain_grad = norm_backward(cot, final_hat, final_inverse, final_gain)

    normed_grad, ffn2_grads = ffn_backward(grad_four, ffn2_state, ffn2_weights)
    ffn2_grads = scatter_groups(ffn2_grads)
    ffn2_out_g, ffn2_in_g = ffn2_grads[:, : 2 * hidden], ffn2_grads[:, 2 * hidden :]
    stream_part, ffn2_gain_grad = norm_backward(normed_grad, ffn2_hat, ffn2_inverse, ffn2_gain)
    grad_three = grad_four + stream_part
    grad_two, conv_grads, conv_small = conv_backward(
        grad_three, conv_state, window_ids, conv_weights
    )
    branch_low = reorder(gather_parts(grad_two.astype(bf16)))
    branch_low, conv_grads = tie(branch_low, conv_grads)
    mix_grads = [
        against(branch_low, output_weight).astype(bf16),
        plain(branch_low, far_output).astype(bf16),
    ]
    layer_low = later(layer_low, branch_low)
    layer_near, layer_far = gather_parts(layer_low), far_swap(layer_low)
    q_grads, kv_grads, all_tile_grads = [], [], []
    turn = scalars
    for shard in (0, 1):
        q_grad, kv_grad, tile_grads = attend_back(
            turn, queries[shard], tiles[shard], query_ids[None], my_ids[:, None],
            mixtures[shard], mix_grads[shard], log_totals[shard], pieces[shard], per_shard,
        )
        if shard == 1:
            kv_grad, kv_grads[0], layer_near, layer_far = tie(
                kv_grad, kv_grads[0], layer_near, layer_far
            )
        for bit in seq_bits:
            half = kv_grad.shape[0] // 2
            kv_grad = (
                kv_grad[:half].astype(jnp.float32)
                + swap(kv_grad[half:], "seq", bit).astype(jnp.float32)
            ).astype(bf16)
            if shard == 0 and bit == 0:
                turn = scalars + mark(kv_grad)
        q_grads.append(q_grad)
        kv_grads.append(kv_grad[0])
        all_tile_grads.append(tile_grads)
    layer_far = gather_parts(layer_far)
    ffn2_out_came = far_swap(ffn2_out_g[:, hidden:])
    ffn2_in_g, conv_grads, kv_grads[1], ffn2_out_came, layer_far = tie(
        ffn2_in_g, conv_grads, kv_grads[1], ffn2_out_came, layer_far
    )
    conv_grads = scatter_groups(conv_grads)
    qkv_grads = [jnp.concatenate(pair, axis=1) for pair in zip(q_grads, kv_grads)]
    grad_parts = [cut_parts(grads) for grads in qkv_grads]
    partials = [against(own, own_qkv) + against(far, far_qkv) for own, far in zip(*grad_parts)]
    normed_grad = reduce_parts(partials)
    low = later(low, partials[0])
    attn_grads = jnp.concatenate(
        [
            grad_of(later(branch_low, partials[0]), jnp.concatenate(mixtures, axis=1)),
            grad_of(low, jnp.concatenate(qkv_grads, axis=1)),
        ],
        axis=1,
    )
    normed_grad, attn_grads = tie(normed_grad, attn_grads)
    stream_part, attn_gain_grad = norm_backward(normed_grad, attn_hat, attn_inverse, attn_gain)
    grad_one = grad_two + stream_part

    own_branch = (0.5 * grad_one).astype(bf16)
    near, far = tie(gather_parts(own_branch), far_swap(own_branch))
    branches = [near, gather_parts(far)]
    attn_grads, conv_grads, branches[0][-1] = tie(attn_grads, conv_grads, branches[0][-1])
    attn_grads = scatter_groups(attn_grads)
    pre_lows, partials = [], []
    for f in (0, 1):
        pre_lows.append(
            [
                (against(branch, ffn1_out) * silu_slope(pre)).astype(bf16)
                for branch, pre in zip(branches[f], ffn1_pre[f])
            ]
        )
        partials.append([against(pre_low, ffn1_in) for pre_low in pre_lows[f]])
    every_frame = lambda lists: join(lists[0] + lists[1])
    table_grads = [
        lax.dot_general(
            offset_sums(tile_grads, branches[0][-1]), onehot, (((1,), (1,)), ((), ())),
            precision=HIGHEST,
        )
        for tile_grads in all_tile_grads
    ]
    last_sent = partials[1][-1]
    ffn1_grads = jnp.concatenate(
        [
            grad_of(later(every_frame(branches), last_sent), every_frame(ffn1_act)),
            grad_of(later(every_frame(ffn1_low), last_sent), every_frame(pre_lows)),
        ],
        axis=1,
    )
    ffn1_grads, attn_grads = tie(ffn1_grads, attn_grads)
    ffn1_grads = scatter_groups(ffn1_grads).astype(jnp.float32)
    partials[0][-1] = later(partials[0][-1], last_sent)
    ffn2_in_came = far_swap(later(ffn2_in_g[:, hidden:], branches[1][0]))
    far_sum, ffn2_in_came = tie(reduce_parts(partials[1]).astype(bf16), ffn2_in_came)
    head_bits = bits(n_heads)
    conv_grads = conv_grads.reshape((2,) * len(head_bits) + (-1, 3 * width))
    for bit in head_bits[:-1]:
        conv_grads = fold_step(later(conv_grads, branches[1][0]), bit)
    far_part, conv_grads = tie(far_swap(far_sum), conv_grads)
    near_sum = reduce_parts(partials[0])
    normed_grad = near_sum + far_part.astype(jnp.float32)
    stream_part, ffn1_gain_grad = norm_backward(normed_grad, *ffn1_norm, ffn1_gain)
    grad_zero = grad_one + stream_part

    low = grad_zero.astype(bf16)
    near, far = tie(gather_parts(low), far_swap(low))
    spread_grad = near, gather_parts(far)

    (f2_out_g,) = add_far(ffn2_out_g, ffn2_out_came, [(0, hidden)])
    (f2_in_g,) = add_far(ffn2_in_g, ffn2_in_came, [(0, hidden)])
    n_out = 2 * out_cols
    conv_grads = fold_step(later(conv_grads, spread_grad[1][0]), head_bits[-1])
    attn_came = far_columns(later(attn_grads, spread_grad[1][0]), [(out_cols, n_out), (n_out + n_qkv, n_out + 2 * n_qkv)])
    o_g, qkv_g = add_far(attn_grads, attn_came, [(0, out_cols), (n_out, n_out + n_qkv)])

    all_heads = jnp.zeros((n_heads * per_shard, position_table.shape[1]), jnp.float32)
    all_heads = lax.dynamic_update_slice_in_dim(all_heads, table_grads[0], place * per_shard, 0)
    all_heads = lax.dynamic_update_slice_in_dim(
        all_heads, table_grads[1], (place ^ team) * per_shard, 0
    )
    gains = [ffn1_gain_grad, attn_gain_grad, ffn2_gain_grad, final_gain_grad] + conv_small
    small = jnp.concatenate([jnp.stack(gains).reshape(-1), all_heads.reshape(-1)])
    small = later(small.reshape(-1, 128), spread_grad[1][0])
    small = sum_everyone(small).reshape(-1)
    gains_all = small[: len(gains) * width].reshape(len(gains), width)
    table_all = small[len(gains) * width :].reshape(all_heads.shape)
    table_mine = lax.dynamic_slice_in_dim(table_all, place * per_shard, per_shard, 0)
    table_cols = table_mine.shape[1] // groups
    table_mine = lax.dynamic_slice_in_dim(table_mine, group_at * table_cols, table_cols, 1)
    group_part = lax.dynamic_slice_in_dim(gains_all[:4], group_at * part, part, 1)
    every = width // (groups * n_heads)
    conv_part = lax.dynamic_slice_in_dim(
        gains_all[4:], lax.axis_index(("dp", "seq", "heads")) * every, every, 1
    )

    def everywhere(parts):
        near, far = reorder(parts[0]), reorder(parts[1])
        first = my_row == 0
        return jnp.stack([jnp.where(first, near, far), jnp.where(first, far, near)])

    return (
        everywhere((layer_near, layer_far)),
        everywhere(spread_grad).astype(jnp.float32),
        group_part[0],
        ffn1_grads[:, hidden1:],
        ffn1_grads[:, :hidden1].T,
        group_part[1],
        qkv_g[:, :q_cols],
        qkv_g[:, q_cols : 2 * q_cols],
        qkv_g[:, 2 * q_cols :],
        o_g.T,
        table_mine,
        conv_part[0],
        conv_grads[:, : 2 * width],
        conv_part[2:],
        conv_part[1],
        conv_grads[:, 2 * width :],
        group_part[2],
        f2_in_g,
        f2_out_g.T,
        group_part[3],
    )


def solution(mesh):
    return jax.shard_map(
        on_device,
        mesh=mesh,
        in_specs=(
            P("dp", "seq", None),
            P("dp", None),
            P(),
            P(),
            P(None, "heads"),
            P("heads", None),
            P(),
            P(None, "heads"),
            P(None, "heads"),
            P(None, "heads"),
            P("heads", None),
            P("heads", None),
            P(("dp", "seq", "heads")),
            P(("dp", "seq", "heads"), None),
            P(None, ("dp", "seq", "heads")),
            P(("dp", "seq", "heads")),
            P(("dp", "seq", "heads"), None),
            P(),
            P(None, "heads"),
            P("heads", None),
            P(),
            P("dp", "seq", None),
        ),
        out_specs=(
            P("dp", "seq", None),
            P("dp", "seq", None),
            P(("dp", "seq")),
            P(("dp", "seq"), "heads"),
            P("heads", ("dp", "seq")),
            P(("dp", "seq")),
            P(("dp", "seq"), "heads"),
            P(("dp", "seq"), "heads"),
            P(("dp", "seq"), "heads"),
            P("heads", ("dp", "seq")),
            P("heads", ("dp", "seq")),
            P(("dp", "seq", "heads")),
            P(("dp", "seq", "heads"), None),
            P(None, ("dp", "seq", "heads")),
            P(("dp", "seq", "heads")),
            P(("dp", "seq", "heads"), None),
            P(("dp", "seq")),
            P(("dp", "seq"), "heads"),
            P("heads", ("dp", "seq")),
            P(("dp", "seq")),
        ),
        check_vma=False,
    )
```

```python
import math
import jax
import jax.numpy as jnp
from jax import lax
from jax.experimental import pallas as pl
from jax.experimental.layout import Layout, with_layout_constraint
from jax.experimental.pallas import tpu as pltpu
from jax.sharding import PartitionSpec as P

HEAD_DIM=128
NEGATIVE=-1e30
LOG2E=math.log2(math.e)
TILE=256

def bias_tiles_kernel(win_ref, out_ref):
    width = win_ref.shape[2]
    rows = jnp.broadcast_to(win_ref[0], (8, width))
    rows = pltpu.roll(rows, width - (TILE - 1), 1, stride=1, stride_axis=0)
    step = 8
    while step < TILE:
        rows = jnp.concatenate([rows, pltpu.roll(rows, step, 1)], axis=0)
        step *= 2
    for t in range(out_ref.shape[1]):
        out_ref[0, t] = rows[:, t * TILE : (t + 1) * TILE]

def bias_tiles(window):
    heads, width = window.shape
    tiles = width // TILE - 1
    return pl.pallas_call(
        bias_tiles_kernel,
        grid=(heads,),
        in_specs=[pl.BlockSpec((1, 1, width), lambda h: (h, 0, 0))],
        out_specs=pl.BlockSpec((1, tiles, TILE, TILE), lambda h: (h, 0, 0, 0)),
        out_shape=jax.ShapeDtypeStruct((heads, tiles, TILE, TILE), jnp.float32),
        cost_estimate=pl.CostEstimate(flops=TILE, transcendentals=0, bytes_accessed=TILE),
    )(window[:, None])

def offset_sums_kernel(when_ref, tiles_ref, out_ref, wide):
    tiles = tiles_ref.shape[1]
    for t in range(tiles):
        wide[:, t * TILE : (t + 1) * TILE] = tiles_ref[0, t]
    wide[:, tiles * TILE :] = jnp.zeros((TILE, TILE), jnp.float32)
    rows = wide[...]
    half = TILE // 2
    while half >= 1:
        rows = pltpu.roll(rows[:half], half, 1) + rows[half:]
        half //= 2
    out_ref[0] = rows

def offset_sums(tile_grads, when):
    heads, tiles = tile_grads.shape[:2]
    width = (tiles + 1) * TILE
    return pl.pallas_call(
        offset_sums_kernel,
        grid=(heads,),
        in_specs=[
            pl.BlockSpec(memory_space=pltpu.SMEM),
            pl.BlockSpec((1, tiles, TILE, TILE), lambda h: (h, 0, 0, 0)),
        ],
        out_specs=pl.BlockSpec((1, 1, width), lambda h: (h, 0, 0)),
        out_shape=jax.ShapeDtypeStruct((heads, 1, width), jnp.float32),
        scratch_shapes=[pltpu.VMEM((TILE, width), jnp.float32)],
        cost_estimate=pl.CostEstimate(flops=TILE, transcendentals=0, bytes_accessed=TILE),
    )(mark(when)[None], tile_grads)[:, 0]

def columns_of(head, per_shard):
    shard, at = head // per_shard, head % per_shard
    key = (shard * 2 * per_shard + at) * HEAD_DIM
    value = key + per_shard * HEAD_DIM
    return pl.multiple_of(key, HEAD_DIM), pl.multiple_of(value, HEAD_DIM)

def load_pieces(scal, pieces, whole, sems):
    local = pieces[0].shape[1]
    copies = []
    count = sum(p.shape[0] for p in pieces)
    nbits = count.bit_length() - 1
    rel = [0]
    n = 0
    for p in pieces:
        ids = [0] if p is pieces[0] else None
        if ids is None:
            bit = nbits - 1 - (n.bit_length() - 1)
            ids = [r ^ (1 << bit) for r in rel]
            rel = rel + ids
        for k, r in enumerate(ids):
            at = pl.multiple_of((scal[0] ^ r) * local, local)
            copies.append(pltpu.make_async_copy(p.at[k], whole.at[pl.ds(at, local)], sems.at[n]))
            n += 1
    for c in copies: c.start()
    for c in copies: c.wait()

def forward_kernel(scal, per_shard, pieces_n, *refs):
    q_ref, bias_ref, qid_ref, kid_ref = refs[:4]
    pieces = refs[4 : 4 + pieces_n]
    out_ref, lse_ref, whole, sems = refs[4 + pieces_n :]
    head = pl.program_id(0)
    @pl.when(head == 0)
    def _(): load_pieces(scal, pieces, whole, sems)
    kcol, vcol = columns_of(head, per_shard)
    scale = LOG2E * HEAD_DIM ** -0.5
    nk = whole.shape[0] // TILE
    for qb in range(q_ref.shape[0] // TILE):
        q = q_ref[qb * TILE : (qb + 1) * TILE, :]
        qid = qid_ref[:, qb * TILE : (qb + 1) * TILE]
        def body(kb, carry):
            top, total, acc = carry
            at = pl.multiple_of(kb * TILE, TILE)
            k = whole[pl.ds(at, TILE), pl.ds(kcol, HEAD_DIM)]
            v = whole[pl.ds(at, TILE), pl.ds(vcol, HEAD_DIM)]
            s = lax.dot_general(k, q, (((1,), (1,)), ((), ())), preferred_element_type=jnp.float32)
            s = s * scale + bias_ref[0, qb - kb + nk - 1]
            s = jnp.where(kid_ref[pl.ds(at, TILE), :] == qid, s, NEGATIVE)
            new_top = jnp.maximum(top, jnp.max(s, axis=0, keepdims=True))
            p = jnp.exp2(s - new_top)
            fade = jnp.exp2(top - new_top)
            total = total * fade + jnp.sum(p, axis=0, keepdims=True)
            acc = acc * fade + lax.dot_general(v, p.astype(jnp.bfloat16), (((0,), (0,)), ((), ())), preferred_element_type=jnp.float32)
            return new_top, total, acc
        top, total, acc = lax.fori_loop(scal[1 + 2 * qb], scal[2 + 2 * qb], body, (
            jnp.full((1, TILE), NEGATIVE, jnp.float32), jnp.zeros((1, TILE), jnp.float32), jnp.zeros((HEAD_DIM, TILE), jnp.float32)))
        out_ref[qb * TILE : (qb + 1) * TILE, :] = (acc / total).T.astype(jnp.bfloat16)
        lse_ref[0, :, qb * TILE : (qb + 1) * TILE] = top + jnp.log2(total)

def attend(scalars, q, tiles, qid, kid, pieces, per_shard):
    tokens, width = q.shape
    heads = width // HEAD_DIM
    length = kid.shape[0]
    count = sum(p.shape[0] for p in pieces)
    n_tiles = tiles.shape[1]
    fn = lambda scal, *refs: forward_kernel(scal, per_shard, len(pieces), *refs)
    flops = 4 * heads * tokens * length * HEAD_DIM
    return pl.pallas_call(
        fn,
        grid_spec=pltpu.PrefetchScalarGridSpec(
            num_scalar_prefetch=1, grid=(heads,),
            in_specs=[
                pl.BlockSpec((tokens, HEAD_DIM), lambda h, s: (0, h)),
                pl.BlockSpec((1, n_tiles, TILE, TILE), lambda h, s: (h, 0, 0, 0)),
                pl.BlockSpec((1, tokens), lambda h, s: (0, 0)),
                pl.BlockSpec((length, 1), lambda h, s: (0, 0)),
            ] + [pl.BlockSpec(memory_space=pl.ANY)] * len(pieces),
            out_specs=[
                pl.BlockSpec((tokens, HEAD_DIM), lambda h, s: (0, h)),
                pl.BlockSpec((1, 1, tokens), lambda h, s: (h, 0, 0)),
            ],
            scratch_shapes=[pltpu.VMEM((length, pieces[0].shape[-1]), jnp.bfloat16), pltpu.SemaphoreType.DMA((count,))],
        ),
        out_shape=[jax.ShapeDtypeStruct((tokens, width), jnp.bfloat16), jax.ShapeDtypeStruct((heads, 1, tokens), jnp.float32)],
        cost_estimate=pl.CostEstimate(flops=flops, transcendentals=heads*tokens*length, bytes_accessed=heads*n_tiles*TILE*TILE*4),
    )(scalars, q, tiles, qid, kid, *pieces)

def backward_kernel(scal, per_shard, pieces_n, *refs):
    q_ref, bias_ref, qid_ref, kid_ref, mix_ref, dmix_ref, lse_ref = refs[:7]
    pieces = refs[7 : 7 + pieces_n]
    dq_ref, dkv_ref, dtile_ref, whole, dk_acc, dv_acc, sems = refs[7 + pieces_n :]
    head = pl.program_id(0)
    @pl.when(head == 0)
    def _(): load_pieces(scal, pieces, whole, sems)
    kcol, vcol = columns_of(head, per_shard)
    scale = HEAD_DIM ** -0.5
    nk = whole.shape[0] // TILE
    dk_acc[...] = jnp.zeros_like(dk_acc)
    dv_acc[...] = jnp.zeros_like(dv_acc)
    dtile_ref[...] = jnp.zeros_like(dtile_ref)
    for qb in range(q_ref.shape[0] // TILE):
        rows = slice(qb * TILE, (qb + 1) * TILE)
        q = q_ref[rows, :]
        qid = qid_ref[:, rows]
        dmix = dmix_ref[rows, :]
        lse = lse_ref[0, :, rows]
        delta = jnp.sum((dmix.astype(jnp.float32) * mix_ref[rows, :].astype(jnp.float32)).T, axis=0, keepdims=True)
        def body(kb, dq):
            at = pl.multiple_of(kb * TILE, TILE)
            k = whole[pl.ds(at, TILE), pl.ds(kcol, HEAD_DIM)]
            v = whole[pl.ds(at, TILE), pl.ds(vcol, HEAD_DIM)]
            s = lax.dot_general(k, q, (((1,), (1,)), ((), ())), preferred_element_type=jnp.float32)
            s = s * (scale * LOG2E) + bias_ref[0, qb - kb + nk - 1]
            s = jnp.where(kid_ref[pl.ds(at, TILE), :] == qid, s, NEGATIVE)
            p = jnp.exp2(s - lse)
            dp = lax.dot_general(v, dmix, (((1,), (1,)), ((), ())), preferred_element_type=jnp.float32)
            ds = p * (dp - delta)
            dtile_ref[0, qb - kb + nk - 1] += ds
            low = ds.astype(jnp.bfloat16)
            dv_acc[pl.ds(at, TILE), :] += jnp.dot(p.astype(jnp.bfloat16), dmix, preferred_element_type=jnp.float32)
            dk_acc[pl.ds(at, TILE), :] += jnp.dot(low, q, preferred_element_type=jnp.float32)
            return dq + lax.dot_general(k, low, (((0,), (0,)), ((), ())), preferred_element_type=jnp.float32)
        dq = lax.fori_loop(scal[1 + 2 * qb], scal[2 + 2 * qb], body, jnp.zeros((HEAD_DIM, TILE), jnp.float32))
        dq_ref[rows, :] = (dq * scale).T.astype(jnp.bfloat16)
    count, local = dkv_ref.shape[:2]
    nbits = count.bit_length() - 1
    for block in range(count):
        diff = scal[0] ^ block
        slot = 0
        for bit in range(nbits):
            slot = slot | (((diff >> bit) & 1) << (nbits - 1 - bit))
        rows = slice(block * local, (block + 1) * local)
        dkv_ref[slot, :, pl.ds(kcol, HEAD_DIM)] = (dk_acc[rows, :] * scale).astype(jnp.bfloat16)
        dkv_ref[slot, :, pl.ds(vcol, HEAD_DIM)] = dv_acc[rows, :].astype(jnp.bfloat16)

def attend_back(scalars, q, tiles, qid, kid, mixture, mix_grad, lse, pieces, per_shard):
    tokens, width = q.shape
    heads = width // HEAD_DIM
    length = kid.shape[0]
    count = sum(p.shape[0] for p in pieces)
    n_tiles = tiles.shape[1]
    kvw = pieces[0].shape[-1]
    fn = lambda scal, *refs: backward_kernel(scal, per_shard, len(pieces), *refs)
    head_block = pl.BlockSpec((tokens, HEAD_DIM), lambda h, s: (0, h))
    tile_block = pl.BlockSpec((1, n_tiles, TILE, TILE), lambda h, s: (h, 0, 0, 0))
    return pl.pallas_call(
        fn,
        grid_spec=pltpu.PrefetchScalarGridSpec(
            num_scalar_prefetch=1, grid=(heads,),
            in_specs=[head_block, tile_block,
                pl.BlockSpec((1, tokens), lambda h, s: (0, 0)),
                pl.BlockSpec((length, 1), lambda h, s: (0, 0)),
                head_block, head_block,
                pl.BlockSpec((1, 1, tokens), lambda h, s: (h, 0, 0)),
            ] + [pl.BlockSpec(memory_space=pl.ANY)] * len(pieces),
            out_specs=[head_block,
                pl.BlockSpec((count, length // count, kvw), lambda h, s: (0, 0, 0)),
                tile_block],
            scratch_shapes=[pltpu.VMEM((length, kvw), jnp.bfloat16), pltpu.VMEM((length, HEAD_DIM), jnp.float32), pltpu.VMEM((length, HEAD_DIM), jnp.float32), pltpu.SemaphoreType.DMA((count,))],
        ),
        out_shape=[jax.ShapeDtypeStruct((tokens, width), jnp.bfloat16),
                   jax.ShapeDtypeStruct((count, length // count, kvw), jnp.bfloat16),
                   jax.ShapeDtypeStruct(tiles.shape, jnp.float32)],
        compiler_params=pltpu.CompilerParams(vmem_limit_bytes=50 * 1024 * 1024),
        cost_estimate=pl.CostEstimate(flops=10 * heads * tokens * length * HEAD_DIM, transcendentals=heads*tokens*length, bytes_accessed=2*heads*n_tiles*TILE*TILE*4),
    )(scalars, q, tiles, qid, kid, mixture, mix_grad, lse, *pieces)


EPSILON = 1e-05
KERNEL = 5
HIGHEST = lax.Precision.HIGHEST


def bits(count):
    return list(range(count.bit_length() - 1))


def swap(array, axis, bit):
    count = lax.axis_size(axis)
    return lax.ppermute(array, axis, [(i, i ^ (1 << bit)) for i in range(count)])


def bit_of(axis, bit):
    return (lax.axis_index(axis) >> bit) & 1


def gather_all(piece):
    return lax.all_gather(piece, ("dp", "seq"), axis=0, tiled=True)


def own_rows(array, shift=0):
    axes = ("dp", "seq")
    count = math.prod(lax.axis_size(axis) for axis in axes)
    part = array.shape[0] // count
    return lax.dynamic_slice_in_dim(array, lax.axis_index(axes) * part + shift, part, 0)


def outer(left, right):
    return lax.dot_general(
        left, right, (((0,), (0,)), ((), ())), preferred_element_type=jnp.float32
    )


def plain(left, right):
    return jnp.dot(left, right, preferred_element_type=jnp.float32)


def against(left, right):
    return lax.dot_general(
        left, right, (((1,), (1,)), ((), ())), preferred_element_type=jnp.float32
    )


def norm_forward(values, gain_vec):
    centred = values - jnp.mean(values, axis=-1, keepdims=True)
    inverse = lax.rsqrt(jnp.mean(centred * centred, axis=-1, keepdims=True) + EPSILON)
    normed = centred * inverse
    return (normed * gain_vec.astype(jnp.float32), normed, inverse)


def norm_backward(gradient, normed, inverse, gain_vec):
    scaled = gradient * gain_vec.astype(jnp.float32)
    mean_grad = jnp.mean(scaled, axis=-1, keepdims=True)
    second = jnp.mean(scaled * normed, axis=-1, keepdims=True)
    gain_grad = jnp.sum((gradient * normed).reshape(-1, gradient.shape[-1]), axis=0)
    return (inverse * (scaled - mean_grad - normed * second), gain_grad)


def silu_slope(values):
    sigmoid = jax.nn.sigmoid(values)
    return sigmoid * (1.0 + values * (1.0 - sigmoid))


def sum_over(array, axes):
    for axis in axes:
        for bit in bits(lax.axis_size(axis)):
            array = array + swap(array, axis, bit)
    return array


def tie(*arrays):
    return lax.optimization_barrier(arrays)


def mark(value):
    first = value[(0,) * value.ndim]
    return (first != first).astype(jnp.int32)


def later(array, value):
    return array + mark(value).astype(array.dtype)


def far_swap(array):
    return swap(array, "heads", bits(lax.axis_size("heads"))[-1])


def team_bits():
    return bits(lax.axis_size("heads"))[:-1]


def gather_parts(own):
    parts = [own]
    for bit in team_bits():
        held = parts[0] if len(parts) == 1 else jnp.concatenate(parts, axis=0)
        parts.append(swap(held, "heads", bit))
    return parts


def reduce_parts(partials):
    partials = list(partials)
    for bit in reversed(team_bits()):
        came = swap(partials.pop().astype(jnp.bfloat16), "heads", bit).astype(jnp.float32)
        at, kept = 0, []
        for item in partials:
            kept.append(item + came[at : at + item.shape[0]])
            at += item.shape[0]
        partials = kept
    return partials[0]


def spread(own):
    return gather_parts(own), gather_parts(far_swap(own))


def reorder(parts):
    team = lax.axis_size("heads") // 2
    mine = lax.axis_index("heads") % team
    whole = join(parts)
    block = whole.shape[0] // team
    if team == 2:
        first, second = parts
        lower = mine == 0
        return jnp.concatenate(
            [jnp.where(lower, first, second), jnp.where(lower, second, first)], axis=0
        )
    return jnp.concatenate(
        [lax.dynamic_slice_in_dim(whole, (at ^ mine) * block, block, 0) for at in range(team)],
        axis=0,
    )


def cut_parts(array):
    team = lax.axis_size("heads") // 2
    mine = lax.axis_index("heads") % team
    block = array.shape[0] // team
    take = lambda at: lax.dynamic_slice_in_dim(array, (at ^ mine) * block, block, 0)
    parts = [take(0)]
    for bit in team_bits():
        parts.append(join([take(at) for at in range(1 << bit, 2 << bit)]))
    return parts


def join(parts):
    return parts[0] if len(parts) == 1 else jnp.concatenate(parts, axis=0)


def scatter_groups(array):
    return lax.psum_scatter(array, ("dp", "seq"), scatter_dimension=0, tiled=True)


def grad_of(left, right):
    grads = outer(left, right).astype(jnp.bfloat16)
    return with_layout_constraint(grads, Layout(major_to_minor=(0, 1)))


def ffn_forward(low_own, weights):
    lows = gather_parts(low_own)
    pres = [[plain(low, weight_in) for weight_in, _ in weights] for low in lows]
    acts = [[jax.nn.silu(pre).astype(jnp.bfloat16) for pre in pair] for pair in pres]
    partials = [
        sum(plain(act, weight_out) for act, (_, weight_out) in zip(pair, weights))
        for pair in acts
    ]
    return reduce_parts(partials), (lows, pres, acts)


def ffn_backward(gradient, saved, weights):
    lows, pres, acts = saved
    branches = gather_parts((0.5 * gradient).astype(jnp.bfloat16))
    pre_lows = [
        [
            (against(branch, weight_out) * silu_slope(pre)).astype(jnp.bfloat16)
            for (_, weight_out), pre in zip(weights, pair)
        ]
        for branch, pair in zip(branches, pres)
    ]
    partials = [
        sum(against(pre_low, weight_in) for pre_low, (weight_in, _) in zip(pair, weights))
        for pair in pre_lows
    ]
    normed_grad = reduce_parts(partials)
    low, branch = join(lows), join(branches)
    wide = lambda items: join([jnp.concatenate(pair, axis=1) for pair in items])
    grads = jnp.concatenate(
        [grad_of(branch, wide(acts)), grad_of(low, wide(pre_lows))], axis=1
    )
    return tie(normed_grad, grads)


def far_columns(array, ranges):
    return far_swap(jnp.concatenate([array[:, a:b] for a, b in ranges], axis=1))


def add_far(array, came, ranges):
    outs, at = [], 0
    for a, b in ranges:
        outs.append(array[:, a:b].astype(jnp.float32) + came[:, at : at + b - a].astype(jnp.float32))
        at += b - a
    return outs


def halo(array, reach):
    peers, n_heads = lax.axis_size("seq"), lax.axis_size("heads")
    team = n_heads // 2
    spot = lambda row, at: (at // team) * n_heads + row * team + at % team
    up = [
        (spot(row, at), spot(row, at + 1))
        for row in range(2)
        for at in range(peers * team - 1)
    ]
    down = [(j, i) for i, j in up]
    before = lax.ppermute(array[array.shape[0] - reach :], ("seq", "heads"), up)
    after_it = lax.ppermute(array[:reach], ("seq", "heads"), down)
    return jnp.concatenate([before, array, after_it], axis=0)


def conv_forward(stream, window_ids, weights):
    in_weight, out_weight, taps, gain_one, gain_two = weights
    tokens, width = stream.shape
    reach = KERNEL // 2
    normed_out, normed, inverse = norm_forward(stream, gain_one)
    low = normed_out.astype(jnp.bfloat16)
    doubled = plain(low, in_weight)
    gate = jax.nn.sigmoid(doubled[:, width:])
    glu_low = (doubled[:, :width] * gate).astype(jnp.bfloat16)
    padded = halo(glu_low, reach)
    centre = window_ids[reach : reach + tokens]
    taps_float = taps.astype(jnp.float32)
    depth = jnp.zeros((tokens, width), jnp.float32)
    for k in range(KERNEL):
        same = (window_ids[k : k + tokens] == centre).astype(jnp.float32)[:, None]
        depth = depth + padded[k : k + tokens].astype(jnp.float32) * taps_float[k] * same
    norm_two, hat_two, inverse_two = norm_forward(depth, gain_two)
    swish_low = jax.nn.silu(norm_two).astype(jnp.bfloat16)
    branch = plain(swish_low, out_weight)
    saved = (normed, inverse, low, doubled, gate, padded, hat_two, inverse_two, norm_two, swish_low)
    return (stream + branch, saved)


def conv_backward(gradient, saved, window_ids, weights):
    in_weight, out_weight, taps, gain_one, gain_two = weights
    normed, inverse, low, doubled, gate, padded, hat_two, inverse_two, norm_two, swish_low = saved
    tokens, width = gradient.shape
    reach = KERNEL // 2
    branch_low = gradient.astype(jnp.bfloat16)
    swish_grad = against(branch_low, out_weight)
    depth_grad, gain_two_grad = norm_backward(
        swish_grad * silu_slope(norm_two), hat_two, inverse_two, gain_two
    )
    depth_low = depth_grad.astype(jnp.bfloat16)
    beside = halo(depth_low, reach)
    centre = window_ids[reach : reach + tokens]
    taps_float = taps.astype(jnp.float32)
    depth_float = depth_low.astype(jnp.float32)
    glu_grad = jnp.zeros((tokens, width), jnp.float32)
    tap_grads = []
    for k in range(KERNEL):
        same = (window_ids[k : k + tokens] == centre).astype(jnp.float32)[:, None]
        tap_grads.append(
            jnp.sum(depth_float * padded[k : k + tokens].astype(jnp.float32) * same, axis=0)
        )
        mirror = 2 * reach - k
        back = (window_ids[mirror : mirror + tokens] == centre).astype(jnp.float32)[:, None]
        glu_grad = (
            glu_grad + beside[mirror : mirror + tokens].astype(jnp.float32) * taps_float[k] * back
        )
    gate_in = doubled[:, :width]
    doubled_low = jnp.concatenate(
        [glu_grad * gate, glu_grad * gate_in * gate * (1.0 - gate)], axis=-1
    ).astype(jnp.bfloat16)
    normed_grad = against(doubled_low, in_weight)
    grads = jnp.concatenate([grad_of(low, doubled_low), grad_of(swish_low, branch_low)], axis=1)
    part, gain_one_grad = norm_backward(normed_grad, normed, inverse, gain_one)
    small = [gain_one_grad, gain_two_grad] + tap_grads
    return (gradient + part, grads, small)


def fold_step(both, bit):
    here = bit_of("heads", bit)
    kept = lax.dynamic_index_in_dim(both, here, both.ndim - 3, keepdims=False)
    sent = lax.dynamic_index_in_dim(both, 1 - here, both.ndim - 3, keepdims=False)
    came = swap(sent.astype(jnp.bfloat16), "heads", bit)
    return kept.astype(jnp.float32) + came.astype(jnp.float32)


def on_device(
    frames,
    segment_ids,
    bucket_of,
    ffn1_gain,
    ffn1_in,
    ffn1_out,
    attn_gain,
    query_weight,
    key_weight,
    value_weight,
    output_weight,
    position_table,
    conv_gain,
    pointwise_in,
    depthwise,
    depth_gain,
    pointwise_out,
    ffn2_gain,
    ffn2_in,
    ffn2_out,
    final_gain,
    cotangent,
):
    row_count, local, width = frames.shape
    length = segment_ids.shape[1]
    n_heads = lax.axis_size("heads")
    team = n_heads // 2
    place = lax.axis_index("heads")
    seq_at = lax.axis_index("seq")
    assert row_count == 2
    my_row, mine = place // team, place % team
    block = local // team
    bf16 = jnp.bfloat16
    groups = lax.axis_size("dp") * lax.axis_size("seq")
    group_at = lax.axis_index(("dp", "seq"))
    part = width // groups

    q_cols, out_cols = query_weight.shape[1], output_weight.shape[0]
    n_qkv = 3 * q_cols
    output_piece = lax.dynamic_slice_in_dim(output_weight, group_at * part, part, 1).T
    attn_piece = [own_rows(w) for w in (query_weight, key_weight, value_weight)]
    attn_piece = far_swap(jnp.concatenate(attn_piece + [output_piece], axis=1))
    small_piece = jnp.concatenate([depthwise, conv_gain[None], depth_gain[None]], axis=0).T
    small_piece = jnp.pad(small_piece, ((0, 0), (0, 128 - small_piece.shape[1])))
    conv_piece = jnp.concatenate([pointwise_in, pointwise_out, small_piece], axis=1)
    rows = [lax.dynamic_index_in_dim(frames, my_row ^ f, 0, keepdims=False) for f in (0, 1)]
    units = [cut_parts(row) for row in rows]
    stream_zero = units[0][0].astype(jnp.float32)
    hidden1 = ffn1_in.shape[1]
    ffn1_low, ffn1_pre, ffn1_act, ffn1_partial = [], [], [], []
    ffn1_norm = None
    for f in (0, 1):
        lows, pres, acts, partials = [], [], [], []
        for unit in units[f]:
            normed_out, normed, inverse = norm_forward(unit.astype(jnp.float32), ffn1_gain)
            if ffn1_norm is None:
                ffn1_norm = (normed, inverse)
            low = normed_out.astype(bf16)
            pre = plain(low, ffn1_in)
            act = jax.nn.silu(pre).astype(bf16)
            lows.append(low)
            pres.append(pre)
            acts.append(act)
            partials.append(plain(act, ffn1_out))
        ffn1_low.append(lows)
        ffn1_pre.append(pres)
        ffn1_act.append(acts)
        ffn1_partial.append(partials)
    attn_piece = later(attn_piece, ffn1_partial[1][-1])
    far_attn = gather_all(attn_piece)
    far_qkv, far_output = far_attn[:, :n_qkv], far_attn[:, n_qkv:]
    for bit in bits(n_heads):
        other = swap(conv_piece, "heads", bit)
        lower = bit_of("heads", bit) == 0
        conv_piece = jnp.concatenate(
            [jnp.where(lower, conv_piece, other), jnp.where(lower, other, conv_piece)], axis=0
        )
        if bit < len(bits(n_heads)) - 1:
            conv_piece = later(conv_piece, ffn1_partial[1][-1])
    summed = reduce_parts(ffn1_partial[1])
    near_first = ffn1_partial[0][:-1] + [later(ffn1_partial[0][-1], summed)]
    n_q, n_k = local // TILE, length // TILE
    reversed_buckets = jnp.pad(bucket_of[::-1], (0, 1))
    window = lax.dynamic_slice_in_dim(reversed_buckets, seq_at * local + mark(summed), (n_q + n_k) * TILE, 0)
    levels = lax.broadcasted_iota(jnp.int32, (position_table.shape[1], window.shape[0]), 0)
    onehot = (levels == window[None, :]).astype(jnp.float32)
    tables = jnp.concatenate([position_table, far_swap(position_table)], axis=0)
    biases = jnp.dot(tables, onehot, precision=HIGHEST) * LOG2E
    per_shard = q_cols // HEAD_DIM
    tiles = [bias_tiles(biases[:per_shard]), bias_tiles(biases[per_shard:])]
    summed = later(later(summed.astype(bf16), ffn1_partial[0][0]), ffn1_partial[0][-1])
    far_part = far_swap(summed)
    far_part, tiles[0], tiles[1], near_part = tie(
        far_part, tiles[0], tiles[1], reduce_parts(near_first)
    )
    stream_one = stream_zero + 0.5 * (
        near_part + far_part.astype(jnp.float32)
    )

    conv_all = gather_all(later(conv_piece, far_part))
    pw_in, pw_out = conv_all[:, : 2 * width], conv_all[:, 2 * width : 3 * width]
    small_all = conv_all[:, 3 * width : 3 * width + KERNEL + 2].T
    conv_weights = (pw_in, pw_out, small_all[:KERNEL], small_all[KERNEL], small_all[KERNEL + 1])

    my_ids = lax.dynamic_index_in_dim(segment_ids, my_row + mark(far_part), 0, keepdims=False)
    reach = KERNEL // 2
    ids_pad = jnp.pad(my_ids, (reach, reach), constant_values=-1)
    query_ids = lax.dynamic_slice_in_dim(my_ids, seq_at * local, local, 0)
    window_ids = lax.dynamic_slice_in_dim(
        ids_pad, seq_at * local + mine * block, block + 2 * reach, 0
    )
    low_ids = query_ids.reshape(n_q, TILE)[:, 0]
    top_ids = query_ids.reshape(n_q, TILE)[:, TILE - 1]
    starts = jnp.sum((my_ids[None] < low_ids[:, None]).astype(jnp.int32), axis=1) // TILE
    ends = jnp.sum((my_ids[None] <= top_ids[:, None]).astype(jnp.int32), axis=1)
    ends = (ends + TILE - 1) // TILE
    scalars = jnp.concatenate(
        [seq_at.astype(jnp.int32)[None], jnp.stack([starts, ends], axis=1).reshape(-1)]
    )

    attn_out, attn_hat, attn_inverse = norm_forward(stream_one, attn_gain)
    low = reorder(gather_parts(attn_out.astype(bf16)))
    hidden = ffn2_in.shape[1]
    ffn2_pieces = [own_rows(ffn2_in, mark(low)), own_rows(ffn2_out, mark(low))]
    ffn2_pieces = [far_swap(piece) for piece in ffn2_pieces]
    seq_bits = bits(lax.axis_size("seq"))
    own_qkv = jnp.concatenate(
        [later(query_weight, far_part), key_weight, value_weight], axis=1
    )
    both_kv = [plain(low, qkv[:, q_cols:]).astype(bf16)[None] for qkv in (own_qkv, far_qkv)]
    pieces, queries, mixtures, log_totals = [], [], [], []
    for shard in (0, 1):
        held = [both_kv[shard]]
        first = both_kv[1] if shard == 0 else mixtures[0]
        for bit in reversed(seq_bits):
            whole = join(held)
            if len(held) == len(seq_bits):
                whole = later(whole, first)
            held.append(swap(whole, "seq", bit))
        pieces.append(held)
        queries.append(plain(low, (own_qkv, far_qkv)[shard][:, :q_cols]).astype(bf16))
        mixture, log_total = attend(
            scalars, queries[shard], tiles[shard], query_ids[None], my_ids[:, None],
            pieces[shard], per_shard,
        )
        mixture, ffn2_pieces[shard] = tie(mixture, ffn2_pieces[shard])
        mixtures.append(mixture)
        log_totals.append(log_total)
    if hidden == width:
        ffn2_pieces = [jnp.concatenate(ffn2_pieces, axis=1)]
    far_ffn2 = [gather_all(piece) for piece in ffn2_pieces]
    if hidden == width:
        far_ffn2 = [far_ffn2[0][:, :hidden], far_ffn2[0][:, hidden:]]
    ffn2_weights = [(ffn2_in, ffn2_out), tuple(far_ffn2)]
    mix_parts = [cut_parts(mixture) for mixture in mixtures]
    branch = reduce_parts(
        [
            plain(own, output_weight) + against(far, far_output)
            for own, far in zip(*mix_parts)
        ]
    )
    stream_two = stream_one + branch

    stream_three, conv_state = conv_forward(stream_two, window_ids, conv_weights)
    ffn2_out_norm, ffn2_hat, ffn2_inverse = norm_forward(stream_three, ffn2_gain)
    branch, ffn2_state = ffn_forward(ffn2_out_norm.astype(bf16), ffn2_weights)
    stream_four = stream_three + 0.5 * branch
    final_out, final_hat, final_inverse = norm_forward(stream_four, final_gain)
    layer_low = final_out.astype(bf16)
    cot = lax.dynamic_index_in_dim(cotangent, my_row, 0, keepdims=False)
    cot = lax.dynamic_slice_in_dim(cot, mine * block, block, 0).astype(jnp.float32)
    grad_four, final_gain_grad = norm_backward(cot, final_hat, final_inverse, final_gain)

    normed_grad, ffn2_grads = ffn_backward(grad_four, ffn2_state, ffn2_weights)
    ffn2_grads = scatter_groups(ffn2_grads)
    ffn2_out_g, ffn2_in_g = ffn2_grads[:, : 2 * hidden], ffn2_grads[:, 2 * hidden :]
    stream_part, ffn2_gain_grad = norm_backward(normed_grad, ffn2_hat, ffn2_inverse, ffn2_gain)
    grad_three = grad_four + stream_part
    grad_two, conv_grads, conv_small = conv_backward(
        grad_three, conv_state, window_ids, conv_weights
    )
    branch_low = reorder(gather_parts(grad_two.astype(bf16)))
    branch_low, conv_grads = tie(branch_low, conv_grads)
    mix_grads = [
        against(branch_low, output_weight).astype(bf16),
        plain(branch_low, far_output).astype(bf16),
    ]
    layer_low = later(layer_low, branch_low)
    layer_near, layer_far = gather_parts(layer_low), far_swap(layer_low)
    q_grads, kv_grads, all_tile_grads = [], [], []
    turn = scalars
    for shard in (0, 1):
        q_grad, kv_grad, tile_grads = attend_back(
            turn, queries[shard], tiles[shard], query_ids[None], my_ids[:, None],
            mixtures[shard], mix_grads[shard], log_totals[shard], pieces[shard], per_shard,
        )
        if shard == 1:
            kv_grad, kv_grads[0], layer_near, layer_far = tie(
                kv_grad, kv_grads[0], layer_near, layer_far
            )
        for bit in seq_bits:
            half = kv_grad.shape[0] // 2
            kv_grad = (
                kv_grad[:half].astype(jnp.float32)
                + swap(kv_grad[half:], "seq", bit).astype(jnp.float32)
            ).astype(bf16)
            if shard == 0 and bit == 0:
                turn = scalars + mark(kv_grad)
        q_grads.append(q_grad)
        kv_grads.append(kv_grad[0])
        all_tile_grads.append(tile_grads)
    layer_far = gather_parts(layer_far)
    ffn2_out_came = far_swap(ffn2_out_g[:, hidden:])
    ffn2_in_g, conv_grads, kv_grads[1], ffn2_out_came, layer_far = tie(
        ffn2_in_g, conv_grads, kv_grads[1], ffn2_out_came, layer_far
    )
    conv_grads = scatter_groups(conv_grads)
    qkv_grads = [jnp.concatenate(pair, axis=1) for pair in zip(q_grads, kv_grads)]
    grad_parts = [cut_parts(grads) for grads in qkv_grads]
    partials = [against(own, own_qkv) + against(far, far_qkv) for own, far in zip(*grad_parts)]
    normed_grad = reduce_parts(partials)
    low = later(low, partials[0])
    attn_grads = jnp.concatenate(
        [
            grad_of(later(branch_low, partials[0]), jnp.concatenate(mixtures, axis=1)),
            grad_of(low, jnp.concatenate(qkv_grads, axis=1)),
        ],
        axis=1,
    )
    normed_grad, attn_grads = tie(normed_grad, attn_grads)
    stream_part, attn_gain_grad = norm_backward(normed_grad, attn_hat, attn_inverse, attn_gain)
    grad_one = grad_two + stream_part

    own_branch = (0.5 * grad_one).astype(bf16)
    near, far = tie(gather_parts(own_branch), far_swap(own_branch))
    branches = [near, gather_parts(far)]
    attn_grads, conv_grads, branches[0][-1] = tie(attn_grads, conv_grads, branches[0][-1])
    attn_grads = scatter_groups(attn_grads)
    pre_lows, partials = [], []
    for f in (0, 1):
        pre_lows.append(
            [
                (against(branch, ffn1_out) * silu_slope(pre)).astype(bf16)
                for branch, pre in zip(branches[f], ffn1_pre[f])
            ]
        )
        partials.append([against(pre_low, ffn1_in) for pre_low in pre_lows[f]])
    every_frame = lambda lists: join(lists[0] + lists[1])
    table_grads = [
        lax.dot_general(
            offset_sums(tile_grads, branches[0][-1]), onehot, (((1,), (1,)), ((), ())),
            precision=HIGHEST,
        )
        for tile_grads in all_tile_grads
    ]
    last_sent = partials[1][-1]
    ffn1_grads = jnp.concatenate(
        [
            grad_of(later(every_frame(branches), last_sent), every_frame(ffn1_act)),
            grad_of(later(every_frame(ffn1_low), last_sent), every_frame(pre_lows)),
        ],
        axis=1,
    )
    ffn1_grads, attn_grads = tie(ffn1_grads, attn_grads)
    ffn1_grads = scatter_groups(ffn1_grads).astype(jnp.float32)
    partials[0][-1] = later(partials[0][-1], last_sent)
    ffn2_in_came = far_swap(later(ffn2_in_g[:, hidden:], branches[1][0]))
    far_sum, ffn2_in_came = tie(reduce_parts(partials[1]).astype(bf16), ffn2_in_came)
    head_bits = bits(n_heads)
    conv_grads = conv_grads.reshape((2,) * len(head_bits) + (-1, 3 * width))
    for bit in head_bits[:-1]:
        conv_grads = fold_step(later(conv_grads, branches[1][0]), bit)
    far_part, conv_grads = tie(far_swap(far_sum), conv_grads)
    near_sum = reduce_parts(partials[0])
    normed_grad = near_sum + far_part.astype(jnp.float32)
    stream_part, ffn1_gain_grad = norm_backward(normed_grad, *ffn1_norm, ffn1_gain)
    grad_zero = grad_one + stream_part

    low = grad_zero.astype(bf16)
    near, far = tie(gather_parts(low), far_swap(low))
    spread_grad = near, gather_parts(far)

    (f2_out_g,) = add_far(ffn2_out_g, ffn2_out_came, [(0, hidden)])
    (f2_in_g,) = add_far(ffn2_in_g, ffn2_in_came, [(0, hidden)])
    n_out = 2 * out_cols
    conv_grads = fold_step(later(conv_grads, spread_grad[0][-1]), head_bits[-1])
    attn_came = far_columns(later(attn_grads, spread_grad[0][-1]), [(out_cols, n_out), (n_out + n_qkv, n_out + 2 * n_qkv)])

    all_heads = jnp.zeros((n_heads * per_shard, position_table.shape[1]), jnp.float32)
    all_heads = lax.dynamic_update_slice_in_dim(all_heads, table_grads[0], place * per_shard, 0)
    all_heads = lax.dynamic_update_slice_in_dim(
        all_heads, table_grads[1], (place ^ team) * per_shard, 0
    )
    gains = [ffn1_gain_grad, attn_gain_grad, ffn2_gain_grad, final_gain_grad] + conv_small
    small = jnp.concatenate([jnp.stack(gains).reshape(-1), all_heads.reshape(-1)])
    small = later(small.reshape(-1, 128), spread_grad[0][-1])
    small, attn_came, conv_grads, spread_grad[1][-1] = tie(
        sum_over(small, ("dp", "seq")), attn_came, conv_grads, spread_grad[1][-1]
    )
    small = sum_over(small, ("heads",)).reshape(-1)
    o_g, qkv_g = add_far(attn_grads, attn_came, [(0, out_cols), (n_out, n_out + n_qkv)])
    gains_all = small[: len(gains) * width].reshape(len(gains), width)
    table_all = small[len(gains) * width :].reshape(all_heads.shape)
    table_mine = lax.dynamic_slice_in_dim(table_all, place * per_shard, per_shard, 0)
    table_cols = table_mine.shape[1] // groups
    table_mine = lax.dynamic_slice_in_dim(table_mine, group_at * table_cols, table_cols, 1)
    group_part = lax.dynamic_slice_in_dim(gains_all[:4], group_at * part, part, 1)
    every = width // (groups * n_heads)
    conv_part = lax.dynamic_slice_in_dim(
        gains_all[4:], lax.axis_index(("dp", "seq", "heads")) * every, every, 1
    )

    def everywhere(parts):
        near, far = reorder(parts[0]), reorder(parts[1])
        first = my_row == 0
        return jnp.stack([jnp.where(first, near, far), jnp.where(first, far, near)])

    return (
        everywhere((layer_near, layer_far)),
        everywhere(spread_grad).astype(jnp.float32),
        group_part[0],
        ffn1_grads[:, hidden1:],
        ffn1_grads[:, :hidden1].T,
        group_part[1],
        qkv_g[:, :q_cols],
        qkv_g[:, q_cols : 2 * q_cols],
        qkv_g[:, 2 * q_cols :],
        o_g.T,
        table_mine,
        conv_part[0],
        conv_grads[:, : 2 * width],
        conv_part[2:],
        conv_part[1],
        conv_grads[:, 2 * width :],
        group_part[2],
        f2_in_g,
        f2_out_g.T,
        group_part[3],
    )


def solution(mesh):
    return jax.shard_map(
        on_device,
        mesh=mesh,
        in_specs=(
            P("dp", "seq", None),
            P("dp", None),
            P(),
            P(),
            P(None, "heads"),
            P("heads", None),
            P(),
            P(None, "heads"),
            P(None, "heads"),
            P(None, "heads"),
            P("heads", None),
            P("heads", None),
            P(("dp", "seq", "heads")),
            P(("dp", "seq", "heads"), None),
            P(None, ("dp", "seq", "heads")),
            P(("dp", "seq", "heads")),
            P(("dp", "seq", "heads"), None),
            P(),
            P(None, "heads"),
            P("heads", None),
            P(),
            P("dp", "seq", None),
        ),
        out_specs=(
            P("dp", "seq", None),
            P("dp", "seq", None),
            P(("dp", "seq")),
            P(("dp", "seq"), "heads"),
            P("heads", ("dp", "seq")),
            P(("dp", "seq")),
            P(("dp", "seq"), "heads"),
            P(("dp", "seq"), "heads"),
            P(("dp", "seq"), "heads"),
            P("heads", ("dp", "seq")),
            P("heads", ("dp", "seq")),
            P(("dp", "seq", "heads")),
            P(("dp", "seq", "heads"), None),
            P(None, ("dp", "seq", "heads")),
            P(("dp", "seq", "heads")),
            P(("dp", "seq", "heads"), None),
            P(("dp", "seq")),
            P(("dp", "seq"), "heads"),
            P("heads", ("dp", "seq")),
            P(("dp", "seq")),
        ),
        check_vma=False,
    )
```

```python
import math
import jax
import jax.numpy as jnp
from jax import lax
from jax.experimental import pallas as pl
from jax.experimental.layout import Layout, with_layout_constraint
from jax.experimental.pallas import tpu as pltpu
from jax.sharding import PartitionSpec as P

HEAD_DIM=128
NEGATIVE=-1e30
LOG2E=math.log2(math.e)
TILE=256

def bias_tiles_kernel(win_ref, out_ref):
    width = win_ref.shape[2]
    rows = jnp.broadcast_to(win_ref[0], (8, width))
    rows = pltpu.roll(rows, width - (TILE - 1), 1, stride=1, stride_axis=0)
    step = 8
    while step < TILE:
        rows = jnp.concatenate([rows, pltpu.roll(rows, step, 1)], axis=0)
        step *= 2
    for t in range(out_ref.shape[1]):
        out_ref[0, t] = rows[:, t * TILE : (t + 1) * TILE]

def bias_tiles(window):
    heads, width = window.shape
    tiles = width // TILE - 1
    return pl.pallas_call(
        bias_tiles_kernel,
        grid=(heads,),
        in_specs=[pl.BlockSpec((1, 1, width), lambda h: (h, 0, 0))],
        out_specs=pl.BlockSpec((1, tiles, TILE, TILE), lambda h: (h, 0, 0, 0)),
        out_shape=jax.ShapeDtypeStruct((heads, tiles, TILE, TILE), jnp.float32),
        cost_estimate=pl.CostEstimate(flops=TILE, transcendentals=0, bytes_accessed=TILE),
    )(window[:, None])

def offset_sums_kernel(when_ref, tiles_ref, out_ref, wide):
    tiles = tiles_ref.shape[1]
    for t in range(tiles):
        wide[:, t * TILE : (t + 1) * TILE] = tiles_ref[0, t]
    wide[:, tiles * TILE :] = jnp.zeros((TILE, TILE), jnp.float32)
    rows = wide[...]
    half = TILE // 2
    while half >= 1:
        rows = pltpu.roll(rows[:half], half, 1) + rows[half:]
        half //= 2
    out_ref[0] = rows

def offset_sums(tile_grads, when):
    heads, tiles = tile_grads.shape[:2]
    width = (tiles + 1) * TILE
    return pl.pallas_call(
        offset_sums_kernel,
        grid=(heads,),
        in_specs=[
            pl.BlockSpec(memory_space=pltpu.SMEM),
            pl.BlockSpec((1, tiles, TILE, TILE), lambda h: (h, 0, 0, 0)),
        ],
        out_specs=pl.BlockSpec((1, 1, width), lambda h: (h, 0, 0)),
        out_shape=jax.ShapeDtypeStruct((heads, 1, width), jnp.float32),
        scratch_shapes=[pltpu.VMEM((TILE, width), jnp.float32)],
        cost_estimate=pl.CostEstimate(flops=TILE, transcendentals=0, bytes_accessed=TILE),
    )(mark(when)[None], tile_grads)[:, 0]

def columns_of(head, per_shard):
    shard, at = head // per_shard, head % per_shard
    key = (shard * 2 * per_shard + at) * HEAD_DIM
    value = key + per_shard * HEAD_DIM
    return pl.multiple_of(key, HEAD_DIM), pl.multiple_of(value, HEAD_DIM)

def load_pieces(scal, pieces, whole, sems):
    local = pieces[0].shape[1]
    copies = []
    count = sum(p.shape[0] for p in pieces)
    nbits = count.bit_length() - 1
    rel = [0]
    n = 0
    for p in pieces:
        ids = [0] if p is pieces[0] else None
        if ids is None:
            bit = nbits - 1 - (n.bit_length() - 1)
            ids = [r ^ (1 << bit) for r in rel]
            rel = rel + ids
        for k, r in enumerate(ids):
            at = pl.multiple_of((scal[0] ^ r) * local, local)
            copies.append(pltpu.make_async_copy(p.at[k], whole.at[pl.ds(at, local)], sems.at[n]))
            n += 1
    for c in copies: c.start()
    for c in copies: c.wait()

def forward_kernel(scal, per_shard, pieces_n, *refs):
    q_ref, bias_ref, qid_ref, kid_ref = refs[:4]
    pieces = refs[4 : 4 + pieces_n]
    out_ref, lse_ref, whole, sems = refs[4 + pieces_n :]
    head = pl.program_id(0)
    @pl.when(head == 0)
    def _(): load_pieces(scal, pieces, whole, sems)
    kcol, vcol = columns_of(head, per_shard)
    scale = LOG2E * HEAD_DIM ** -0.5
    nk = whole.shape[0] // TILE
    for qb in range(q_ref.shape[0] // TILE):
        q = q_ref[qb * TILE : (qb + 1) * TILE, :]
        qid = qid_ref[:, qb * TILE : (qb + 1) * TILE]
        def body(kb, carry):
            top, total, acc = carry
            at = pl.multiple_of(kb * TILE, TILE)
            k = whole[pl.ds(at, TILE), pl.ds(kcol, HEAD_DIM)]
            v = whole[pl.ds(at, TILE), pl.ds(vcol, HEAD_DIM)]
            s = lax.dot_general(k, q, (((1,), (1,)), ((), ())), preferred_element_type=jnp.float32)
            s = s * scale + bias_ref[0, qb - kb + nk - 1]
            s = jnp.where(kid_ref[pl.ds(at, TILE), :] == qid, s, NEGATIVE)
            new_top = jnp.maximum(top, jnp.max(s, axis=0, keepdims=True))
            p = jnp.exp2(s - new_top)
            fade = jnp.exp2(top - new_top)
            total = total * fade + jnp.sum(p, axis=0, keepdims=True)
            acc = acc * fade + lax.dot_general(v, p.astype(jnp.bfloat16), (((0,), (0,)), ((), ())), preferred_element_type=jnp.float32)
            return new_top, total, acc
        top, total, acc = lax.fori_loop(scal[1 + 2 * qb], scal[2 + 2 * qb], body, (
            jnp.full((1, TILE), NEGATIVE, jnp.float32), jnp.zeros((1, TILE), jnp.float32), jnp.zeros((HEAD_DIM, TILE), jnp.float32)))
        out_ref[qb * TILE : (qb + 1) * TILE, :] = (acc / total).T.astype(jnp.bfloat16)
        lse_ref[0, :, qb * TILE : (qb + 1) * TILE] = top + jnp.log2(total)

def attend(scalars, q, tiles, qid, kid, pieces, per_shard):
    tokens, width = q.shape
    heads = width // HEAD_DIM
    length = kid.shape[0]
    count = sum(p.shape[0] for p in pieces)
    n_tiles = tiles.shape[1]
    fn = lambda scal, *refs: forward_kernel(scal, per_shard, len(pieces), *refs)
    flops = 4 * heads * tokens * length * HEAD_DIM
    return pl.pallas_call(
        fn,
        grid_spec=pltpu.PrefetchScalarGridSpec(
            num_scalar_prefetch=1, grid=(heads,),
            in_specs=[
                pl.BlockSpec((tokens, HEAD_DIM), lambda h, s: (0, h)),
                pl.BlockSpec((1, n_tiles, TILE, TILE), lambda h, s: (h, 0, 0, 0)),
                pl.BlockSpec((1, tokens), lambda h, s: (0, 0)),
                pl.BlockSpec((length, 1), lambda h, s: (0, 0)),
            ] + [pl.BlockSpec(memory_space=pl.ANY)] * len(pieces),
            out_specs=[
                pl.BlockSpec((tokens, HEAD_DIM), lambda h, s: (0, h)),
                pl.BlockSpec((1, 1, tokens), lambda h, s: (h, 0, 0)),
            ],
            scratch_shapes=[pltpu.VMEM((length, pieces[0].shape[-1]), jnp.bfloat16), pltpu.SemaphoreType.DMA((count,))],
        ),
        out_shape=[jax.ShapeDtypeStruct((tokens, width), jnp.bfloat16), jax.ShapeDtypeStruct((heads, 1, tokens), jnp.float32)],
        cost_estimate=pl.CostEstimate(flops=flops, transcendentals=heads*tokens*length, bytes_accessed=heads*n_tiles*TILE*TILE*4),
    )(scalars, q, tiles, qid, kid, *pieces)

def backward_kernel(scal, per_shard, pieces_n, *refs):
    q_ref, bias_ref, qid_ref, kid_ref, mix_ref, dmix_ref, lse_ref = refs[:7]
    pieces = refs[7 : 7 + pieces_n]
    dq_ref, dkv_ref, dtile_ref, whole, dk_acc, dv_acc, sems = refs[7 + pieces_n :]
    head = pl.program_id(0)
    @pl.when(head == 0)
    def _(): load_pieces(scal, pieces, whole, sems)
    kcol, vcol = columns_of(head, per_shard)
    scale = HEAD_DIM ** -0.5
    nk = whole.shape[0] // TILE
    dk_acc[...] = jnp.zeros_like(dk_acc)
    dv_acc[...] = jnp.zeros_like(dv_acc)
    dtile_ref[...] = jnp.zeros_like(dtile_ref)
    for qb in range(q_ref.shape[0] // TILE):
        rows = slice(qb * TILE, (qb + 1) * TILE)
        q = q_ref[rows, :]
        qid = qid_ref[:, rows]
        dmix = dmix_ref[rows, :]
        lse = lse_ref[0, :, rows]
        delta = jnp.sum((dmix.astype(jnp.float32) * mix_ref[rows, :].astype(jnp.float32)).T, axis=0, keepdims=True)
        def body(kb, dq):
            at = pl.multiple_of(kb * TILE, TILE)
            k = whole[pl.ds(at, TILE), pl.ds(kcol, HEAD_DIM)]
            v = whole[pl.ds(at, TILE), pl.ds(vcol, HEAD_DIM)]
            s = lax.dot_general(k, q, (((1,), (1,)), ((), ())), preferred_element_type=jnp.float32)
            s = s * (scale * LOG2E) + bias_ref[0, qb - kb + nk - 1]
            s = jnp.where(kid_ref[pl.ds(at, TILE), :] == qid, s, NEGATIVE)
            p = jnp.exp2(s - lse)
            dp = lax.dot_general(v, dmix, (((1,), (1,)), ((), ())), preferred_element_type=jnp.float32)
            ds = p * (dp - delta)
            dtile_ref[0, qb - kb + nk - 1] += ds
            low = ds.astype(jnp.bfloat16)
            dv_acc[pl.ds(at, TILE), :] += jnp.dot(p.astype(jnp.bfloat16), dmix, preferred_element_type=jnp.float32)
            dk_acc[pl.ds(at, TILE), :] += jnp.dot(low, q, preferred_element_type=jnp.float32)
            return dq + lax.dot_general(k, low, (((0,), (0,)), ((), ())), preferred_element_type=jnp.float32)
        dq = lax.fori_loop(scal[1 + 2 * qb], scal[2 + 2 * qb], body, jnp.zeros((HEAD_DIM, TILE), jnp.float32))
        dq_ref[rows, :] = (dq * scale).T.astype(jnp.bfloat16)
    count, local = dkv_ref.shape[:2]
    nbits = count.bit_length() - 1
    for block in range(count):
        diff = scal[0] ^ block
        slot = 0
        for bit in range(nbits):
            slot = slot | (((diff >> bit) & 1) << (nbits - 1 - bit))
        rows = slice(block * local, (block + 1) * local)
        dkv_ref[slot, :, pl.ds(kcol, HEAD_DIM)] = (dk_acc[rows, :] * scale).astype(jnp.bfloat16)
        dkv_ref[slot, :, pl.ds(vcol, HEAD_DIM)] = dv_acc[rows, :].astype(jnp.bfloat16)

def attend_back(scalars, q, tiles, qid, kid, mixture, mix_grad, lse, pieces, per_shard):
    tokens, width = q.shape
    heads = width // HEAD_DIM
    length = kid.shape[0]
    count = sum(p.shape[0] for p in pieces)
    n_tiles = tiles.shape[1]
    kvw = pieces[0].shape[-1]
    fn = lambda scal, *refs: backward_kernel(scal, per_shard, len(pieces), *refs)
    head_block = pl.BlockSpec((tokens, HEAD_DIM), lambda h, s: (0, h))
    tile_block = pl.BlockSpec((1, n_tiles, TILE, TILE), lambda h, s: (h, 0, 0, 0))
    return pl.pallas_call(
        fn,
        grid_spec=pltpu.PrefetchScalarGridSpec(
            num_scalar_prefetch=1, grid=(heads,),
            in_specs=[head_block, tile_block,
                pl.BlockSpec((1, tokens), lambda h, s: (0, 0)),
                pl.BlockSpec((length, 1), lambda h, s: (0, 0)),
                head_block, head_block,
                pl.BlockSpec((1, 1, tokens), lambda h, s: (h, 0, 0)),
            ] + [pl.BlockSpec(memory_space=pl.ANY)] * len(pieces),
            out_specs=[head_block,
                pl.BlockSpec((count, length // count, kvw), lambda h, s: (0, 0, 0)),
                tile_block],
            scratch_shapes=[pltpu.VMEM((length, kvw), jnp.bfloat16), pltpu.VMEM((length, HEAD_DIM), jnp.float32), pltpu.VMEM((length, HEAD_DIM), jnp.float32), pltpu.SemaphoreType.DMA((count,))],
        ),
        out_shape=[jax.ShapeDtypeStruct((tokens, width), jnp.bfloat16),
                   jax.ShapeDtypeStruct((count, length // count, kvw), jnp.bfloat16),
                   jax.ShapeDtypeStruct(tiles.shape, jnp.float32)],
        compiler_params=pltpu.CompilerParams(vmem_limit_bytes=50 * 1024 * 1024),
        cost_estimate=pl.CostEstimate(flops=10 * heads * tokens * length * HEAD_DIM, transcendentals=heads*tokens*length, bytes_accessed=2*heads*n_tiles*TILE*TILE*4),
    )(scalars, q, tiles, qid, kid, mixture, mix_grad, lse, *pieces)


EPSILON = 1e-05
KERNEL = 5
HIGHEST = lax.Precision.HIGHEST


def bits(count):
    return list(range(count.bit_length() - 1))


def swap(array, axis, bit):
    count = lax.axis_size(axis)
    return lax.ppermute(array, axis, [(i, i ^ (1 << bit)) for i in range(count)])


def bit_of(axis, bit):
    return (lax.axis_index(axis) >> bit) & 1


def gather_all(piece):
    return lax.all_gather(piece, ("dp", "seq"), axis=0, tiled=True)


def own_rows(array, shift=0):
    axes = ("dp", "seq")
    count = math.prod(lax.axis_size(axis) for axis in axes)
    part = array.shape[0] // count
    return lax.dynamic_slice_in_dim(array, lax.axis_index(axes) * part + shift, part, 0)


def outer(left, right):
    return lax.dot_general(
        left, right, (((0,), (0,)), ((), ())), preferred_element_type=jnp.float32
    )


def plain(left, right):
    return jnp.dot(left, right, preferred_element_type=jnp.float32)


def against(left, right):
    return lax.dot_general(
        left, right, (((1,), (1,)), ((), ())), preferred_element_type=jnp.float32
    )


def norm_forward(values, gain_vec):
    centred = values - jnp.mean(values, axis=-1, keepdims=True)
    inverse = lax.rsqrt(jnp.mean(centred * centred, axis=-1, keepdims=True) + EPSILON)
    normed = centred * inverse
    return (normed * gain_vec.astype(jnp.float32), normed, inverse)


def norm_backward(gradient, normed, inverse, gain_vec):
    scaled = gradient * gain_vec.astype(jnp.float32)
    mean_grad = jnp.mean(scaled, axis=-1, keepdims=True)
    second = jnp.mean(scaled * normed, axis=-1, keepdims=True)
    gain_grad = jnp.sum((gradient * normed).reshape(-1, gradient.shape[-1]), axis=0)
    return (inverse * (scaled - mean_grad - normed * second), gain_grad)


def silu_slope(values):
    sigmoid = jax.nn.sigmoid(values)
    return sigmoid * (1.0 + values * (1.0 - sigmoid))


def sum_over(array, axes):
    for axis in axes:
        for bit in bits(lax.axis_size(axis)):
            array = array + swap(array, axis, bit)
    return array


def tie(*arrays):
    return lax.optimization_barrier(arrays)


def mark(value):
    first = value[(0,) * value.ndim]
    return (first != first).astype(jnp.int32)


def later(array, value):
    return array + mark(value).astype(array.dtype)


def far_swap(array):
    return swap(array, "heads", bits(lax.axis_size("heads"))[-1])


def team_bits():
    return bits(lax.axis_size("heads"))[:-1]


def gather_parts(own):
    parts = [own]
    for bit in team_bits():
        held = parts[0] if len(parts) == 1 else jnp.concatenate(parts, axis=0)
        parts.append(swap(held, "heads", bit))
    return parts


def reduce_parts(partials):
    partials = list(partials)
    for bit in reversed(team_bits()):
        came = swap(partials.pop().astype(jnp.bfloat16), "heads", bit).astype(jnp.float32)
        at, kept = 0, []
        for item in partials:
            kept.append(item + came[at : at + item.shape[0]])
            at += item.shape[0]
        partials = kept
    return partials[0]


def spread(own):
    return gather_parts(own), gather_parts(far_swap(own))


def reorder(parts):
    team = lax.axis_size("heads") // 2
    mine = lax.axis_index("heads") % team
    whole = join(parts)
    block = whole.shape[0] // team
    if team == 2:
        first, second = parts
        lower = mine == 0
        return jnp.concatenate(
            [jnp.where(lower, first, second), jnp.where(lower, second, first)], axis=0
        )
    return jnp.concatenate(
        [lax.dynamic_slice_in_dim(whole, (at ^ mine) * block, block, 0) for at in range(team)],
        axis=0,
    )


def cut_parts(array):
    team = lax.axis_size("heads") // 2
    mine = lax.axis_index("heads") % team
    block = array.shape[0] // team
    take = lambda at: lax.dynamic_slice_in_dim(array, (at ^ mine) * block, block, 0)
    parts = [take(0)]
    for bit in team_bits():
        parts.append(join([take(at) for at in range(1 << bit, 2 << bit)]))
    return parts


def join(parts):
    return parts[0] if len(parts) == 1 else jnp.concatenate(parts, axis=0)


def scatter_groups(array):
    return lax.psum_scatter(array, ("dp", "seq"), scatter_dimension=0, tiled=True)


def grad_of(left, right):
    grads = outer(left, right).astype(jnp.bfloat16)
    return with_layout_constraint(grads, Layout(major_to_minor=(0, 1)))


def ffn_forward(low_own, weights):
    lows = gather_parts(low_own)
    pres = [[plain(low, weight_in) for weight_in, _ in weights] for low in lows]
    acts = [[jax.nn.silu(pre).astype(jnp.bfloat16) for pre in pair] for pair in pres]
    partials = [
        sum(plain(act, weight_out) for act, (_, weight_out) in zip(pair, weights))
        for pair in acts
    ]
    return reduce_parts(partials), (lows, pres, acts)


def ffn_backward(gradient, saved, weights):
    lows, pres, acts = saved
    branches = gather_parts((0.5 * gradient).astype(jnp.bfloat16))
    pre_lows = [
        [
            (against(branch, weight_out) * silu_slope(pre)).astype(jnp.bfloat16)
            for (_, weight_out), pre in zip(weights, pair)
        ]
        for branch, pair in zip(branches, pres)
    ]
    partials = [
        sum(against(pre_low, weight_in) for pre_low, (weight_in, _) in zip(pair, weights))
        for pair in pre_lows
    ]
    normed_grad = reduce_parts(partials)
    low, branch = join(lows), join(branches)
    wide = lambda items: join([jnp.concatenate(pair, axis=1) for pair in items])
    grads = jnp.concatenate(
        [grad_of(branch, wide(acts)), grad_of(low, wide(pre_lows))], axis=1
    )
    return tie(normed_grad, grads)


def far_columns(array, ranges):
    return far_swap(jnp.concatenate([array[:, a:b] for a, b in ranges], axis=1))


def add_far(array, came, ranges):
    outs, at = [], 0
    for a, b in ranges:
        outs.append(array[:, a:b].astype(jnp.float32) + came[:, at : at + b - a].astype(jnp.float32))
        at += b - a
    return outs


def halo(array, reach):
    peers, n_heads = lax.axis_size("seq"), lax.axis_size("heads")
    team = n_heads // 2
    spot = lambda row, at: (at // team) * n_heads + row * team + at % team
    up = [
        (spot(row, at), spot(row, at + 1))
        for row in range(2)
        for at in range(peers * team - 1)
    ]
    down = [(j, i) for i, j in up]
    before = lax.ppermute(array[array.shape[0] - reach :], ("seq", "heads"), up)
    after_it = lax.ppermute(array[:reach], ("seq", "heads"), down)
    return jnp.concatenate([before, array, after_it], axis=0)


def conv_forward(stream, window_ids, weights):
    in_weight, out_weight, taps, gain_one, gain_two = weights
    tokens, width = stream.shape
    reach = KERNEL // 2
    normed_out, normed, inverse = norm_forward(stream, gain_one)
    low = normed_out.astype(jnp.bfloat16)
    doubled = plain(low, in_weight)
    gate = jax.nn.sigmoid(doubled[:, width:])
    glu_low = (doubled[:, :width] * gate).astype(jnp.bfloat16)
    padded = halo(glu_low, reach)
    centre = window_ids[reach : reach + tokens]
    taps_float = taps.astype(jnp.float32)
    depth = jnp.zeros((tokens, width), jnp.float32)
    for k in range(KERNEL):
        same = (window_ids[k : k + tokens] == centre).astype(jnp.float32)[:, None]
        depth = depth + padded[k : k + tokens].astype(jnp.float32) * taps_float[k] * same
    norm_two, hat_two, inverse_two = norm_forward(depth, gain_two)
    swish_low = jax.nn.silu(norm_two).astype(jnp.bfloat16)
    branch = plain(swish_low, out_weight)
    saved = (normed, inverse, low, doubled, gate, padded, hat_two, inverse_two, norm_two, swish_low)
    return (stream + branch, saved)


def conv_backward(gradient, saved, window_ids, weights):
    in_weight, out_weight, taps, gain_one, gain_two = weights
    normed, inverse, low, doubled, gate, padded, hat_two, inverse_two, norm_two, swish_low = saved
    tokens, width = gradient.shape
    reach = KERNEL // 2
    branch_low = gradient.astype(jnp.bfloat16)
    swish_grad = against(branch_low, out_weight)
    depth_grad, gain_two_grad = norm_backward(
        swish_grad * silu_slope(norm_two), hat_two, inverse_two, gain_two
    )
    depth_low = depth_grad.astype(jnp.bfloat16)
    beside = halo(depth_low, reach)
    centre = window_ids[reach : reach + tokens]
    taps_float = taps.astype(jnp.float32)
    depth_float = depth_low.astype(jnp.float32)
    glu_grad = jnp.zeros((tokens, width), jnp.float32)
    tap_grads = []
    for k in range(KERNEL):
        same = (window_ids[k : k + tokens] == centre).astype(jnp.float32)[:, None]
        tap_grads.append(
            jnp.sum(depth_float * padded[k : k + tokens].astype(jnp.float32) * same, axis=0)
        )
        mirror = 2 * reach - k
        back = (window_ids[mirror : mirror + tokens] == centre).astype(jnp.float32)[:, None]
        glu_grad = (
            glu_grad + beside[mirror : mirror + tokens].astype(jnp.float32) * taps_float[k] * back
        )
    gate_in = doubled[:, :width]
    doubled_low = jnp.concatenate(
        [glu_grad * gate, glu_grad * gate_in * gate * (1.0 - gate)], axis=-1
    ).astype(jnp.bfloat16)
    normed_grad = against(doubled_low, in_weight)
    grads = jnp.concatenate([grad_of(low, doubled_low), grad_of(swish_low, branch_low)], axis=1)
    part, gain_one_grad = norm_backward(normed_grad, normed, inverse, gain_one)
    small = [gain_one_grad, gain_two_grad] + tap_grads
    return (gradient + part, grads, small)


def fold_step(both, bit):
    here = bit_of("heads", bit)
    kept = lax.dynamic_index_in_dim(both, here, both.ndim - 3, keepdims=False)
    sent = lax.dynamic_index_in_dim(both, 1 - here, both.ndim - 3, keepdims=False)
    came = swap(sent.astype(jnp.bfloat16), "heads", bit)
    return kept.astype(jnp.float32) + came.astype(jnp.float32)


def on_device(
    frames,
    segment_ids,
    bucket_of,
    ffn1_gain,
    ffn1_in,
    ffn1_out,
    attn_gain,
    query_weight,
    key_weight,
    value_weight,
    output_weight,
    position_table,
    conv_gain,
    pointwise_in,
    depthwise,
    depth_gain,
    pointwise_out,
    ffn2_gain,
    ffn2_in,
    ffn2_out,
    final_gain,
    cotangent,
):
    row_count, local, width = frames.shape
    length = segment_ids.shape[1]
    n_heads = lax.axis_size("heads")
    team = n_heads // 2
    place = lax.axis_index("heads")
    seq_at = lax.axis_index("seq")
    assert row_count == 2
    my_row, mine = place // team, place % team
    block = local // team
    bf16 = jnp.bfloat16
    groups = lax.axis_size("dp") * lax.axis_size("seq")
    group_at = lax.axis_index(("dp", "seq"))
    part = width // groups

    q_cols, out_cols = query_weight.shape[1], output_weight.shape[0]
    n_qkv = 3 * q_cols
    output_piece = lax.dynamic_slice_in_dim(output_weight, group_at * part, part, 1).T
    attn_piece = [own_rows(w) for w in (query_weight, key_weight, value_weight)]
    attn_piece = far_swap(jnp.concatenate(attn_piece + [output_piece], axis=1))
    small_piece = jnp.concatenate([depthwise, conv_gain[None], depth_gain[None]], axis=0).T
    small_piece = jnp.pad(small_piece, ((0, 0), (0, 128 - small_piece.shape[1])))
    conv_piece = jnp.concatenate([pointwise_in, pointwise_out, small_piece], axis=1)
    rows = [lax.dynamic_index_in_dim(frames, my_row ^ f, 0, keepdims=False) for f in (0, 1)]
    units = [cut_parts(row) for row in rows]
    stream_zero = units[0][0].astype(jnp.float32)
    hidden1 = ffn1_in.shape[1]
    ffn1_low, ffn1_pre, ffn1_act, ffn1_partial = [], [], [], []
    ffn1_norm = None
    for f in (0, 1):
        lows, pres, acts, partials = [], [], [], []
        for unit in units[f]:
            normed_out, normed, inverse = norm_forward(unit.astype(jnp.float32), ffn1_gain)
            if ffn1_norm is None:
                ffn1_norm = (normed, inverse)
            low = normed_out.astype(bf16)
            pre = plain(low, ffn1_in)
            act = jax.nn.silu(pre).astype(bf16)
            lows.append(low)
            pres.append(pre)
            acts.append(act)
            partials.append(plain(act, ffn1_out))
        ffn1_low.append(lows)
        ffn1_pre.append(pres)
        ffn1_act.append(acts)
        ffn1_partial.append(partials)
    attn_piece = later(attn_piece, ffn1_partial[1][-1])
    far_attn = gather_all(attn_piece)
    far_qkv, far_output = far_attn[:, :n_qkv], far_attn[:, n_qkv:]
    for bit in bits(n_heads):
        other = swap(conv_piece, "heads", bit)
        lower = bit_of("heads", bit) == 0
        conv_piece = jnp.concatenate(
            [jnp.where(lower, conv_piece, other), jnp.where(lower, other, conv_piece)], axis=0
        )
        if bit < len(bits(n_heads)) - 1:
            conv_piece = later(conv_piece, ffn1_partial[1][-1])
    summed, conv_piece = tie(reduce_parts(ffn1_partial[1]), conv_piece)
    near_first = ffn1_partial[0][:-1] + [later(ffn1_partial[0][-1], summed)]
    n_q, n_k = local // TILE, length // TILE
    reversed_buckets = jnp.pad(bucket_of[::-1], (0, 1))
    window = lax.dynamic_slice_in_dim(reversed_buckets, seq_at * local + mark(summed), (n_q + n_k) * TILE, 0)
    levels = lax.broadcasted_iota(jnp.int32, (position_table.shape[1], window.shape[0]), 0)
    onehot = (levels == window[None, :]).astype(jnp.float32)
    tables = jnp.concatenate([position_table, far_swap(position_table)], axis=0)
    biases = jnp.dot(tables, onehot, precision=HIGHEST) * LOG2E
    per_shard = q_cols // HEAD_DIM
    tiles = [bias_tiles(biases[:per_shard]), bias_tiles(biases[per_shard:])]
    summed = later(later(summed.astype(bf16), ffn1_partial[0][0]), ffn1_partial[0][-1])
    far_part = far_swap(summed)
    far_part, tiles[0], tiles[1], near_part = tie(
        far_part, tiles[0], tiles[1], reduce_parts(near_first)
    )
    stream_one = stream_zero + 0.5 * (
        near_part + far_part.astype(jnp.float32)
    )

    my_ids = lax.dynamic_index_in_dim(segment_ids, my_row + mark(far_part), 0, keepdims=False)
    reach = KERNEL // 2
    ids_pad = jnp.pad(my_ids, (reach, reach), constant_values=-1)
    query_ids = lax.dynamic_slice_in_dim(my_ids, seq_at * local, local, 0)
    window_ids = lax.dynamic_slice_in_dim(
        ids_pad, seq_at * local + mine * block, block + 2 * reach, 0
    )
    low_ids = query_ids.reshape(n_q, TILE)[:, 0]
    top_ids = query_ids.reshape(n_q, TILE)[:, TILE - 1]
    starts = jnp.sum((my_ids[None] < low_ids[:, None]).astype(jnp.int32), axis=1) // TILE
    ends = jnp.sum((my_ids[None] <= top_ids[:, None]).astype(jnp.int32), axis=1)
    ends = (ends + TILE - 1) // TILE
    scalars = jnp.concatenate(
        [seq_at.astype(jnp.int32)[None], jnp.stack([starts, ends], axis=1).reshape(-1)]
    )

    attn_out, attn_hat, attn_inverse = norm_forward(stream_one, attn_gain)
    low = reorder(gather_parts(attn_out.astype(bf16)))
    conv_all = gather_all(later(conv_piece, far_part))
    pw_in, pw_out = conv_all[:, : 2 * width], conv_all[:, 2 * width : 3 * width]
    small_all = conv_all[:, 3 * width : 3 * width + KERNEL + 2].T
    conv_weights = (pw_in, pw_out, small_all[:KERNEL], small_all[KERNEL], small_all[KERNEL + 1])
    hidden = ffn2_in.shape[1]
    ffn2_pieces = [own_rows(ffn2_in, mark(low)), own_rows(ffn2_out, mark(low))]
    ffn2_pieces = [far_swap(piece) for piece in ffn2_pieces]
    seq_bits = bits(lax.axis_size("seq"))
    own_qkv = jnp.concatenate(
        [later(query_weight, far_part), key_weight, value_weight], axis=1
    )
    both_kv = [plain(low, qkv[:, q_cols:]).astype(bf16)[None] for qkv in (own_qkv, far_qkv)]
    pieces, queries, mixtures, log_totals = [], [], [], []
    for shard in (0, 1):
        held = [both_kv[shard]]
        first = both_kv[1] if shard == 0 else mixtures[0]
        for bit in reversed(seq_bits):
            whole = join(held)
            if len(held) == len(seq_bits):
                whole = later(whole, first)
            held.append(swap(whole, "seq", bit))
        pieces.append(held)
        queries.append(plain(low, (own_qkv, far_qkv)[shard][:, :q_cols]).astype(bf16))
        mixture, log_total = attend(
            scalars, queries[shard], tiles[shard], query_ids[None], my_ids[:, None],
            pieces[shard], per_shard,
        )
        mixture, ffn2_pieces[shard] = tie(mixture, ffn2_pieces[shard])
        mixtures.append(mixture)
        log_totals.append(log_total)
    if hidden == width:
        ffn2_pieces = [jnp.concatenate(ffn2_pieces, axis=1)]
    far_ffn2 = [gather_all(piece) for piece in ffn2_pieces]
    if hidden == width:
        far_ffn2 = [far_ffn2[0][:, :hidden], far_ffn2[0][:, hidden:]]
    ffn2_weights = [(ffn2_in, ffn2_out), tuple(far_ffn2)]
    mix_parts = [cut_parts(mixture) for mixture in mixtures]
    branch = reduce_parts(
        [
            plain(own, output_weight) + against(far, far_output)
            for own, far in zip(*mix_parts)
        ]
    )
    stream_two = stream_one + branch

    stream_three, conv_state = conv_forward(stream_two, window_ids, conv_weights)
    ffn2_out_norm, ffn2_hat, ffn2_inverse = norm_forward(stream_three, ffn2_gain)
    branch, ffn2_state = ffn_forward(ffn2_out_norm.astype(bf16), ffn2_weights)
    stream_four = stream_three + 0.5 * branch
    final_out, final_hat, final_inverse = norm_forward(stream_four, final_gain)
    layer_low = final_out.astype(bf16)
    cot = lax.dynamic_index_in_dim(cotangent, my_row, 0, keepdims=False)
    cot = lax.dynamic_slice_in_dim(cot, mine * block, block, 0).astype(jnp.float32)
    grad_four, final_gain_grad = norm_backward(cot, final_hat, final_inverse, final_gain)

    normed_grad, ffn2_grads = ffn_backward(grad_four, ffn2_state, ffn2_weights)
    ffn2_grads = scatter_groups(ffn2_grads)
    ffn2_out_g, ffn2_in_g = ffn2_grads[:, : 2 * hidden], ffn2_grads[:, 2 * hidden :]
    stream_part, ffn2_gain_grad = norm_backward(normed_grad, ffn2_hat, ffn2_inverse, ffn2_gain)
    grad_three = grad_four + stream_part
    grad_two, conv_grads, conv_small = conv_backward(
        grad_three, conv_state, window_ids, conv_weights
    )
    branch_low = reorder(gather_parts(grad_two.astype(bf16)))
    branch_low, conv_grads = tie(branch_low, conv_grads)
    mix_grads = [
        against(branch_low, output_weight).astype(bf16),
        plain(branch_low, far_output).astype(bf16),
    ]
    layer_low = later(layer_low, branch_low)
    layer_near, layer_far = gather_parts(layer_low), far_swap(layer_low)
    q_grads, kv_grads, all_tile_grads = [], [], []
    turn = scalars
    for shard in (0, 1):
        q_grad, kv_grad, tile_grads = attend_back(
            turn, queries[shard], tiles[shard], query_ids[None], my_ids[:, None],
            mixtures[shard], mix_grads[shard], log_totals[shard], pieces[shard], per_shard,
        )
        if shard == 1:
            kv_grad, kv_grads[0], layer_near, layer_far = tie(
                kv_grad, kv_grads[0], layer_near, layer_far
            )
        for bit in seq_bits:
            half = kv_grad.shape[0] // 2
            kv_grad = (
                kv_grad[:half].astype(jnp.float32)
                + swap(kv_grad[half:], "seq", bit).astype(jnp.float32)
            ).astype(bf16)
            if shard == 0 and bit == 0:
                turn = scalars + mark(kv_grad)
        q_grads.append(q_grad)
        kv_grads.append(kv_grad[0])
        all_tile_grads.append(tile_grads)
    layer_far = gather_parts(layer_far)
    ffn2_out_came = far_swap(ffn2_out_g[:, hidden:])
    ffn2_in_g, conv_grads, kv_grads[1], ffn2_out_came, layer_far = tie(
        ffn2_in_g, conv_grads, kv_grads[1], ffn2_out_came, layer_far
    )
    conv_grads = scatter_groups(conv_grads)
    qkv_grads = [jnp.concatenate(pair, axis=1) for pair in zip(q_grads, kv_grads)]
    grad_parts = [cut_parts(grads) for grads in qkv_grads]
    partials = [against(own, own_qkv) + against(far, far_qkv) for own, far in zip(*grad_parts)]
    normed_grad = reduce_parts(partials)
    low = later(low, partials[0])
    attn_grads = jnp.concatenate(
        [
            grad_of(later(branch_low, partials[0]), jnp.concatenate(mixtures, axis=1)),
            grad_of(low, jnp.concatenate(qkv_grads, axis=1)),
        ],
        axis=1,
    )
    normed_grad, attn_grads = tie(normed_grad, attn_grads)
    stream_part, attn_gain_grad = norm_backward(normed_grad, attn_hat, attn_inverse, attn_gain)
    grad_one = grad_two + stream_part

    own_branch = (0.5 * grad_one).astype(bf16)
    near, far = tie(gather_parts(own_branch), far_swap(own_branch))
    branches = [near, gather_parts(far)]
    attn_grads, conv_grads, branches[0][-1] = tie(attn_grads, conv_grads, branches[0][-1])
    attn_grads = scatter_groups(attn_grads)
    pre_lows, partials = [], []
    for f in (0, 1):
        pre_lows.append(
            [
                (against(branch, ffn1_out) * silu_slope(pre)).astype(bf16)
                for branch, pre in zip(branches[f], ffn1_pre[f])
            ]
        )
        partials.append([against(pre_low, ffn1_in) for pre_low in pre_lows[f]])
    every_frame = lambda lists: join(lists[0] + lists[1])
    table_grads = [
        lax.dot_general(
            offset_sums(tile_grads, branches[0][-1]), onehot, (((1,), (1,)), ((), ())),
            precision=HIGHEST,
        )
        for tile_grads in all_tile_grads
    ]
    last_sent = partials[1][-1]
    ffn1_grads = jnp.concatenate(
        [
            grad_of(later(every_frame(branches), last_sent), every_frame(ffn1_act)),
            grad_of(later(every_frame(ffn1_low), last_sent), every_frame(pre_lows)),
        ],
        axis=1,
    )
    ffn1_grads, attn_grads = tie(ffn1_grads, attn_grads)
    ffn1_grads = scatter_groups(ffn1_grads).astype(jnp.float32)
    partials[0][-1] = later(partials[0][-1], last_sent)
    ffn2_in_came = far_swap(later(ffn2_in_g[:, hidden:], branches[1][0]))
    far_sum, ffn2_in_came = tie(reduce_parts(partials[1]).astype(bf16), ffn2_in_came)
    head_bits = bits(n_heads)
    conv_grads = conv_grads.reshape((2,) * len(head_bits) + (-1, 3 * width))
    for bit in head_bits[:-1]:
        conv_grads = fold_step(later(conv_grads, branches[1][0]), bit)
    far_part, conv_grads = tie(far_swap(far_sum), conv_grads)
    near_sum = reduce_parts(partials[0])
    normed_grad = near_sum + far_part.astype(jnp.float32)
    stream_part, ffn1_gain_grad = norm_backward(normed_grad, *ffn1_norm, ffn1_gain)
    grad_zero = grad_one + stream_part

    low = grad_zero.astype(bf16)
    near, far = tie(gather_parts(low), far_swap(low))
    spread_grad = near, gather_parts(far)

    (f2_out_g,) = add_far(ffn2_out_g, ffn2_out_came, [(0, hidden)])
    (f2_in_g,) = add_far(ffn2_in_g, ffn2_in_came, [(0, hidden)])
    n_out = 2 * out_cols
    conv_grads = fold_step(later(conv_grads, spread_grad[0][-1]), head_bits[-1])
    attn_came = far_columns(later(attn_grads, spread_grad[0][-1]), [(out_cols, n_out), (n_out + n_qkv, n_out + 2 * n_qkv)])

    all_heads = jnp.zeros((n_heads * per_shard, position_table.shape[1]), jnp.float32)
    all_heads = lax.dynamic_update_slice_in_dim(all_heads, table_grads[0], place * per_shard, 0)
    all_heads = lax.dynamic_update_slice_in_dim(
        all_heads, table_grads[1], (place ^ team) * per_shard, 0
    )
    gains = [ffn1_gain_grad, attn_gain_grad, ffn2_gain_grad, final_gain_grad] + conv_small
    small = jnp.concatenate([jnp.stack(gains).reshape(-1), all_heads.reshape(-1)])
    small = later(small.reshape(-1, 128), spread_grad[0][-1])
    small, attn_came = tie(sum_over(small, ("dp", "seq")), attn_came)
    small = sum_over(small, ("heads",)).reshape(-1)
    o_g, qkv_g = add_far(attn_grads, attn_came, [(0, out_cols), (n_out, n_out + n_qkv)])
    gains_all = small[: len(gains) * width].reshape(len(gains), width)
    table_all = small[len(gains) * width :].reshape(all_heads.shape)
    table_mine = lax.dynamic_slice_in_dim(table_all, place * per_shard, per_shard, 0)
    table_cols = table_mine.shape[1] // groups
    table_mine = lax.dynamic_slice_in_dim(table_mine, group_at * table_cols, table_cols, 1)
    group_part = lax.dynamic_slice_in_dim(gains_all[:4], group_at * part, part, 1)
    every = width // (groups * n_heads)
    conv_part = lax.dynamic_slice_in_dim(
        gains_all[4:], lax.axis_index(("dp", "seq", "heads")) * every, every, 1
    )

    def everywhere(parts):
        near, far = reorder(parts[0]), reorder(parts[1])
        first = my_row == 0
        return jnp.stack([jnp.where(first, near, far), jnp.where(first, far, near)])

    return (
        everywhere((layer_near, layer_far)),
        everywhere(spread_grad).astype(jnp.float32),
        group_part[0],
        ffn1_grads[:, hidden1:],
        ffn1_grads[:, :hidden1].T,
        group_part[1],
        qkv_g[:, :q_cols],
        qkv_g[:, q_cols : 2 * q_cols],
        qkv_g[:, 2 * q_cols :],
        o_g.T,
        table_mine,
        conv_part[0],
        conv_grads[:, : 2 * width],
        conv_part[2:],
        conv_part[1],
        conv_grads[:, 2 * width :],
        group_part[2],
        f2_in_g,
        f2_out_g.T,
        group_part[3],
    )


def solution(mesh):
    return jax.shard_map(
        on_device,
        mesh=mesh,
        in_specs=(
            P("dp", "seq", None),
            P("dp", None),
            P(),
            P(),
            P(None, "heads"),
            P("heads", None),
            P(),
            P(None, "heads"),
            P(None, "heads"),
            P(None, "heads"),
            P("heads", None),
            P("heads", None),
            P(("dp", "seq", "heads")),
            P(("dp", "seq", "heads"), None),
            P(None, ("dp", "seq", "heads")),
            P(("dp", "seq", "heads")),
            P(("dp", "seq", "heads"), None),
            P(),
            P(None, "heads"),
            P("heads", None),
            P(),
            P("dp", "seq", None),
        ),
        out_specs=(
            P("dp", "seq", None),
            P("dp", "seq", None),
            P(("dp", "seq")),
            P(("dp", "seq"), "heads"),
            P("heads", ("dp", "seq")),
            P(("dp", "seq")),
            P(("dp", "seq"), "heads"),
            P(("dp", "seq"), "heads"),
            P(("dp", "seq"), "heads"),
            P("heads", ("dp", "seq")),
            P("heads", ("dp", "seq")),
            P(("dp", "seq", "heads")),
            P(("dp", "seq", "heads"), None),
            P(None, ("dp", "seq", "heads")),
            P(("dp", "seq", "heads")),
            P(("dp", "seq", "heads"), None),
            P(("dp", "seq")),
            P(("dp", "seq"), "heads"),
            P("heads", ("dp", "seq")),
            P(("dp", "seq")),
        ),
        check_vma=False,
    )
```

```python
import math
import jax
import jax.numpy as jnp
from jax import lax
from jax.experimental import pallas as pl
from jax.experimental.layout import Layout, with_layout_constraint
from jax.experimental.pallas import tpu as pltpu
from jax.sharding import PartitionSpec as P

HEAD_DIM=128
NEGATIVE=-1e30
LOG2E=math.log2(math.e)
TILE=256

def bias_tiles_kernel(win_ref, out_ref):
    width = win_ref.shape[2]
    rows = jnp.broadcast_to(win_ref[0], (8, width))
    rows = pltpu.roll(rows, width - (TILE - 1), 1, stride=1, stride_axis=0)
    step = 8
    while step < TILE:
        rows = jnp.concatenate([rows, pltpu.roll(rows, step, 1)], axis=0)
        step *= 2
    for t in range(out_ref.shape[1]):
        out_ref[0, t] = rows[:, t * TILE : (t + 1) * TILE]

def bias_tiles(window):
    heads, width = window.shape
    tiles = width // TILE - 1
    return pl.pallas_call(
        bias_tiles_kernel,
        grid=(heads,),
        in_specs=[pl.BlockSpec((1, 1, width), lambda h: (h, 0, 0))],
        out_specs=pl.BlockSpec((1, tiles, TILE, TILE), lambda h: (h, 0, 0, 0)),
        out_shape=jax.ShapeDtypeStruct((heads, tiles, TILE, TILE), jnp.float32),
        cost_estimate=pl.CostEstimate(flops=TILE, transcendentals=0, bytes_accessed=TILE),
    )(window[:, None])

def offset_sums_kernel(when_ref, tiles_ref, out_ref, wide):
    tiles = tiles_ref.shape[1]
    for t in range(tiles):
        wide[:, t * TILE : (t + 1) * TILE] = tiles_ref[0, t]
    wide[:, tiles * TILE :] = jnp.zeros((TILE, TILE), jnp.float32)
    rows = wide[...]
    half = TILE // 2
    while half >= 1:
        rows = pltpu.roll(rows[:half], half, 1) + rows[half:]
        half //= 2
    out_ref[0] = rows

def offset_sums(tile_grads, when):
    heads, tiles = tile_grads.shape[:2]
    width = (tiles + 1) * TILE
    return pl.pallas_call(
        offset_sums_kernel,
        grid=(heads,),
        in_specs=[
            pl.BlockSpec(memory_space=pltpu.SMEM),
            pl.BlockSpec((1, tiles, TILE, TILE), lambda h: (h, 0, 0, 0)),
        ],
        out_specs=pl.BlockSpec((1, 1, width), lambda h: (h, 0, 0)),
        out_shape=jax.ShapeDtypeStruct((heads, 1, width), jnp.float32),
        scratch_shapes=[pltpu.VMEM((TILE, width), jnp.float32)],
        cost_estimate=pl.CostEstimate(flops=TILE, transcendentals=0, bytes_accessed=TILE),
    )(mark(when)[None], tile_grads)[:, 0]

def columns_of(head, per_shard):
    shard, at = head // per_shard, head % per_shard
    key = (shard * 2 * per_shard + at) * HEAD_DIM
    value = key + per_shard * HEAD_DIM
    return pl.multiple_of(key, HEAD_DIM), pl.multiple_of(value, HEAD_DIM)

def load_pieces(scal, pieces, whole, sems):
    local = pieces[0].shape[1]
    copies = []
    count = sum(p.shape[0] for p in pieces)
    nbits = count.bit_length() - 1
    rel = [0]
    n = 0
    for p in pieces:
        ids = [0] if p is pieces[0] else None
        if ids is None:
            bit = nbits - 1 - (n.bit_length() - 1)
            ids = [r ^ (1 << bit) for r in rel]
            rel = rel + ids
        for k, r in enumerate(ids):
            at = pl.multiple_of((scal[0] ^ r) * local, local)
            copies.append(pltpu.make_async_copy(p.at[k], whole.at[pl.ds(at, local)], sems.at[n]))
            n += 1
    for c in copies: c.start()
    for c in copies: c.wait()

def forward_kernel(scal, per_shard, pieces_n, *refs):
    q_ref, bias_ref, qid_ref, kid_ref = refs[:4]
    pieces = refs[4 : 4 + pieces_n]
    out_ref, lse_ref, whole, sems = refs[4 + pieces_n :]
    head = pl.program_id(0)
    @pl.when(head == 0)
    def _(): load_pieces(scal, pieces, whole, sems)
    kcol, vcol = columns_of(head, per_shard)
    scale = LOG2E * HEAD_DIM ** -0.5
    nk = whole.shape[0] // TILE
    for qb in range(q_ref.shape[0] // TILE):
        q = q_ref[qb * TILE : (qb + 1) * TILE, :]
        qid = qid_ref[:, qb * TILE : (qb + 1) * TILE]
        def body(kb, carry):
            top, total, acc = carry
            at = pl.multiple_of(kb * TILE, TILE)
            k = whole[pl.ds(at, TILE), pl.ds(kcol, HEAD_DIM)]
            v = whole[pl.ds(at, TILE), pl.ds(vcol, HEAD_DIM)]
            s = lax.dot_general(k, q, (((1,), (1,)), ((), ())), preferred_element_type=jnp.float32)
            s = s * scale + bias_ref[0, qb - kb + nk - 1]
            s = jnp.where(kid_ref[pl.ds(at, TILE), :] == qid, s, NEGATIVE)
            new_top = jnp.maximum(top, jnp.max(s, axis=0, keepdims=True))
            p = jnp.exp2(s - new_top)
            fade = jnp.exp2(top - new_top)
            total = total * fade + jnp.sum(p, axis=0, keepdims=True)
            acc = acc * fade + lax.dot_general(v, p.astype(jnp.bfloat16), (((0,), (0,)), ((), ())), preferred_element_type=jnp.float32)
            return new_top, total, acc
        top, total, acc = lax.fori_loop(scal[1 + 2 * qb], scal[2 + 2 * qb], body, (
            jnp.full((1, TILE), NEGATIVE, jnp.float32), jnp.zeros((1, TILE), jnp.float32), jnp.zeros((HEAD_DIM, TILE), jnp.float32)))
        out_ref[qb * TILE : (qb + 1) * TILE, :] = (acc / total).T.astype(jnp.bfloat16)
        lse_ref[0, :, qb * TILE : (qb + 1) * TILE] = top + jnp.log2(total)

def attend(scalars, q, tiles, qid, kid, pieces, per_shard):
    tokens, width = q.shape
    heads = width // HEAD_DIM
    length = kid.shape[0]
    count = sum(p.shape[0] for p in pieces)
    n_tiles = tiles.shape[1]
    fn = lambda scal, *refs: forward_kernel(scal, per_shard, len(pieces), *refs)
    flops = 4 * heads * tokens * length * HEAD_DIM
    return pl.pallas_call(
        fn,
        grid_spec=pltpu.PrefetchScalarGridSpec(
            num_scalar_prefetch=1, grid=(heads,),
            in_specs=[
                pl.BlockSpec((tokens, HEAD_DIM), lambda h, s: (0, h)),
                pl.BlockSpec((1, n_tiles, TILE, TILE), lambda h, s: (h, 0, 0, 0)),
                pl.BlockSpec((1, tokens), lambda h, s: (0, 0)),
                pl.BlockSpec((length, 1), lambda h, s: (0, 0)),
            ] + [pl.BlockSpec(memory_space=pl.ANY)] * len(pieces),
            out_specs=[
                pl.BlockSpec((tokens, HEAD_DIM), lambda h, s: (0, h)),
                pl.BlockSpec((1, 1, tokens), lambda h, s: (h, 0, 0)),
            ],
            scratch_shapes=[pltpu.VMEM((length, pieces[0].shape[-1]), jnp.bfloat16), pltpu.SemaphoreType.DMA((count,))],
        ),
        out_shape=[jax.ShapeDtypeStruct((tokens, width), jnp.bfloat16), jax.ShapeDtypeStruct((heads, 1, tokens), jnp.float32)],
        cost_estimate=pl.CostEstimate(flops=flops, transcendentals=heads*tokens*length, bytes_accessed=heads*n_tiles*TILE*TILE*4),
    )(scalars, q, tiles, qid, kid, *pieces)

def backward_kernel(scal, per_shard, pieces_n, *refs):
    q_ref, bias_ref, qid_ref, kid_ref, mix_ref, dmix_ref, lse_ref = refs[:7]
    pieces = refs[7 : 7 + pieces_n]
    dq_ref, dkv_ref, dtile_ref, whole, dk_acc, dv_acc, sems = refs[7 + pieces_n :]
    head = pl.program_id(0)
    @pl.when(head == 0)
    def _(): load_pieces(scal, pieces, whole, sems)
    kcol, vcol = columns_of(head, per_shard)
    scale = HEAD_DIM ** -0.5
    nk = whole.shape[0] // TILE
    dk_acc[...] = jnp.zeros_like(dk_acc)
    dv_acc[...] = jnp.zeros_like(dv_acc)
    dtile_ref[...] = jnp.zeros_like(dtile_ref)
    for qb in range(q_ref.shape[0] // TILE):
        rows = slice(qb * TILE, (qb + 1) * TILE)
        q = q_ref[rows, :]
        qid = qid_ref[:, rows]
        dmix = dmix_ref[rows, :]
        lse = lse_ref[0, :, rows]
        delta = jnp.sum((dmix.astype(jnp.float32) * mix_ref[rows, :].astype(jnp.float32)).T, axis=0, keepdims=True)
        def body(kb, dq):
            at = pl.multiple_of(kb * TILE, TILE)
            k = whole[pl.ds(at, TILE), pl.ds(kcol, HEAD_DIM)]
            v = whole[pl.ds(at, TILE), pl.ds(vcol, HEAD_DIM)]
            s = lax.dot_general(k, q, (((1,), (1,)), ((), ())), preferred_element_type=jnp.float32)
            s = s * (scale * LOG2E) + bias_ref[0, qb - kb + nk - 1]
            s = jnp.where(kid_ref[pl.ds(at, TILE), :] == qid, s, NEGATIVE)
            p = jnp.exp2(s - lse)
            dp = lax.dot_general(v, dmix, (((1,), (1,)), ((), ())), preferred_element_type=jnp.float32)
            ds = p * (dp - delta)
            dtile_ref[0, qb - kb + nk - 1] += ds
            low = ds.astype(jnp.bfloat16)
            dv_acc[pl.ds(at, TILE), :] += jnp.dot(p.astype(jnp.bfloat16), dmix, preferred_element_type=jnp.float32)
            dk_acc[pl.ds(at, TILE), :] += jnp.dot(low, q, preferred_element_type=jnp.float32)
            return dq + lax.dot_general(k, low, (((0,), (0,)), ((), ())), preferred_element_type=jnp.float32)
        dq = lax.fori_loop(scal[1 + 2 * qb], scal[2 + 2 * qb], body, jnp.zeros((HEAD_DIM, TILE), jnp.float32))
        dq_ref[rows, :] = (dq * scale).T.astype(jnp.bfloat16)
    count, local = dkv_ref.shape[:2]
    nbits = count.bit_length() - 1
    for block in range(count):
        diff = scal[0] ^ block
        slot = 0
        for bit in range(nbits):
            slot = slot | (((diff >> bit) & 1) << (nbits - 1 - bit))
        rows = slice(block * local, (block + 1) * local)
        dkv_ref[slot, :, pl.ds(kcol, HEAD_DIM)] = (dk_acc[rows, :] * scale).astype(jnp.bfloat16)
        dkv_ref[slot, :, pl.ds(vcol, HEAD_DIM)] = dv_acc[rows, :].astype(jnp.bfloat16)

def attend_back(scalars, q, tiles, qid, kid, mixture, mix_grad, lse, pieces, per_shard):
    tokens, width = q.shape
    heads = width // HEAD_DIM
    length = kid.shape[0]
    count = sum(p.shape[0] for p in pieces)
    n_tiles = tiles.shape[1]
    kvw = pieces[0].shape[-1]
    fn = lambda scal, *refs: backward_kernel(scal, per_shard, len(pieces), *refs)
    head_block = pl.BlockSpec((tokens, HEAD_DIM), lambda h, s: (0, h))
    tile_block = pl.BlockSpec((1, n_tiles, TILE, TILE), lambda h, s: (h, 0, 0, 0))
    return pl.pallas_call(
        fn,
        grid_spec=pltpu.PrefetchScalarGridSpec(
            num_scalar_prefetch=1, grid=(heads,),
            in_specs=[head_block, tile_block,
                pl.BlockSpec((1, tokens), lambda h, s: (0, 0)),
                pl.BlockSpec((length, 1), lambda h, s: (0, 0)),
                head_block, head_block,
                pl.BlockSpec((1, 1, tokens), lambda h, s: (h, 0, 0)),
            ] + [pl.BlockSpec(memory_space=pl.ANY)] * len(pieces),
            out_specs=[head_block,
                pl.BlockSpec((count, length // count, kvw), lambda h, s: (0, 0, 0)),
                tile_block],
            scratch_shapes=[pltpu.VMEM((length, kvw), jnp.bfloat16), pltpu.VMEM((length, HEAD_DIM), jnp.float32), pltpu.VMEM((length, HEAD_DIM), jnp.float32), pltpu.SemaphoreType.DMA((count,))],
        ),
        out_shape=[jax.ShapeDtypeStruct((tokens, width), jnp.bfloat16),
                   jax.ShapeDtypeStruct((count, length // count, kvw), jnp.bfloat16),
                   jax.ShapeDtypeStruct(tiles.shape, jnp.float32)],
        compiler_params=pltpu.CompilerParams(vmem_limit_bytes=50 * 1024 * 1024),
        cost_estimate=pl.CostEstimate(flops=10 * heads * tokens * length * HEAD_DIM, transcendentals=heads*tokens*length, bytes_accessed=2*heads*n_tiles*TILE*TILE*4),
    )(scalars, q, tiles, qid, kid, mixture, mix_grad, lse, *pieces)


EPSILON = 1e-05
KERNEL = 5
HIGHEST = lax.Precision.HIGHEST


def bits(count):
    return list(range(count.bit_length() - 1))


def swap(array, axis, bit):
    count = lax.axis_size(axis)
    return lax.ppermute(array, axis, [(i, i ^ (1 << bit)) for i in range(count)])


def bit_of(axis, bit):
    return (lax.axis_index(axis) >> bit) & 1


def gather_all(piece):
    return lax.all_gather(piece, ("dp", "seq"), axis=0, tiled=True)


def own_rows(array, shift=0):
    axes = ("dp", "seq")
    count = math.prod(lax.axis_size(axis) for axis in axes)
    part = array.shape[0] // count
    return lax.dynamic_slice_in_dim(array, lax.axis_index(axes) * part + shift, part, 0)


def outer(left, right):
    return lax.dot_general(
        left, right, (((0,), (0,)), ((), ())), preferred_element_type=jnp.float32
    )


def plain(left, right):
    return jnp.dot(left, right, preferred_element_type=jnp.float32)


def against(left, right):
    return lax.dot_general(
        left, right, (((1,), (1,)), ((), ())), preferred_element_type=jnp.float32
    )


def norm_forward(values, gain_vec):
    centred = values - jnp.mean(values, axis=-1, keepdims=True)
    inverse = lax.rsqrt(jnp.mean(centred * centred, axis=-1, keepdims=True) + EPSILON)
    normed = centred * inverse
    return (normed * gain_vec.astype(jnp.float32), normed, inverse)


def norm_backward(gradient, normed, inverse, gain_vec):
    scaled = gradient * gain_vec.astype(jnp.float32)
    mean_grad = jnp.mean(scaled, axis=-1, keepdims=True)
    second = jnp.mean(scaled * normed, axis=-1, keepdims=True)
    gain_grad = jnp.sum((gradient * normed).reshape(-1, gradient.shape[-1]), axis=0)
    return (inverse * (scaled - mean_grad - normed * second), gain_grad)


def silu_slope(values):
    sigmoid = jax.nn.sigmoid(values)
    return sigmoid * (1.0 + values * (1.0 - sigmoid))


def sum_everyone(array):
    for axis in ("heads", "dp", "seq"):
        for bit in bits(lax.axis_size(axis)):
            array = array + swap(array, axis, bit)
    return array


def tie(*arrays):
    return lax.optimization_barrier(arrays)


def mark(value):
    first = value[(0,) * value.ndim]
    return (first != first).astype(jnp.int32)


def later(array, value):
    return array + mark(value).astype(array.dtype)


def far_swap(array):
    return swap(array, "heads", bits(lax.axis_size("heads"))[-1])


def team_bits():
    return bits(lax.axis_size("heads"))[:-1]


def gather_parts(own):
    parts = [own]
    for bit in team_bits():
        held = parts[0] if len(parts) == 1 else jnp.concatenate(parts, axis=0)
        parts.append(swap(held, "heads", bit))
    return parts


def reduce_parts(partials):
    partials = list(partials)
    for bit in reversed(team_bits()):
        came = swap(partials.pop().astype(jnp.bfloat16), "heads", bit).astype(jnp.float32)
        at, kept = 0, []
        for item in partials:
            kept.append(item + came[at : at + item.shape[0]])
            at += item.shape[0]
        partials = kept
    return partials[0]


def spread(own):
    return gather_parts(own), gather_parts(far_swap(own))


def reorder(parts):
    team = lax.axis_size("heads") // 2
    mine = lax.axis_index("heads") % team
    whole = join(parts)
    block = whole.shape[0] // team
    if team == 2:
        first, second = parts
        lower = mine == 0
        return jnp.concatenate(
            [jnp.where(lower, first, second), jnp.where(lower, second, first)], axis=0
        )
    return jnp.concatenate(
        [lax.dynamic_slice_in_dim(whole, (at ^ mine) * block, block, 0) for at in range(team)],
        axis=0,
    )


def cut_parts(array):
    team = lax.axis_size("heads") // 2
    mine = lax.axis_index("heads") % team
    block = array.shape[0] // team
    take = lambda at: lax.dynamic_slice_in_dim(array, (at ^ mine) * block, block, 0)
    parts = [take(0)]
    for bit in team_bits():
        parts.append(join([take(at) for at in range(1 << bit, 2 << bit)]))
    return parts


def join(parts):
    return parts[0] if len(parts) == 1 else jnp.concatenate(parts, axis=0)


def scatter_groups(array):
    return lax.psum_scatter(array, ("dp", "seq"), scatter_dimension=0, tiled=True)


def grad_of(left, right):
    grads = outer(left, right).astype(jnp.bfloat16)
    return with_layout_constraint(grads, Layout(major_to_minor=(0, 1)))


def ffn_forward(low_own, weights):
    lows = gather_parts(low_own)
    pres = [[plain(low, weight_in) for weight_in, _ in weights] for low in lows]
    acts = [[jax.nn.silu(pre).astype(jnp.bfloat16) for pre in pair] for pair in pres]
    partials = [
        sum(plain(act, weight_out) for act, (_, weight_out) in zip(pair, weights))
        for pair in acts
    ]
    return reduce_parts(partials), (lows, pres, acts)


def ffn_backward(gradient, saved, weights):
    lows, pres, acts = saved
    branches = gather_parts((0.5 * gradient).astype(jnp.bfloat16))
    pre_lows = [
        [
            (against(branch, weight_out) * silu_slope(pre)).astype(jnp.bfloat16)
            for (_, weight_out), pre in zip(weights, pair)
        ]
        for branch, pair in zip(branches, pres)
    ]
    partials = [
        sum(against(pre_low, weight_in) for pre_low, (weight_in, _) in zip(pair, weights))
        for pair in pre_lows
    ]
    normed_grad = reduce_parts(partials)
    low, branch = join(lows), join(branches)
    wide = lambda items: join([jnp.concatenate(pair, axis=1) for pair in items])
    grads = jnp.concatenate(
        [grad_of(branch, wide(acts)), grad_of(low, wide(pre_lows))], axis=1
    )
    return tie(normed_grad, grads)


def far_columns(array, ranges):
    return far_swap(jnp.concatenate([array[:, a:b] for a, b in ranges], axis=1))


def add_far(array, came, ranges):
    outs, at = [], 0
    for a, b in ranges:
        outs.append(array[:, a:b].astype(jnp.float32) + came[:, at : at + b - a].astype(jnp.float32))
        at += b - a
    return outs


def halo(array, reach):
    peers, n_heads = lax.axis_size("seq"), lax.axis_size("heads")
    team = n_heads // 2
    spot = lambda row, at: (at // team) * n_heads + row * team + at % team
    up = [
        (spot(row, at), spot(row, at + 1))
        for row in range(2)
        for at in range(peers * team - 1)
    ]
    down = [(j, i) for i, j in up]
    before = lax.ppermute(array[array.shape[0] - reach :], ("seq", "heads"), up)
    after_it = lax.ppermute(array[:reach], ("seq", "heads"), down)
    return jnp.concatenate([before, array, after_it], axis=0)


def conv_forward(stream, window_ids, weights):
    in_weight, out_weight, taps, gain_one, gain_two = weights
    tokens, width = stream.shape
    reach = KERNEL // 2
    normed_out, normed, inverse = norm_forward(stream, gain_one)
    low = normed_out.astype(jnp.bfloat16)
    doubled = plain(low, in_weight)
    gate = jax.nn.sigmoid(doubled[:, width:])
    glu_low = (doubled[:, :width] * gate).astype(jnp.bfloat16)
    padded = halo(glu_low, reach)
    centre = window_ids[reach : reach + tokens]
    taps_float = taps.astype(jnp.float32)
    depth = jnp.zeros((tokens, width), jnp.float32)
    for k in range(KERNEL):
        same = (window_ids[k : k + tokens] == centre).astype(jnp.float32)[:, None]
        depth = depth + padded[k : k + tokens].astype(jnp.float32) * taps_float[k] * same
    norm_two, hat_two, inverse_two = norm_forward(depth, gain_two)
    swish_low = jax.nn.silu(norm_two).astype(jnp.bfloat16)
    branch = plain(swish_low, out_weight)
    saved = (normed, inverse, low, doubled, gate, padded, hat_two, inverse_two, norm_two, swish_low)
    return (stream + branch, saved)


def conv_backward(gradient, saved, window_ids, weights):
    in_weight, out_weight, taps, gain_one, gain_two = weights
    normed, inverse, low, doubled, gate, padded, hat_two, inverse_two, norm_two, swish_low = saved
    tokens, width = gradient.shape
    reach = KERNEL // 2
    branch_low = gradient.astype(jnp.bfloat16)
    swish_grad = against(branch_low, out_weight)
    depth_grad, gain_two_grad = norm_backward(
        swish_grad * silu_slope(norm_two), hat_two, inverse_two, gain_two
    )
    depth_low = depth_grad.astype(jnp.bfloat16)
    beside = halo(depth_low, reach)
    centre = window_ids[reach : reach + tokens]
    taps_float = taps.astype(jnp.float32)
    depth_float = depth_low.astype(jnp.float32)
    glu_grad = jnp.zeros((tokens, width), jnp.float32)
    tap_grads = []
    for k in range(KERNEL):
        same = (window_ids[k : k + tokens] == centre).astype(jnp.float32)[:, None]
        tap_grads.append(
            jnp.sum(depth_float * padded[k : k + tokens].astype(jnp.float32) * same, axis=0)
        )
        mirror = 2 * reach - k
        back = (window_ids[mirror : mirror + tokens] == centre).astype(jnp.float32)[:, None]
        glu_grad = (
            glu_grad + beside[mirror : mirror + tokens].astype(jnp.float32) * taps_float[k] * back
        )
    gate_in = doubled[:, :width]
    doubled_low = jnp.concatenate(
        [glu_grad * gate, glu_grad * gate_in * gate * (1.0 - gate)], axis=-1
    ).astype(jnp.bfloat16)
    normed_grad = against(doubled_low, in_weight)
    grads = jnp.concatenate([grad_of(low, doubled_low), grad_of(swish_low, branch_low)], axis=1)
    part, gain_one_grad = norm_backward(normed_grad, normed, inverse, gain_one)
    small = [gain_one_grad, gain_two_grad] + tap_grads
    return (gradient + part, grads, small)


def fold_step(both, bit):
    here = bit_of("heads", bit)
    kept = lax.dynamic_index_in_dim(both, here, both.ndim - 3, keepdims=False)
    sent = lax.dynamic_index_in_dim(both, 1 - here, both.ndim - 3, keepdims=False)
    came = swap(sent.astype(jnp.bfloat16), "heads", bit)
    return kept.astype(jnp.float32) + came.astype(jnp.float32)


def on_device(
    frames,
    segment_ids,
    bucket_of,
    ffn1_gain,
    ffn1_in,
    ffn1_out,
    attn_gain,
    query_weight,
    key_weight,
    value_weight,
    output_weight,
    position_table,
    conv_gain,
    pointwise_in,
    depthwise,
    depth_gain,
    pointwise_out,
    ffn2_gain,
    ffn2_in,
    ffn2_out,
    final_gain,
    cotangent,
):
    row_count, local, width = frames.shape
    length = segment_ids.shape[1]
    n_heads = lax.axis_size("heads")
    team = n_heads // 2
    place = lax.axis_index("heads")
    seq_at = lax.axis_index("seq")
    assert row_count == 2
    my_row, mine = place // team, place % team
    block = local // team
    bf16 = jnp.bfloat16
    groups = lax.axis_size("dp") * lax.axis_size("seq")
    group_at = lax.axis_index(("dp", "seq"))
    part = width // groups

    own_qkv = jnp.concatenate([query_weight, key_weight, value_weight], axis=1)
    q_cols, out_cols, n_qkv = query_weight.shape[1], output_weight.shape[0], own_qkv.shape[1]
    output_piece = lax.dynamic_slice_in_dim(output_weight, group_at * part, part, 1).T
    attn_piece = [own_rows(w) for w in (query_weight, key_weight, value_weight)]
    attn_piece = far_swap(jnp.concatenate(attn_piece + [output_piece], axis=1))
    small_piece = jnp.concatenate([depthwise, conv_gain[None], depth_gain[None]], axis=0).T
    small_piece = jnp.pad(small_piece, ((0, 0), (0, 128 - small_piece.shape[1])))
    conv_piece = jnp.concatenate([pointwise_in, pointwise_out, small_piece], axis=1)
    rows = [lax.dynamic_index_in_dim(frames, my_row ^ f, 0, keepdims=False) for f in (0, 1)]
    units = [cut_parts(row) for row in rows]
    stream_zero = units[0][0].astype(jnp.float32)
    hidden1 = ffn1_in.shape[1]
    ffn1_low, ffn1_pre, ffn1_act, ffn1_partial = [], [], [], []
    ffn1_norm = None
    for f in (0, 1):
        lows, pres, acts, partials = [], [], [], []
        for unit in units[f]:
            normed_out, normed, inverse = norm_forward(unit.astype(jnp.float32), ffn1_gain)
            if ffn1_norm is None:
                ffn1_norm = (normed, inverse)
            low = normed_out.astype(bf16)
            pre = plain(low, ffn1_in)
            act = jax.nn.silu(pre).astype(bf16)
            lows.append(low)
            pres.append(pre)
            acts.append(act)
            partials.append(plain(act, ffn1_out))
        ffn1_low.append(lows)
        ffn1_pre.append(pres)
        ffn1_act.append(acts)
        ffn1_partial.append(partials)
    attn_piece = later(attn_piece, ffn1_partial[1][-1])
    far_attn = gather_all(attn_piece)
    far_qkv, far_output = far_attn[:, :n_qkv], far_attn[:, n_qkv:]
    for bit in bits(n_heads):
        other = swap(conv_piece, "heads", bit)
        lower = bit_of("heads", bit) == 0
        conv_piece = jnp.concatenate(
            [jnp.where(lower, conv_piece, other), jnp.where(lower, other, conv_piece)], axis=0
        )
        if bit < len(bits(n_heads)) - 1:
            conv_piece = later(conv_piece, ffn1_partial[1][-1])
    summed = reduce_parts(ffn1_partial[1])
    conv_all = gather_all(later(conv_piece, ffn1_partial[1][0]))
    pw_in, pw_out = conv_all[:, : 2 * width], conv_all[:, 2 * width : 3 * width]
    small_all = conv_all[:, 3 * width : 3 * width + KERNEL + 2].T
    conv_weights = (pw_in, pw_out, small_all[:KERNEL], small_all[KERNEL], small_all[KERNEL + 1])
    n_q, n_k = local // TILE, length // TILE
    my_ids = lax.dynamic_index_in_dim(segment_ids, my_row, 0, keepdims=False)
    reach = KERNEL // 2
    ids_pad = jnp.pad(my_ids, (reach, reach), constant_values=-1)
    query_ids = lax.dynamic_slice_in_dim(my_ids, seq_at * local, local, 0)
    window_ids = lax.dynamic_slice_in_dim(
        ids_pad, seq_at * local + mine * block, block + 2 * reach, 0
    )
    low_ids = query_ids.reshape(n_q, TILE)[:, 0]
    top_ids = query_ids.reshape(n_q, TILE)[:, TILE - 1]
    starts = jnp.sum((my_ids[None] < low_ids[:, None]).astype(jnp.int32), axis=1) // TILE
    ends = jnp.sum((my_ids[None] <= top_ids[:, None]).astype(jnp.int32), axis=1)
    ends = (ends + TILE - 1) // TILE
    scalars = jnp.concatenate(
        [seq_at.astype(jnp.int32)[None], jnp.stack([starts, ends], axis=1).reshape(-1)]
    )
    reversed_buckets = jnp.pad(bucket_of[::-1], (0, 1))
    window = lax.dynamic_slice_in_dim(reversed_buckets, seq_at * local + mark(summed), (n_q + n_k) * TILE, 0)
    levels = lax.broadcasted_iota(jnp.int32, (position_table.shape[1], window.shape[0]), 0)
    onehot = (levels == window[None, :]).astype(jnp.float32)
    tables = jnp.concatenate([position_table, far_swap(position_table)], axis=0)
    biases = jnp.dot(tables, onehot, precision=HIGHEST) * LOG2E
    per_shard = q_cols // HEAD_DIM
    tiles = [bias_tiles(biases[:per_shard]), bias_tiles(biases[per_shard:])]
    summed = later(later(summed.astype(bf16), ffn1_partial[0][0]), ffn1_partial[0][-1])
    far_part = far_swap(summed)
    far_part, tiles[0], tiles[1], scalars, own_qkv = tie(
        far_part, tiles[0], tiles[1], scalars, own_qkv
    )
    stream_one = stream_zero + 0.5 * (
        reduce_parts(ffn1_partial[0]) + far_part.astype(jnp.float32)
    )

    attn_out, attn_hat, attn_inverse = norm_forward(stream_one, attn_gain)
    low = reorder(gather_parts(attn_out.astype(bf16)))
    hidden = ffn2_in.shape[1]
    ffn2_pieces = [own_rows(ffn2_in, mark(low)), own_rows(ffn2_out, mark(low))]
    ffn2_pieces = [far_swap(piece) for piece in ffn2_pieces]
    seq_bits = bits(lax.axis_size("seq"))
    both_kv = [plain(low, qkv[:, q_cols:]).astype(bf16)[None] for qkv in (own_qkv, far_qkv)]
    pieces, queries, mixtures, log_totals = [], [], [], []
    for shard in (0, 1):
        held = [both_kv[shard]]
        first = both_kv[1] if shard == 0 else mixtures[0]
        for bit in reversed(seq_bits):
            whole = join(held)
            if len(held) == len(seq_bits):
                whole = later(whole, first)
            held.append(swap(whole, "seq", bit))
        pieces.append(held)
        queries.append(plain(low, (own_qkv, far_qkv)[shard][:, :q_cols]).astype(bf16))
        mixture, log_total = attend(
            scalars, queries[shard], tiles[shard], query_ids[None], my_ids[:, None],
            pieces[shard], per_shard,
        )
        mixture, ffn2_pieces[shard] = tie(mixture, ffn2_pieces[shard])
        mixtures.append(mixture)
        log_totals.append(log_total)
    if hidden == width:
        ffn2_pieces = [jnp.concatenate(ffn2_pieces, axis=1)]
    far_ffn2 = [gather_all(piece) for piece in ffn2_pieces]
    if hidden == width:
        far_ffn2 = [far_ffn2[0][:, :hidden], far_ffn2[0][:, hidden:]]
    ffn2_weights = [(ffn2_in, ffn2_out), tuple(far_ffn2)]
    mix_parts = [cut_parts(mixture) for mixture in mixtures]
    branch = reduce_parts(
        [
            plain(own, output_weight) + against(far, far_output)
            for own, far in zip(*mix_parts)
        ]
    )
    stream_two = stream_one + branch

    stream_three, conv_state = conv_forward(stream_two, window_ids, conv_weights)
    ffn2_out_norm, ffn2_hat, ffn2_inverse = norm_forward(stream_three, ffn2_gain)
    branch, ffn2_state = ffn_forward(ffn2_out_norm.astype(bf16), ffn2_weights)
    stream_four = stream_three + 0.5 * branch
    final_out, final_hat, final_inverse = norm_forward(stream_four, final_gain)
    layer_low = final_out.astype(bf16)
    cot = lax.dynamic_index_in_dim(cotangent, my_row, 0, keepdims=False)
    cot = lax.dynamic_slice_in_dim(cot, mine * block, block, 0).astype(jnp.float32)
    grad_four, final_gain_grad = norm_backward(cot, final_hat, final_inverse, final_gain)

    normed_grad, ffn2_grads = ffn_backward(grad_four, ffn2_state, ffn2_weights)
    ffn2_grads = scatter_groups(ffn2_grads)
    ffn2_out_g, ffn2_in_g = ffn2_grads[:, : 2 * hidden], ffn2_grads[:, 2 * hidden :]
    stream_part, ffn2_gain_grad = norm_backward(normed_grad, ffn2_hat, ffn2_inverse, ffn2_gain)
    grad_three = grad_four + stream_part
    grad_two, conv_grads, conv_small = conv_backward(
        grad_three, conv_state, window_ids, conv_weights
    )
    branch_low = reorder(gather_parts(grad_two.astype(bf16)))
    branch_low, conv_grads = tie(branch_low, conv_grads)
    mix_grads = [
        against(branch_low, output_weight).astype(bf16),
        plain(branch_low, far_output).astype(bf16),
    ]
    layer_low = later(layer_low, branch_low)
    layer_near, layer_far = gather_parts(layer_low), far_swap(layer_low)
    q_grads, kv_grads, all_tile_grads = [], [], []
    turn = scalars
    for shard in (0, 1):
        q_grad, kv_grad, tile_grads = attend_back(
            turn, queries[shard], tiles[shard], query_ids[None], my_ids[:, None],
            mixtures[shard], mix_grads[shard], log_totals[shard], pieces[shard], per_shard,
        )
        if shard == 1:
            kv_grad, kv_grads[0], layer_near, layer_far = tie(
                kv_grad, kv_grads[0], layer_near, layer_far
            )
        for bit in seq_bits:
            half = kv_grad.shape[0] // 2
            kv_grad = (
                kv_grad[:half].astype(jnp.float32)
                + swap(kv_grad[half:], "seq", bit).astype(jnp.float32)
            ).astype(bf16)
            if shard == 0 and bit == 0:
                turn = scalars + mark(kv_grad)
        q_grads.append(q_grad)
        kv_grads.append(kv_grad[0])
        all_tile_grads.append(tile_grads)
    layer_far = gather_parts(layer_far)
    ffn2_out_came = far_swap(ffn2_out_g[:, hidden:])
    ffn2_in_g, conv_grads, kv_grads[1], ffn2_out_came, layer_far = tie(
        ffn2_in_g, conv_grads, kv_grads[1], ffn2_out_came, layer_far
    )
    conv_grads = scatter_groups(conv_grads)
    qkv_grads = [jnp.concatenate(pair, axis=1) for pair in zip(q_grads, kv_grads)]
    grad_parts = [cut_parts(grads) for grads in qkv_grads]
    partials = [against(own, own_qkv) + against(far, far_qkv) for own, far in zip(*grad_parts)]
    normed_grad = reduce_parts(partials)
    low = later(low, partials[0])
    attn_grads = jnp.concatenate(
        [
            grad_of(later(branch_low, partials[0]), jnp.concatenate(mixtures, axis=1)),
            grad_of(low, jnp.concatenate(qkv_grads, axis=1)),
        ],
        axis=1,
    )
    normed_grad, attn_grads = tie(normed_grad, attn_grads)
    stream_part, attn_gain_grad = norm_backward(normed_grad, attn_hat, attn_inverse, attn_gain)
    grad_one = grad_two + stream_part

    own_branch = (0.5 * grad_one).astype(bf16)
    near, far = tie(gather_parts(own_branch), far_swap(own_branch))
    branches = [near, gather_parts(far)]
    attn_grads, conv_grads, branches[0][-1] = tie(attn_grads, conv_grads, branches[0][-1])
    attn_grads = scatter_groups(attn_grads)
    pre_lows, partials = [], []
    for f in (0, 1):
        pre_lows.append(
            [
                (against(branch, ffn1_out) * silu_slope(pre)).astype(bf16)
                for branch, pre in zip(branches[f], ffn1_pre[f])
            ]
        )
        partials.append([against(pre_low, ffn1_in) for pre_low in pre_lows[f]])
    every_frame = lambda lists: join(lists[0] + lists[1])
    table_grads = [
        lax.dot_general(
            offset_sums(tile_grads, branches[0][-1]), onehot, (((1,), (1,)), ((), ())),
            precision=HIGHEST,
        )
        for tile_grads in all_tile_grads
    ]
    last_sent = partials[1][-1]
    ffn1_grads = jnp.concatenate(
        [
            grad_of(later(every_frame(branches), last_sent), every_frame(ffn1_act)),
            grad_of(later(every_frame(ffn1_low), last_sent), every_frame(pre_lows)),
        ],
        axis=1,
    )
    ffn1_grads, attn_grads = tie(ffn1_grads, attn_grads)
    ffn1_grads = scatter_groups(ffn1_grads).astype(jnp.float32)
    partials[0][-1] = later(partials[0][-1], last_sent)
    ffn2_in_came = far_swap(later(ffn2_in_g[:, hidden:], branches[1][0]))
    far_sum, ffn2_in_came = tie(reduce_parts(partials[1]).astype(bf16), ffn2_in_came)
    head_bits = bits(n_heads)
    conv_grads = conv_grads.reshape((2,) * len(head_bits) + (-1, 3 * width))
    for bit in head_bits[:-1]:
        conv_grads = fold_step(later(conv_grads, branches[1][0]), bit)
    far_part, conv_grads = tie(far_swap(far_sum), conv_grads)
    near_sum = reduce_parts(partials[0])
    normed_grad = near_sum + far_part.astype(jnp.float32)
    stream_part, ffn1_gain_grad = norm_backward(normed_grad, *ffn1_norm, ffn1_gain)
    grad_zero = grad_one + stream_part

    low = grad_zero.astype(bf16)
    near, far = tie(gather_parts(low), far_swap(low))
    spread_grad = near, gather_parts(far)

    (f2_out_g,) = add_far(ffn2_out_g, ffn2_out_came, [(0, hidden)])
    (f2_in_g,) = add_far(ffn2_in_g, ffn2_in_came, [(0, hidden)])
    n_out = 2 * out_cols
    conv_grads = fold_step(later(conv_grads, spread_grad[1][0]), head_bits[-1])
    attn_came = far_columns(later(attn_grads, spread_grad[1][0]), [(out_cols, n_out), (n_out + n_qkv, n_out + 2 * n_qkv)])
    o_g, qkv_g = add_far(attn_grads, attn_came, [(0, out_cols), (n_out, n_out + n_qkv)])

    all_heads = jnp.zeros((n_heads * per_shard, position_table.shape[1]), jnp.float32)
    all_heads = lax.dynamic_update_slice_in_dim(all_heads, table_grads[0], place * per_shard, 0)
    all_heads = lax.dynamic_update_slice_in_dim(
        all_heads, table_grads[1], (place ^ team) * per_shard, 0
    )
    gains = [ffn1_gain_grad, attn_gain_grad, ffn2_gain_grad, final_gain_grad] + conv_small
    small = jnp.concatenate([jnp.stack(gains).reshape(-1), all_heads.reshape(-1)])
    small = later(small.reshape(-1, 128), spread_grad[1][0])
    small = sum_everyone(small).reshape(-1)
    gains_all = small[: len(gains) * width].reshape(len(gains), width)
    table_all = small[len(gains) * width :].reshape(all_heads.shape)
    table_mine = lax.dynamic_slice_in_dim(table_all, place * per_shard, per_shard, 0)
    table_cols = table_mine.shape[1] // groups
    table_mine = lax.dynamic_slice_in_dim(table_mine, group_at * table_cols, table_cols, 1)
    group_part = lax.dynamic_slice_in_dim(gains_all[:4], group_at * part, part, 1)
    every = width // (groups * n_heads)
    conv_part = lax.dynamic_slice_in_dim(
        gains_all[4:], lax.axis_index(("dp", "seq", "heads")) * every, every, 1
    )

    def everywhere(parts):
        near, far = reorder(parts[0]), reorder(parts[1])
        first = my_row == 0
        return jnp.stack([jnp.where(first, near, far), jnp.where(first, far, near)])

    return (
        everywhere((layer_near, layer_far)),
        everywhere(spread_grad).astype(jnp.float32),
        group_part[0],
        ffn1_grads[:, hidden1:],
        ffn1_grads[:, :hidden1].T,
        group_part[1],
        qkv_g[:, :q_cols],
        qkv_g[:, q_cols : 2 * q_cols],
        qkv_g[:, 2 * q_cols :],
        o_g.T,
        table_mine,
        conv_part[0],
        conv_grads[:, : 2 * width],
        conv_part[2:],
        conv_part[1],
        conv_grads[:, 2 * width :],
        group_part[2],
        f2_in_g,
        f2_out_g.T,
        group_part[3],
    )


def solution(mesh):
    return jax.shard_map(
        on_device,
        mesh=mesh,
        in_specs=(
            P("dp", "seq", None),
            P("dp", None),
            P(),
            P(),
            P(None, "heads"),
            P("heads", None),
            P(),
            P(None, "heads"),
            P(None, "heads"),
            P(None, "heads"),
            P("heads", None),
            P("heads", None),
            P(("dp", "seq", "heads")),
            P(("dp", "seq", "heads"), None),
            P(None, ("dp", "seq", "heads")),
            P(("dp", "seq", "heads")),
            P(("dp", "seq", "heads"), None),
            P(),
            P(None, "heads"),
            P("heads", None),
            P(),
            P("dp", "seq", None),
        ),
        out_specs=(
            P("dp", "seq", None),
            P("dp", "seq", None),
            P(("dp", "seq")),
            P(("dp", "seq"), "heads"),
            P("heads", ("dp", "seq")),
            P(("dp", "seq")),
            P(("dp", "seq"), "heads"),
            P(("dp", "seq"), "heads"),
            P(("dp", "seq"), "heads"),
            P("heads", ("dp", "seq")),
            P("heads", ("dp", "seq")),
            P(("dp", "seq", "heads")),
            P(("dp", "seq", "heads"), None),
            P(None, ("dp", "seq", "heads")),
            P(("dp", "seq", "heads")),
            P(("dp", "seq", "heads"), None),
            P(("dp", "seq")),
            P(("dp", "seq"), "heads"),
            P("heads", ("dp", "seq")),
            P(("dp", "seq")),
        ),
        check_vma=False,
    )
```
